256 devices in a mesh: gx: 16 (over x, z_lo), gy: 4 (over z_hi, core), gz: 4 (over y).
Axes of the slice: x: 4, y: 4, z: 8 (z_hi: 2, z_lo: 4; z = z_hi * 4 + z_lo), core: 2. Of those that a mesh axis runs over, the one named last changes fastest.
Arguments:
- point_frac: float32 [3, 1048576], P(None, ('gx', 'gy', 'gz')), may hold values from 0.5 to 1.5
- cell_offset: int32 [3, 1048576], P(None, ('gx', 'gy', 'gz')), may hold values from 0 to 3
- point_velocity: float32 [3, 1048576], P(None, ('gx', 'gy', 'gz')), may hold values from -6 to 6
- point_affine: float32 [9, 1048576], P(None, ('gx', 'gy', 'gz')), may hold values from -3 to 3
- point_stress: float32 [6, 1048576], P(None, ('gx', 'gy', 'gz')), may hold values from -9.5 to 3, as said below
- point_mass: float32 [1048576], P(('gx', 'gy', 'gz')), may hold values from 0.5 to 2
- block_tile: int32 [8192], P(('gx', 'gy', 'gz')), may hold values from 0 to 511, as said below
- block_count: int32 [8192], P(('gx', 'gy', 'gz')), may hold values from 1 to 128, as said below
Outputs:
- new_velocity: float32 [3, 1048576], P(None, ('gx', 'gy', 'gz'))
- new_affine: float32 [9, 1048576], P(None, ('gx', 'gy', 'gz'))
- new_stress: float32 [6, 1048576], P(None, ('gx', 'gy', 'gz'))
- grid_velocity: float32 [3, 256, 256, 128], P(None, 'gx', 'gy', 'gz')
The draws below stay inside these ranges and needn't reach their ends.
Inputs may be any that keep to these rules, and one draw needn't show every extreme that they name: `block_tile`: block b lies on the device numbered b // 32 (gz fastest, then gy, then gx) and names a tile of that device's region, t = (tx 64 / 4 + ty) * 8 + tz; a tile may be named by no block or by several. The first block_count slots of a block hold live points. `point_stress`: components in the order xx, yy, zz, yz, xz, xy.
All inputs are finite; a program needn't handle non-finite values.
Results may differ from the reference program's by a relative error of at most 0.0003.
Values sent between devices are 32-bit elements; how exact they have to be, the bound alone decides.
A program may use at most 128 MiB of HBM per device.

```python
import math
import jax
import jax.numpy as jnp
from jax import lax

CX = 16
CY = 64
CZ = 32
BLOCK = 128
B_DEV = 32
TILES_DEV = 512
BLOCKS = 8192
POINTS = 1048576
NX = 256
NY = 256
NZ = 128
N_GY = 4
N_GZ = 4
DEVICES = 256


def draw_point_stress(key, part):
    subkeys = jax.random.split(key, 2)
    pressure = jnp.exp(jax.random.uniform(subkeys[0], (POINTS,), jnp.float32, math.log(0.5), math.log(8.0)))
    spread = jnp.clip(jax.random.normal(subkeys[1], (6, POINTS), jnp.float32), -3.0, 3.0)
    scales = jnp.array([0.5, 0.5, 0.5, 1.0, 1.0, 1.0], jnp.float32)
    diagonal_pick = jnp.array([1.0, 1.0, 1.0, 0.0, 0.0, 0.0], jnp.float32)
    return spread * scales[:, None] - pressure[None, :] * diagonal_pick[:, None]


def draw_block_tile(key, part):
    subkeys = jax.random.split(key, 2)
    first_draw = jax.random.randint(subkeys[0], (BLOCKS,), 0, TILES_DEV)
    second_draw = jax.random.randint(subkeys[1], (BLOCKS,), 0, TILES_DEV)
    skewed = first_draw * (second_draw + 1) // TILES_DEV
    position = jnp.arange(BLOCKS, dtype=jnp.int32)
    return jnp.where(position % B_DEV == 1, TILES_DEV - 1, skewed).astype(jnp.int32)


def draw_block_count(key, part):
    counts_drawn = jax.random.randint(key, (BLOCKS,), 1, BLOCK + 1)
    position = jnp.arange(BLOCKS, dtype=jnp.int32)
    return jnp.where(position % 64 == 0, BLOCK, counts_drawn).astype(jnp.int32)


def with_ends(entries, rng, smallest, largest):
    longest = entries.shape.index(max(entries.shape))
    spots = []
    for shift in (0, 1):
        where = [jax.random.randint(jax.random.fold_in(rng, axis), (), 0, length) for axis, length in enumerate(entries.shape)]
        where[longest] = (where[longest] + shift) % entries.shape[longest]
        spots.append(tuple(where))
    return entries.at[spots[0]].set(smallest).at[spots[1]].set(largest)


def shard_levels(own_key, shape, pieces, smallest, high):
    def one(axis_at, shards_of):
        steps = jax.random.uniform(jax.random.fold_in(jax.random.fold_in(own_key, 6), axis_at), (shards_of,), jnp.float32, smallest / len(pieces), high / len(pieces))
        return jnp.repeat(jnp.exp(steps), shape[axis_at] // shards_of).reshape((-1,) + (1,) * (len(shape) - axis_at - 1))

    loudness = one(*pieces[0])
    for cut in pieces[1:]:
        loudness = loudness * one(*cut)
    return loudness


def centred(key, extent, width, bound, cuts=(), kind=jnp.bfloat16):
    drawn = width * jax.random.normal(key, extent, jnp.float32)
    if cuts:
        drawn = drawn * shard_levels(key, extent, cuts, -0.22, 0.18)
    return jnp.clip(drawn, -bound, bound).astype(kind)


def setup_inputs(seed: int = 0) -> dict:
    key_of = jax.random.split(jax.random.key(seed), 9)
    return {
        "point_frac": jnp.clip(0.5 + 1.0 * jax.random.uniform(key_of[0], (3, POINTS), jnp.float32) ** shard_levels(key_of[0], (3, POINTS), ((1, 256),), -0.2, 0.2), 0.5, 1.5),
        "cell_offset": with_ends(jax.random.randint(key_of[1], (3, POINTS), 0, 4), jax.random.fold_in(key_of[1], 1), 0, 3).astype(jnp.int32),
        "point_velocity": centred(key_of[2], (3, POINTS), 1.0, 6.0, ((1, 256),), jnp.float32),
        "point_affine": centred(key_of[3], (9, POINTS), 0.5, 3.0, ((1, 256),), jnp.float32),
        "point_stress": draw_point_stress(jax.random.fold_in(key_of[8], 71), 0),
        "point_mass": jnp.clip(jnp.exp(math.log(2.0) - 1.3862944 * jax.random.uniform(key_of[5], (POINTS,), jnp.float32) ** shard_levels(key_of[5], (POINTS,), ((0, 256),), -0.2, 0.2)), 0.5, 2.0),
        "block_tile": draw_block_tile(jax.random.fold_in(key_of[8], 71), 0),
        "block_count": draw_block_count(jax.random.fold_in(key_of[8], 71), 0),
    }


time_step = 0.1
gravity = 1.0
shear_modulus = 2.0
bulk_modulus = 4.0
friction_static = 0.38
friction_limit = 0.64
inertial_ref = 0.28
grain_size = 0.5
grain_density = 1.0
pressure_floor = 0.5
shear_floor = 0.5
mass_floor = 0.05
stress_scale = 0.4
pair_index = ((0, 5, 4), (5, 1, 3), (4, 3, 2))
component_pairs = ((0, 0), (1, 1), (2, 2), (1, 2), (0, 2), (0, 1))

def stress_update(stress, affine):
    strain_rate = [[0.5 * (affine[3 * row_dim + col_dim] + affine[3 * col_dim + row_dim]) for col_dim in range(3)] for row_dim in range(3)]
    volume_rate = strain_rate[0][0] + strain_rate[1][1] + strain_rate[2][2]
    deviator = [[strain_rate[row_dim][col_dim] - (volume_rate / 3.0 if row_dim == col_dim else 0.0) for col_dim in range(3)] for row_dim in range(3)]
    trial_stress = []
    for component in range(6):
        row_dim, col_dim = component_pairs[component]
        value = stress[component] + time_step * 2.0 * shear_modulus * deviator[row_dim][col_dim]
        if component < 3:
            value = value + time_step * bulk_modulus * volume_rate
        trial_stress.append(value)
    pressure = -(trial_stress[0] + trial_stress[1] + trial_stress[2]) / 3.0
    shear_part = [trial_stress[component] + pressure for component in range(3)] + trial_stress[3:]
    shear_stress = jnp.sqrt(0.5 * (shear_part[0] ** 2 + shear_part[1] ** 2 + shear_part[2] ** 2) + shear_part[3] ** 2 + shear_part[4] ** 2 + shear_part[5] ** 2)
    shear_rate = jnp.sqrt(2.0 * (deviator[0][0] ** 2 + deviator[1][1] ** 2 + deviator[2][2] ** 2 + 2.0 * (deviator[1][2] ** 2 + deviator[0][2] ** 2 + deviator[0][1] ** 2)))
    inertial = shear_rate * grain_size / jnp.sqrt(jnp.maximum(pressure, pressure_floor) / grain_density)
    friction = friction_static + (friction_limit - friction_static) * inertial / (inertial_ref + inertial)
    support = jnp.maximum(pressure, 0.0)
    factor = jnp.minimum(1.0, friction * support / jnp.maximum(shear_stress, shear_floor))
    result = [shear_part[component] * factor - support for component in range(3)] + [shear_part[component] * factor for component in range(3, 6)]
    return jnp.stack(result)

def spline_slots(fraction, offset):
    slot_index = jnp.arange(6, dtype=jnp.int32)
    shifted = slot_index - offset[..., None]
    left_weight = 0.5 * (1.5 - fraction) ** 2
    middle = 0.75 - (fraction - 1.0) ** 2
    right_weight = 0.5 * (fraction - 0.5) ** 2
    return jnp.where(shifted == 0, left_weight[..., None], 0.0) + jnp.where(shifted == 1, middle[..., None], 0.0) + jnp.where(shifted == 2, right_weight[..., None], 0.0)

def block_weights(fraction, offset):
    along_x = spline_slots(fraction[0], offset[0])
    along_y = spline_slots(fraction[1], offset[1])
    along_z = spline_slots(fraction[2], offset[2])
    product = along_x[:, :, :, None, None] * along_y[:, :, None, :, None] * along_z[:, :, None, None, :]
    return product.reshape(product.shape[0], product.shape[1], 216)

def node_coords():
    node = jnp.arange(216, dtype=jnp.int32)
    return [(node // 36).astype(jnp.float32), (node // 6 % 6).astype(jnp.float32), (node % 6).astype(jnp.float32)]

def deposit(fraction, offset, velocity, affine, stress, live_mass):
    weights = block_weights(fraction, offset)
    position = [offset[dim_index].astype(jnp.float32) + fraction[dim_index] for dim_index in range(3)]
    matrix = [[live_mass * (affine[3 * row_dim + col_dim] - stress_scale * stress[pair_index[row_dim][col_dim]]) for col_dim in range(3)] for row_dim in range(3)]
    moment = [live_mass * velocity[row_dim] - matrix[row_dim][0] * position[0] - matrix[row_dim][1] * position[1] - matrix[row_dim][2] * position[2] for row_dim in range(3)]
    channels = jnp.stack([live_mass] + moment + [matrix[row_dim][col_dim] for row_dim in range(3) for col_dim in range(3)])
    node_sums = jnp.einsum('cgp,gpn->gcn', channels, weights, precision=lax.Precision.HIGHEST)
    coords = node_coords()
    momentum = [node_sums[:, 1 + row_dim] + node_sums[:, 4 + 3 * row_dim] * coords[0] + node_sums[:, 5 + 3 * row_dim] * coords[1] + node_sums[:, 6 + 3 * row_dim] * coords[2] for row_dim in range(3)]
    return jnp.stack(momentum + [node_sums[:, 0]], axis=1)

def collect(fraction, offset, node_values):
    weights = block_weights(fraction, offset)
    coords = node_coords()
    node_table = jnp.stack([node_values[:, row_dim] for row_dim in range(3)] + [node_values[:, row_dim] * coords[col_dim] for row_dim in range(3) for col_dim in range(3)], axis=1)
    result = jnp.einsum('gpn,gcn->cgp', weights, node_table, precision=lax.Precision.HIGHEST)
    position = [offset[dim_index].astype(jnp.float32) + fraction[dim_index] for dim_index in range(3)]
    velocity = result[0:3]
    affine = jnp.stack([4.0 * (result[3 + 3 * row_dim + col_dim] - result[row_dim] * position[col_dim]) for row_dim in range(3) for col_dim in range(3)])
    return (velocity, affine)

def grid_step(reduced, x_index, y_index, z_index, width_x, depth_z):
    inverse = 1.0 / (reduced[3] + mass_floor)
    velocity_x = reduced[0] * inverse
    velocity_y = reduced[1] * inverse - time_step * gravity
    velocity_z = reduced[2] * inverse
    outlet = (x_index >= width_x // 4) & (x_index < width_x - width_x // 4)
    floor_cells = (y_index < 2) & jnp.logical_not(outlet)
    velocity_y = jnp.where(floor_cells, jnp.maximum(velocity_y, 0.0), velocity_y)
    velocity_z = jnp.where(z_index < 2, jnp.maximum(velocity_z, 0.0), velocity_z)
    velocity_z = jnp.where(z_index >= depth_z - 2, jnp.minimum(velocity_z, 0.0), velocity_z)
    velocity_x = jnp.broadcast_to(velocity_x, velocity_y.shape)
    return jnp.stack([velocity_x, velocity_y, velocity_z])

def node_index(device, tile_ids):
    tiles_y = CY // 4
    tiles_z = CZ // 4
    corner_x = device // (N_GY * N_GZ) * CX + 4 * (tile_ids // (tiles_y * tiles_z)) - 1
    corner_y = device // N_GZ % N_GY * CY + 4 * (tile_ids // tiles_z % tiles_y) - 1
    corner_z = device % N_GZ * CZ + 4 * (tile_ids % tiles_z) - 1
    node = jnp.arange(216, dtype=jnp.int32)
    cell_x = (corner_x[:, None] + (node // 36)[None, :]) % NX
    cell_y = (corner_y[:, None] + (node // 6 % 6)[None, :]) % NY
    cell_z = (corner_z[:, None] + (node % 6)[None, :]) % NZ
    return ((cell_x * NY + cell_y) * NZ + cell_z).astype(jnp.int32)

def by_device(values):
    return jnp.moveaxis(values.reshape(values.shape[0], DEVICES, B_DEV, BLOCK), 1, 0)

def reference(point_frac, cell_offset, point_velocity, point_affine, point_stress, point_mass, block_tile, block_count):
    new_stress = stress_update(point_stress, point_affine)
    slot_index = jnp.arange(BLOCK, dtype=jnp.int32)
    live_mask = (slot_index[None, :] < block_count[:, None]).astype(jnp.float32)
    live_mass = point_mass.reshape(BLOCKS, BLOCK) * live_mask
    devices = jnp.arange(DEVICES, dtype=jnp.int32)
    frac_parts = by_device(point_frac)
    offset_parts = by_device(cell_offset)
    tile_parts = block_tile.reshape(DEVICES, B_DEV)

    def deposit_device(grid_sums, inputs):
        device, fraction, offset, velocity, affine, stress, masses, tile_ids = inputs
        node_sums = deposit(fraction, offset, velocity, affine, stress, masses)
        flat_index = node_index(device, tile_ids).reshape(-1)
        grid_sums = grid_sums.at[:, flat_index].add(jnp.moveaxis(node_sums, 1, 0).reshape(4, -1))
        return (grid_sums, None)
    grid_sums = jnp.zeros((4, NX * NY * NZ), jnp.float32)
    grid_sums, _ = lax.scan(deposit_device, grid_sums, (devices, frac_parts, offset_parts, by_device(point_velocity), by_device(point_affine), by_device(new_stress), live_mass.reshape(DEVICES, B_DEV, BLOCK), tile_parts))
    reduced = grid_sums.reshape(4, NX, NY, NZ)
    x_index = jnp.arange(NX, dtype=jnp.int32)[:, None, None]
    y_index = jnp.arange(NY, dtype=jnp.int32)[None, :, None]
    z_index = jnp.arange(NZ, dtype=jnp.int32)[None, None, :]
    grid_velocity = grid_step(reduced, x_index, y_index, z_index, NX, NZ)
    flat_velocity = grid_velocity.reshape(3, -1)

    def collect_device(carry, inputs):
        device, fraction, offset, tile_ids = inputs
        flat_index = node_index(device, tile_ids)
        node_values = jnp.moveaxis(flat_velocity[:, flat_index], 0, 1)
        velocity, affine = collect(fraction, offset, node_values)
        return (carry, (velocity, affine))
    _, outputs = lax.scan(collect_device, None, (devices, frac_parts, offset_parts, tile_parts))
    new_velocity = jnp.moveaxis(outputs[0], 0, 1).reshape(3, POINTS)
    new_affine = jnp.moveaxis(outputs[1], 0, 1).reshape(9, POINTS)
    return (new_velocity, new_affine, new_stress, grid_velocity)
```

```python
import jax
import jax.numpy as jnp
from jax import lax
from jax.experimental import pallas as pl
from jax.experimental.pallas import tpu as pltpu
from jax.sharding import PartitionSpec as P

CX = 16
CY = 64
CZ = 32
BLOCK = 128

time_step = 0.1
gravity = 1.0
shear_modulus = 2.0
bulk_modulus = 4.0
friction_static = 0.38
friction_limit = 0.64
inertial_ref = 0.28
grain_size = 0.5
grain_density = 1.0
pressure_floor = 0.5
shear_floor = 0.5
mass_floor = 0.05
stress_scale = 0.4
pair_index = ((0, 5, 4), (5, 1, 3), (4, 3, 2))
component_pairs = ((0, 0), (1, 1), (2, 2), (1, 2), (0, 2), (0, 1))

PX = CX + 2
PY = 72
PITCH = 40
LANES = 128
ROWS = PX * PY
MESH = pl.DeviceIdType.MESH

T_WX, T_WXD = 0, 6
T_LY, T_MY, T_RY, T_OY, T_Y = 12, 13, 14, 15, 16
T_LZ, T_MZ, T_RZ, T_OZ, T_Z = 17, 18, 19, 20, 21
T_SHARED = 22
T_MASS, T_MV, T_A = 22, 23, 26
T_ALL = 35


def stress_update(stress, affine):
    strain_rate = [
        [
            0.5 * (affine[3 * row_dim + col_dim] + affine[3 * col_dim + row_dim])
            for col_dim in range(3)
        ]
        for row_dim in range(3)
    ]
    volume_rate = strain_rate[0][0] + strain_rate[1][1] + strain_rate[2][2]
    deviator = [
        [
            strain_rate[row_dim][col_dim] - (volume_rate / 3.0 if row_dim == col_dim else 0.0)
            for col_dim in range(3)
        ]
        for row_dim in range(3)
    ]
    trial_stress = []
    for component in range(6):
        row_dim, col_dim = component_pairs[component]
        value = stress[component] + time_step * 2.0 * shear_modulus * deviator[row_dim][col_dim]
        if component < 3:
            value = value + time_step * bulk_modulus * volume_rate
        trial_stress.append(value)
    pressure = -(trial_stress[0] + trial_stress[1] + trial_stress[2]) / 3.0
    shear_part = [trial_stress[component] + pressure for component in range(3)] + trial_stress[3:]
    shear_stress = jnp.sqrt(
        0.5 * (shear_part[0] ** 2 + shear_part[1] ** 2 + shear_part[2] ** 2)
        + shear_part[3] ** 2
        + shear_part[4] ** 2
        + shear_part[5] ** 2
    )
    shear_rate = jnp.sqrt(
        2.0
        * (
            deviator[0][0] ** 2
            + deviator[1][1] ** 2
            + deviator[2][2] ** 2
            + 2.0 * (deviator[1][2] ** 2 + deviator[0][2] ** 2 + deviator[0][1] ** 2)
        )
    )
    inertial = (
        shear_rate * grain_size / jnp.sqrt(jnp.maximum(pressure, pressure_floor) / grain_density)
    )
    friction = friction_static + (friction_limit - friction_static) * inertial / (
        inertial_ref + inertial
    )
    support = jnp.maximum(pressure, 0.0)
    factor = jnp.minimum(1.0, friction * support / jnp.maximum(shear_stress, shear_floor))
    return [shear_part[component] * factor - support for component in range(3)] + [
        shear_part[component] * factor for component in range(3, 6)
    ]


def split(values):
    high = values.astype(jnp.bfloat16)
    low = (values - high.astype(jnp.float32)).astype(jnp.bfloat16)
    return high, low


def tile_coords(tile_ref, block):
    tile = tile_ref[block]
    return tile // 128, (tile // 8) % 16, tile % 8


def axis_weights(row, left, middle, right, offset, position):
    index = lax.broadcasted_iota(jnp.int32, (8, LANES), 0).astype(jnp.float32)
    shifted = index - row(offset)
    weight = jnp.where(
        shifted == 0.0,
        row(left),
        jnp.where(shifted == 1.0, row(middle), jnp.where(shifted == 2.0, row(right), 0.0)),
    )
    return weight, weight * (index - row(position))


def deposit_kernel(
    tile_ref,
    count_ref,
    frac_ref,
    offset_ref,
    velocity_ref,
    affine_ref,
    stress_ref,
    mass_ref,
    new_stress_ref,
    mom_ref,
    grid_mass_ref,
    shared_ref,
    gathered,
    table,
    stress_out,
):
    blocks = mass_ref.shape[0]
    lane = lax.broadcasted_iota(jnp.int32, (1, LANES), 1)
    stride = 48
    for block in range(blocks):
        cols = slice(block * BLOCK, (block + 1) * BLOCK)
        at = block * stride
        gathered[at : at + 3, :] = frac_ref[:, cols]
        gathered[at + 8 : at + 11, :] = offset_ref[:, cols].astype(jnp.float32)
        gathered[at + 16 : at + 19, :] = velocity_ref[:, cols]
        gathered[at + 24 : at + 33, :] = affine_ref[:, cols]
        gathered[at + 40 : at + 46, :] = stress_ref[:, cols]
        row = T_MASS * blocks + block
        table[row : row + 1, :] = jnp.where(
            lane < count_ref[block], mass_ref[block : block + 1, :], 0.0
        )

    def dense(component):
        return gathered[pl.ds(component, blocks, stride=stride), :]

    def put(index, value):
        table[index * blocks : (index + 1) * blocks, :] = value

    affine = [dense(24 + component) for component in range(9)]
    stress = stress_update([dense(40 + component) for component in range(6)], affine)
    for component in range(6):
        stress_out[component * blocks : (component + 1) * blocks, :] = stress[component]
    live_mass = table[T_MASS * blocks : (T_MASS + 1) * blocks, :]
    for row_dim in range(3):
        put(T_MV + row_dim, live_mass * dense(16 + row_dim))
        for col_dim in range(3):
            put(
                T_A + 3 * row_dim + col_dim,
                live_mass
                * (
                    affine[3 * row_dim + col_dim]
                    - stress_scale * stress[pair_index[row_dim][col_dim]]
                ),
            )
    spline = []
    for dim in range(3):
        fraction = dense(dim)
        spline.append(
            (
                0.5 * (1.5 - fraction) ** 2,
                0.75 - (fraction - 1.0) ** 2,
                0.5 * (fraction - 0.5) ** 2,
                dense(8 + dim),
                dense(8 + dim) + fraction,
            )
        )
    left, middle, right, offset, position = spline[0]
    for node in range(6):
        shifted = float(node) - offset
        weight = jnp.where(
            shifted == 0.0,
            left,
            jnp.where(shifted == 1.0, middle, jnp.where(shifted == 2.0, right, 0.0)),
        )
        put(T_WX + node, weight)
        put(T_WXD + node, weight * (float(node) - position))
    for index in range(5):
        put(T_LY + index, spline[1][index])
        put(T_LZ + index, spline[2][index])
    shared_ref[...] = table[: T_SHARED * blocks, :]
    for block in range(blocks):
        new_stress_ref[:, block * BLOCK : (block + 1) * BLOCK] = stress_out[
            pl.ds(block, 6, stride=blocks), :
        ]
    mom_ref[...] = jnp.zeros_like(mom_ref)
    grid_mass_ref[...] = jnp.zeros_like(grid_mass_ref)

    lanes = lax.broadcasted_iota(jnp.int32, (8, LANES), 1)
    gap = jnp.zeros((PITCH - 8, LANES), jnp.float32)
    blank = jnp.zeros((8, LANES), jnp.float32)

    def one(block, carry):
        def row(index):
            return jnp.broadcast_to(table[pl.ds(index * blocks + block, 1), :], (8, LANES))

        wy, wyd = axis_weights(row, T_LY, T_MY, T_RY, T_OY, T_Y)
        wz, wzd = axis_weights(row, T_LZ, T_MZ, T_RZ, T_OZ, T_Z)
        wx = [row(T_WX + node) for node in range(6)]
        wxd = [row(T_WXD + node) for node in range(6)]
        left_side = jnp.concatenate(
            [
                jnp.concatenate([w * wy for w in wx], axis=0),
                jnp.concatenate([w * wy for w in wxd], axis=0),
                jnp.concatenate([w * wyd for w in wx], axis=0),
            ],
            axis=1,
        )
        value_rows = [
            wz * row(T_MV + dim) + wzd * row(T_A + 3 * dim + 2) for dim in range(3)
        ] + [wz * row(T_MASS)]
        x_rows = [wz * row(T_A + 3 * dim) for dim in range(3)] + [blank]
        y_rows = [wz * row(T_A + 3 * dim + 1) for dim in range(3)] + [blank]
        right_side = jnp.concatenate(
            [
                jnp.concatenate([r[0], gap, r[1], gap, r[2], gap, r[3]], axis=0)
                for r in (value_rows, x_rows, y_rows)
            ],
            axis=1,
        )
        left_high, left_low = split(left_side)
        right_high, right_low = split(right_side)

        def product(a, b):
            return lax.dot_general(
                a, b, (((1,), (1,)), ((), ())), preferred_element_type=jnp.float32
            )

        sums = (
            product(left_high, right_high)
            + product(left_high, right_low)
            + product(left_low, right_high)
        )
        tile_x, tile_y, tile_z = tile_coords(tile_ref, block)
        for node in range(6):
            part = sums[8 * node : 8 * node + 8]
            at = pl.ds(pl.multiple_of((4 * tile_x + node) * PY + 4 * tile_y, 4), 8)
            mom_ref[at, :] += pltpu.roll(
                jnp.where(lanes < 3 * PITCH, part, 0.0), 4 * tile_z, axis=1
            )
            grid_mass_ref[at, :] += pltpu.roll(
                jnp.where(lanes >= 3 * PITCH, part, 0.0), 8 + 4 * tile_z, axis=1
            )
        return carry

    lax.fori_loop(0, blocks, one, 0)


def exchange_kernel(
    mom_in,
    mass_in,
    mom,
    mass,
    z_send,
    z_recv,
    xm_recv,
    xs_send,
    xs_recv,
    y_send,
    y_recv,
    e_send,
    e_recv,
    send_sem,
    recv_sem,
):
    axes = ("gx", "gy", "gz")
    me = {axis: lax.axis_index(axis) for axis in axes}
    count = {axis: lax.axis_size(axis) for axis in axes}

    def device(dx, dy, dz):
        return tuple(
            lax.rem(me[axis] + count[axis] + step, count[axis])
            for axis, step in zip(axes, (dx, dy, dz))
        )

    z_steps = [(0, 0, -1), (0, 0, 1)]
    x_steps = [(-1, 0, 0), (1, 0, 0)]
    y_steps = [(0, -1, 0), (0, 1, 0)]
    e_steps = [(-1, -1, 0), (-1, 1, 0), (1, -1, 0), (1, 1, 0)]
    barrier = pltpu.get_barrier_semaphore()
    for step in z_steps + x_steps + y_steps + e_steps:
        pl.semaphore_signal(barrier, inc=1, device_id=device(*step), device_id_type=MESH)

    def copy(src, dst, slot, step):
        return pltpu.make_async_remote_copy(
            src_ref=src,
            dst_ref=dst,
            send_sem=send_sem.at[slot],
            recv_sem=recv_sem.at[slot],
            device_id=device(*step),
            device_id_type=MESH,
        )

    lane = lax.broadcasted_iota(jnp.int32, (PY, LANES), 1)
    in_mom = lane < 3 * PITCH
    in_pitch = lax.rem(lane, PITCH)
    third = PY // 3
    lane3 = lane[:third]
    in_pitch3 = in_pitch[:third]
    in_mom3 = in_mom[:third]

    for side in range(2):
        shift = 0 if side == 0 else LANES - CZ

        def pack(x, carry):
            packed, packed_mass = carry
            at = pl.ds(pl.multiple_of(x * PY, 8), PY)
            mine = (in_pitch >= 2 * x) & (in_pitch < 2 * x + 2) & in_mom
            packed = jnp.where(
                mine, pltpu.roll(mom_in[at, :], lax.rem(2 * x + shift, LANES), axis=1), packed
            )
            layer = mass_in[at, :]
            for group in range(3):
                start = PITCH * group
                here = (lane3 >= start + 2 * x) & (lane3 < start + 2 * x + 2)
                packed_mass = jnp.where(
                    here,
                    pltpu.roll(
                        layer[group * third : (group + 1) * third],
                        lax.rem(start + 2 * x + shift, LANES),
                        axis=1,
                    ),
                    packed_mass,
                )
            return packed, packed_mass

        packed, packed_mass = lax.fori_loop(
            0,
            PX,
            pack,
            (jnp.zeros((PY, LANES), jnp.float32), jnp.zeros((third, LANES), jnp.float32)),
        )
        z_send[side, :PY, :] = packed
        z_send[side, PY:, :] = packed_mass

    pl.semaphore_wait(barrier, 10)
    z_copies = [
        copy(z_send.at[side], z_recv.at[1 - side], side, z_steps[side]) for side in range(2)
    ]
    for c in z_copies:
        c.start()
    for c in z_copies:
        c.wait()

    low = (in_pitch < 2) & in_mom
    high = (in_pitch >= CZ) & (in_pitch < CZ + 2) & in_mom
    low3 = lane3 < 2
    high3 = (lane3 >= CZ) & (lane3 < CZ + 2)

    def unpack(x, carry):
        at = pl.ds(pl.multiple_of(x * PY, 8), PY)
        from_low = pltpu.roll(z_recv[0, :PY, :], lax.rem(LANES - 2 * x, LANES), axis=1)
        from_high = pltpu.roll(z_recv[1, :PY, :], lax.rem(LANES + CZ - 2 * x, LANES), axis=1)
        mom[at, :] = (
            mom_in[at, :] + jnp.where(low, from_low, 0.0) + jnp.where(high, from_high, 0.0)
        )
        for group in range(3):
            start = PITCH * group
            rows = pl.ds(pl.multiple_of(x * PY + group * third, 8), third)
            from_low = pltpu.roll(
                z_recv[0, PY:, :], lax.rem(2 * LANES - start - 2 * x, LANES), axis=1
            )
            from_high = pltpu.roll(
                z_recv[1, PY:, :], lax.rem(2 * LANES + CZ - start - 2 * x, LANES), axis=1
            )
            mass[rows, :] = (
                mass_in[rows, :]
                + jnp.where(low3, from_low, 0.0)
                + jnp.where(high3, from_high, 0.0)
            )
        return carry

    lax.fori_loop(0, PX, unpack, 0)

    firsts = (0, CX)
    y_firsts = (0, CY)
    copies = []
    for side in range(2):
        first = firsts[side] * PY
        xs_send[side] = mass[first : first + PY, :] + pltpu.roll(
            mass[first + PY : first + 2 * PY, :], 64, axis=1
        )
        copies.append(
            copy(
                mom.at[pl.ds(first, 2 * PY), :], xm_recv.at[1 - side], 2 + side, x_steps[side]
            )
        )
        copies.append(copy(xs_send.at[side], xs_recv.at[1 - side], 4 + side, x_steps[side]))
    for c in copies:
        c.start()
    more = []
    for side in range(2):
        y0 = y_firsts[side]
        y_send[side, 0:PX, :] = mom[pl.ds(y0, PX, stride=PY), :]
        y_send[side, 24 : 24 + PX, :] = mom[pl.ds(y0 + 1, PX, stride=PY), :]
        y_send[side, 48 : 48 + PX, :] = mass[pl.ds(y0, PX, stride=PY), :] + pltpu.roll(
            mass[pl.ds(y0 + 1, PX, stride=PY), :], 64, axis=1
        )
        y_send[side, PX:24, :] = jnp.zeros((24 - PX, LANES), jnp.float32)
        y_send[side, 24 + PX : 48, :] = jnp.zeros((24 - PX, LANES), jnp.float32)
        y_send[side, 48 + PX : 72, :] = jnp.zeros((24 - PX, LANES), jnp.float32)
        more.append(copy(y_send.at[side], y_recv.at[1 - side], 6 + side, y_steps[side]))
    for edge in range(4):
        x0, y0 = firsts[edge // 2], y_firsts[edge % 2]
        for layer in range(2):
            at = (x0 + layer) * PY + y0
            e_send[edge, 2 * layer : 2 * layer + 2, :] = mom[at : at + 2, :]
            e_send[edge, 4 + 2 * layer : 6 + 2 * layer, :] = mass[at : at + 2, :]
        more.append(copy(e_send.at[edge], e_recv.at[3 - edge], 8 + edge, e_steps[edge]))
    for c in more:
        c.start()
    for c in copies + more:
        c.wait()
    front = lane < 64
    front_x = lax.broadcasted_iota(jnp.int32, (PX, LANES), 1) < 64
    for side in range(2):
        first = firsts[side] * PY
        mom[first : first + 2 * PY, :] += xm_recv[side]
        got = xs_recv[side]
        mass[first : first + PY, :] += jnp.where(front, got, 0.0)
        mass[first + PY : first + 2 * PY, :] += jnp.where(
            front, pltpu.roll(got, 64, axis=1), 0.0
        )
    for side in range(2):
        y0 = y_firsts[side]
        got = y_recv[side, 48 : 48 + PX, :]
        at0 = pl.ds(y0, PX, stride=PY)
        at1 = pl.ds(y0 + 1, PX, stride=PY)
        mom[at0, :] = mom[at0, :] + y_recv[side, 0:PX, :]
        mom[at1, :] = mom[at1, :] + y_recv[side, 24 : 24 + PX, :]
        mass[at0, :] = mass[at0, :] + jnp.where(front_x, got, 0.0)
        mass[at1, :] = mass[at1, :] + jnp.where(front_x, pltpu.roll(got, 64, axis=1), 0.0)
    for edge in range(4):
        x0, y0 = firsts[edge // 2], y_firsts[edge % 2]
        for layer in range(2):
            at = (x0 + layer) * PY + y0
            mom[at : at + 2, :] += e_recv[edge, 2 * layer : 2 * layer + 2, :]
            mass[at : at + 2, :] += e_recv[edge, 4 + 2 * layer : 6 + 2 * layer, :]


def collect_kernel(
    tile_ref,
    mom_ref,
    mass_ref,
    shared_ref,
    new_velocity_ref,
    new_affine_ref,
    grid_velocity_ref,
    velocity,
    partial,
    final,
):
    blocks = tile_ref.shape[0]
    width_x = lax.axis_size("gx") * CX
    height_y = lax.axis_size("gy") * CY
    depth_z = lax.axis_size("gz") * CZ
    lane = lax.broadcasted_iota(jnp.int32, (PY, LANES), 1)
    row_index = lax.broadcasted_iota(jnp.int32, (PY, LANES), 0)
    first_z = lax.axis_index("gz") * CZ
    first_y = lax.axis_index("gy") * CY
    first_x = lax.axis_index("gx") * CX
    z_index = lax.rem(lane - 2 * PITCH - 1 + first_z + depth_z, depth_z)
    y_index = lax.rem(row_index - 1 + first_y + height_y, height_y)
    is_y = (lane >= PITCH) & (lane < 2 * PITCH)
    is_z = (lane >= 2 * PITCH) & (lane < 3 * PITCH)
    z_floor = is_z & (z_index < 2)
    z_top = is_z & (z_index >= depth_z - 2)
    y_floor = is_y & (y_index < 2)
    fall = jnp.where(is_y, time_step * gravity, 0.0)

    def layer(x, carry):
        at = pl.ds(pl.multiple_of(x * PY, 8), PY)
        x_index = lax.rem(first_x + x - 1 + width_x, width_x)
        outlet = (x_index >= width_x // 4) & (x_index < width_x - width_x // 4)
        inverse = 1.0 / (mass_ref[at, :] + mass_floor)
        inverse = jnp.where(
            lane < PITCH,
            inverse,
            jnp.where(
                is_y, pltpu.roll(inverse, PITCH, axis=1), pltpu.roll(inverse, 2 * PITCH, axis=1)
            ),
        )
        values = mom_ref[at, :] * inverse - fall
        lifted = jnp.maximum(values, 0.0)
        values = jnp.where(
            z_floor | (y_floor & jnp.logical_not(outlet)), lifted, values
        )
        values = jnp.where(z_top, jnp.minimum(values, 0.0), values)
        velocity[at, :] = values
        return carry

    lax.fori_loop(0, PX, layer, 0)

    def output(x, carry):
        rows = velocity[pl.ds((x + 1) * PY + 1, CY), :]
        for dim in range(3):
            grid_velocity_ref[dim, x] = pltpu.roll(
                rows, LANES - PITCH * dim - 1, axis=1
            )[:, :CZ]
        return carry

    lax.fori_loop(0, CX, output, 0)

    lanes = lax.broadcasted_iota(jnp.int32, (8, LANES), 1)

    def one(block, carry):
        def row(index):
            return jnp.broadcast_to(shared_ref[pl.ds(index * blocks + block, 1), :], (8, LANES))

        wy, wyd = axis_weights(row, T_LY, T_MY, T_RY, T_OY, T_Y)
        wz, wzd = axis_weights(row, T_LZ, T_MZ, T_RZ, T_OZ, T_Z)
        wx = [row(T_WX + node) for node in range(6)]
        wxd = [row(T_WXD + node) for node in range(6)]
        right_side = jnp.concatenate(
            [
                jnp.concatenate([w * wz for w in wx], axis=0),
                jnp.concatenate([w * wz for w in wxd], axis=0),
                jnp.concatenate([w * wzd for w in wx], axis=0),
            ],
            axis=1,
        )
        tile_x, tile_y, tile_z = tile_coords(tile_ref, block)
        planes = []
        for node in range(6):
            at = pl.ds(pl.multiple_of((4 * tile_x + node) * PY + 4 * tile_y, 4), 8)
            planes.append(velocity[at, :])
        rows = []
        for dim in range(3):
            merged = None
            for node in range(6):
                moved = pltpu.roll(
                    planes[node],
                    lax.rem(2 * LANES + 8 * node - PITCH * dim - 4 * tile_z, LANES),
                    axis=1,
                )
                merged = moved if merged is None else jnp.where(lanes < 8 * node, merged, moved)
            rows.append(merged)
        left_side = jnp.concatenate(rows, axis=0)[:, :48]
        left_high, left_low = split(left_side)
        right_high, right_low = split(right_side)
        sums = (
            jnp.dot(left_high, right_high, preferred_element_type=jnp.float32)
            + jnp.dot(left_high, right_low, preferred_element_type=jnp.float32)
            + jnp.dot(left_low, right_high, preferred_element_type=jnp.float32)
        )
        for dim in range(3):
            part = sums[8 * dim : 8 * dim + 8]
            terms = (
                (dim, wy * part[:, :128]),
                (3 + 3 * dim, wy * part[:, 128:256]),
                (4 + 3 * dim, wyd * part[:, :128]),
                (5 + 3 * dim, wy * part[:, 256:]),
            )
            for component, value in terms:
                at = pl.ds(pl.multiple_of(component * 8 * blocks + 8 * block, 8), 8)
                partial[at, :] = value
        return carry

    lax.fori_loop(0, blocks, one, 0)
    for component in range(12):
        total = partial[pl.ds(component * 8 * blocks, blocks, stride=8), :]
        for node in range(1, 6):
            total = total + partial[pl.ds(component * 8 * blocks + node, blocks, stride=8), :]
        if component >= 3:
            total = 4.0 * total
        final[component * blocks : (component + 1) * blocks, :] = total
    for block in range(blocks):
        cols = slice(block * BLOCK, (block + 1) * BLOCK)
        new_velocity_ref[:, cols] = final[pl.ds(block, 3, stride=blocks), :]
        new_affine_ref[:, cols] = final[pl.ds(3 * blocks + block, 9, stride=blocks), :]


def shards(
    point_frac,
    cell_offset,
    point_velocity,
    point_affine,
    point_stress,
    point_mass,
    block_tile,
    block_count,
):
    blocks = block_tile.shape[0]
    points = blocks * BLOCK
    vmem = pl.BlockSpec(memory_space=pltpu.VMEM)
    smem = pl.BlockSpec(memory_space=pltpu.SMEM)
    f32 = jnp.float32
    grid_shape = jax.ShapeDtypeStruct((ROWS, LANES), f32)
    new_stress, mom, mass, shared = pl.pallas_call(
        deposit_kernel,
        name="deposit",
        out_shape=(
            jax.ShapeDtypeStruct((6, points), f32),
            grid_shape,
            grid_shape,
            jax.ShapeDtypeStruct((T_SHARED * blocks, LANES), f32),
        ),
        in_specs=[smem, smem] + [vmem] * 6,
        out_specs=(vmem,) * 4,
        scratch_shapes=[
            pltpu.VMEM((48 * blocks, LANES), f32),
            pltpu.VMEM((T_ALL * blocks, LANES), f32),
            pltpu.VMEM((8 * blocks, LANES), f32),
        ],
    )(
        block_tile,
        block_count,
        point_frac,
        cell_offset,
        point_velocity,
        point_affine,
        point_stress,
        point_mass.reshape(blocks, BLOCK),
    )
    mom, mass = pl.pallas_call(
        exchange_kernel,
        name="exchange",
        out_shape=(grid_shape, grid_shape),
        in_specs=[vmem] * 2,
        out_specs=(vmem,) * 2,
        scratch_shapes=[
            pltpu.VMEM((2, PY + PY // 3, LANES), f32),
            pltpu.VMEM((2, PY + PY // 3, LANES), f32),
            pltpu.VMEM((2, 2 * PY, LANES), f32),
            pltpu.VMEM((2, PY, LANES), f32),
            pltpu.VMEM((2, PY, LANES), f32),
            pltpu.VMEM((2, 72, LANES), f32),
            pltpu.VMEM((2, 72, LANES), f32),
            pltpu.VMEM((4, 8, LANES), f32),
            pltpu.VMEM((4, 8, LANES), f32),
            pltpu.SemaphoreType.DMA((12,)),
            pltpu.SemaphoreType.DMA((12,)),
        ],
        compiler_params=pltpu.CompilerParams(collective_id=0, has_side_effects=True),
    )(mom, mass)
    new_velocity, new_affine, grid_velocity = pl.pallas_call(
        collect_kernel,
        name="collect",
        out_shape=(
            jax.ShapeDtypeStruct((3, points), f32),
            jax.ShapeDtypeStruct((9, points), f32),
            jax.ShapeDtypeStruct((3, CX, CY, CZ), f32),
        ),
        in_specs=[smem] + [vmem] * 3,
        out_specs=(vmem,) * 3,
        scratch_shapes=[
            pltpu.VMEM((ROWS, LANES), f32),
            pltpu.VMEM((12 * 8 * blocks, LANES), f32),
            pltpu.VMEM((12 * blocks, LANES), f32),
        ],
    )(block_tile, mom, mass, shared)
    return (new_velocity, new_affine, new_stress, grid_velocity)


def solution(mesh):
    points = P(None, ("gx", "gy", "gz"))
    flat = P(("gx", "gy", "gz"))
    return jax.shard_map(
        shards,
        mesh=mesh,
        in_specs=(points,) * 5 + (flat,) * 3,
        out_specs=(points, points, points, P(None, "gx", "gy", "gz")),
        check_vma=False,
    )
```

```python
import jax
import jax.numpy as jnp
from jax import lax
from jax.experimental import pallas as pl
from jax.experimental.pallas import tpu as pltpu
from jax.sharding import PartitionSpec as P

CX = 16
CY = 64
CZ = 32
BLOCK = 128

time_step = 0.1
gravity = 1.0
shear_modulus = 2.0
bulk_modulus = 4.0
friction_static = 0.38
friction_limit = 0.64
inertial_ref = 0.28
grain_size = 0.5
grain_density = 1.0
pressure_floor = 0.5
shear_floor = 0.5
mass_floor = 0.05
stress_scale = 0.4
pair_index = ((0, 5, 4), (5, 1, 3), (4, 3, 2))
component_pairs = ((0, 0), (1, 1), (2, 2), (1, 2), (0, 2), (0, 1))

PX = CX + 2
PY = 72
PITCH = 40
LANES = 128
ROWS = PX * PY
GROUP = 4
VMEM_LIMIT = 16 * 1024 * 1024
MESH = pl.DeviceIdType.MESH

T_WX, T_WXD = 0, 6
T_LY, T_MY, T_RY, T_OY, T_Y = 12, 13, 14, 15, 16
T_LZ, T_MZ, T_RZ, T_OZ, T_Z = 17, 18, 19, 20, 21
T_SHARED = 22
T_MASS, T_MV, T_A = 22, 23, 26
T_ALL = 35


def stress_update(stress, affine):
    strain_rate = [
        [
            0.5 * (affine[3 * row_dim + col_dim] + affine[3 * col_dim + row_dim])
            for col_dim in range(3)
        ]
        for row_dim in range(3)
    ]
    volume_rate = strain_rate[0][0] + strain_rate[1][1] + strain_rate[2][2]
    deviator = [
        [
            strain_rate[row_dim][col_dim] - (volume_rate / 3.0 if row_dim == col_dim else 0.0)
            for col_dim in range(3)
        ]
        for row_dim in range(3)
    ]
    trial_stress = []
    for component in range(6):
        row_dim, col_dim = component_pairs[component]
        value = stress[component] + time_step * 2.0 * shear_modulus * deviator[row_dim][col_dim]
        if component < 3:
            value = value + time_step * bulk_modulus * volume_rate
        trial_stress.append(value)
    pressure = -(trial_stress[0] + trial_stress[1] + trial_stress[2]) / 3.0
    shear_part = [trial_stress[component] + pressure for component in range(3)] + trial_stress[3:]
    shear_stress = jnp.sqrt(
        0.5 * (shear_part[0] ** 2 + shear_part[1] ** 2 + shear_part[2] ** 2)
        + shear_part[3] ** 2
        + shear_part[4] ** 2
        + shear_part[5] ** 2
    )
    shear_rate = jnp.sqrt(
        2.0
        * (
            deviator[0][0] ** 2
            + deviator[1][1] ** 2
            + deviator[2][2] ** 2
            + 2.0 * (deviator[1][2] ** 2 + deviator[0][2] ** 2 + deviator[0][1] ** 2)
        )
    )
    inertial = (
        shear_rate * grain_size / jnp.sqrt(jnp.maximum(pressure, pressure_floor) / grain_density)
    )
    friction = friction_static + (friction_limit - friction_static) * inertial / (
        inertial_ref + inertial
    )
    support = jnp.maximum(pressure, 0.0)
    factor = jnp.minimum(1.0, friction * support / jnp.maximum(shear_stress, shear_floor))
    return [shear_part[component] * factor - support for component in range(3)] + [
        shear_part[component] * factor for component in range(3, 6)
    ]


def split(values):
    high = values.astype(jnp.bfloat16)
    low = (values - high.astype(jnp.float32)).astype(jnp.bfloat16)
    return high, low


def tile_coords(tile_ref, block):
    tile = tile_ref[block]
    return tile >> 7, (tile >> 3) & 15, tile & 7


def axis_weights(row, left, middle, right, offset, position):
    index = lax.broadcasted_iota(jnp.int32, (8, LANES), 0).astype(jnp.float32)
    shifted = index - row(offset)
    weight = jnp.where(
        shifted == 0.0,
        row(left),
        jnp.where(shifted == 1.0, row(middle), jnp.where(shifted == 2.0, row(right), 0.0)),
    )
    return weight, weight * (index - row(position))


def deposit_kernel(
    tile_ref,
    count_ref,
    frac_ref,
    offset_ref,
    velocity_ref,
    affine_ref,
    stress_ref,
    mass_ref,
    new_stress_ref,
    mom_ref,
    grid_mass_ref,
    shared_ref,
    gathered,
    table,
    stress_out,
):
    blocks = mass_ref.shape[0]
    lane = lax.broadcasted_iota(jnp.int32, (1, LANES), 1)
    stride = 48
    for block in range(blocks):
        cols = slice(block * BLOCK, (block + 1) * BLOCK)
        at = block * stride
        gathered[at : at + 3, :] = frac_ref[:, cols]
        gathered[at + 8 : at + 11, :] = offset_ref[:, cols].astype(jnp.float32)
        gathered[at + 16 : at + 19, :] = velocity_ref[:, cols]
        gathered[at + 24 : at + 33, :] = affine_ref[:, cols]
        gathered[at + 40 : at + 46, :] = stress_ref[:, cols]
        row = T_MASS * blocks + block
        table[row : row + 1, :] = jnp.where(
            lane < count_ref[block], mass_ref[block : block + 1, :], 0.0
        )

    def dense(component):
        return gathered[pl.ds(component, blocks, stride=stride), :]

    def put(index, value):
        table[index * blocks : (index + 1) * blocks, :] = value

    affine = [dense(24 + component) for component in range(9)]
    stress = stress_update([dense(40 + component) for component in range(6)], affine)
    for component in range(6):
        stress_out[component * blocks : (component + 1) * blocks, :] = stress[component]
    live_mass = table[T_MASS * blocks : (T_MASS + 1) * blocks, :]
    for row_dim in range(3):
        put(T_MV + row_dim, live_mass * dense(16 + row_dim))
        for col_dim in range(3):
            put(
                T_A + 3 * row_dim + col_dim,
                live_mass
                * (
                    affine[3 * row_dim + col_dim]
                    - stress_scale * stress[pair_index[row_dim][col_dim]]
                ),
            )
    spline = []
    for dim in range(3):
        fraction = dense(dim)
        spline.append(
            (
                0.5 * (1.5 - fraction) ** 2,
                0.75 - (fraction - 1.0) ** 2,
                0.5 * (fraction - 0.5) ** 2,
                dense(8 + dim),
                dense(8 + dim) + fraction,
            )
        )
    left, middle, right, offset, position = spline[0]
    for node in range(6):
        shifted = float(node) - offset
        weight = jnp.where(
            shifted == 0.0,
            left,
            jnp.where(shifted == 1.0, middle, jnp.where(shifted == 2.0, right, 0.0)),
        )
        put(T_WX + node, weight)
        put(T_WXD + node, weight * (float(node) - position))
    for index in range(5):
        put(T_LY + index, spline[1][index])
        put(T_LZ + index, spline[2][index])
    shared_ref[...] = table[: T_SHARED * blocks, :]
    for block in range(blocks):
        new_stress_ref[:, block * BLOCK : (block + 1) * BLOCK] = stress_out[
            pl.ds(block, 6, stride=blocks), :
        ]
    mom_ref[...] = jnp.zeros_like(mom_ref)
    grid_mass_ref[...] = jnp.zeros_like(grid_mass_ref)

    lanes = lax.broadcasted_iota(jnp.int32, (8, 32), 1)
    channel = [(lanes >= 8 * index) & (lanes < 8 * index + 8) for index in range(4)]
    rest = jnp.zeros((8, LANES - 32), jnp.float32)
    blank = jnp.zeros((8, LANES), jnp.float32)

    def block_sums(block):
        def row(index):
            return jnp.broadcast_to(table[pl.ds(index * blocks + block, 1), :], (8, LANES))

        wy, wyd = axis_weights(row, T_LY, T_MY, T_RY, T_OY, T_Y)
        wz, wzd = axis_weights(row, T_LZ, T_MZ, T_RZ, T_OZ, T_Z)
        wx = [row(T_WX + node) for node in range(6)]
        wxd = [row(T_WXD + node) for node in range(6)]
        left_side = jnp.concatenate(
            [
                jnp.concatenate([w * wy for w in wx], axis=0),
                jnp.concatenate([w * wy for w in wxd], axis=0),
                jnp.concatenate([w * wyd for w in wx], axis=0),
            ],
            axis=1,
        )
        value_rows = [
            wz * row(T_MV + dim) + wzd * row(T_A + 3 * dim + 2) for dim in range(3)
        ] + [wz * row(T_MASS)]
        x_rows = [wz * row(T_A + 3 * dim) for dim in range(3)] + [blank]
        y_rows = [wz * row(T_A + 3 * dim + 1) for dim in range(3)] + [blank]
        right_side = jnp.concatenate(
            [jnp.concatenate(r, axis=0) for r in (value_rows, x_rows, y_rows)], axis=1
        )
        left_high, left_low = split(left_side)
        right_high, right_low = split(right_side)

        def product(a, b):
            return lax.dot_general(
                a, b, (((1,), (1,)), ((), ())), preferred_element_type=jnp.float32
            )

        return (
            product(left_high, right_high)
            + product(left_high, right_low)
            + product(left_low, right_high)
        )

    def scatter(block, sums):
        tile_x, tile_y, tile_z = tile_coords(tile_ref, block)
        starts = (0, PITCH - 8, 2 * PITCH - 16, LANES - 24)
        places, moved = [], []
        for node in range(6):
            part = sums[8 * node : 8 * node + 8]
            places.append(pl.ds(pl.multiple_of((4 * tile_x + node) * PY + 4 * tile_y, 4), 8))
            moved.append(
                [
                    pltpu.roll(
                        jnp.concatenate([jnp.where(channel[index], part, 0.0), rest], axis=1),
                        starts[index] + 4 * tile_z,
                        axis=1,
                    )
                    for index in range(4)
                ]
            )
        mom = [mom_ref[at, :] for at in places]
        mass = [grid_mass_ref[at, :] for at in places]
        for node, at in enumerate(places):
            mom_ref[at, :] = mom[node] + moved[node][0] + moved[node][1] + moved[node][2]
            grid_mass_ref[at, :] = mass[node] + moved[node][3]

    def group_sums(step):
        return tuple(block_sums(step * GROUP + member) for member in range(GROUP))

    def group_scatter(step, sums):
        for member in range(GROUP):
            scatter(step * GROUP + member, sums[member])

    def group(step, sums):
        following = group_sums(step)
        group_scatter(step - 1, sums)
        return following

    steps = blocks // GROUP
    group_scatter(steps - 1, lax.fori_loop(1, steps, group, group_sums(0)))


def exchange_kernel(
    mom_in,
    mass_in,
    mom,
    mass,
    z_send,
    z_recv,
    xm_recv,
    xs_send,
    xs_recv,
    y_send,
    y_recv,
    e_send,
    e_recv,
    send_sem,
    recv_sem,
):
    axes = ("gx", "gy", "gz")
    me = {axis: lax.axis_index(axis) for axis in axes}
    count = {axis: lax.axis_size(axis) for axis in axes}

    def device(dx, dy, dz):
        return tuple(
            lax.rem(me[axis] + count[axis] + step, count[axis])
            for axis, step in zip(axes, (dx, dy, dz))
        )

    z_steps = [(0, 0, -1), (0, 0, 1)]
    x_steps = [(-1, 0, 0), (1, 0, 0)]
    y_steps = [(0, -1, 0), (0, 1, 0)]
    e_steps = [(-1, -1, 0), (-1, 1, 0), (1, -1, 0), (1, 1, 0)]
    barrier = pltpu.get_barrier_semaphore()
    for step in z_steps + x_steps + y_steps + e_steps:
        pl.semaphore_signal(barrier, inc=1, device_id=device(*step), device_id_type=MESH)

    def copy(src, dst, slot, step):
        return pltpu.make_async_remote_copy(
            src_ref=src,
            dst_ref=dst,
            send_sem=send_sem.at[slot],
            recv_sem=recv_sem.at[slot],
            device_id=device(*step),
            device_id_type=MESH,
        )

    lane = lax.broadcasted_iota(jnp.int32, (PY, LANES), 1)
    in_mom = lane < 3 * PITCH
    in_pitch = lax.rem(lane, PITCH)
    third = PY // 3
    lane3 = lane[:third]
    in_pitch3 = in_pitch[:third]
    in_mom3 = in_mom[:third]

    for side in range(2):
        shift = 0 if side == 0 else LANES - CZ

        def pack(x, carry):
            packed, packed_mass = carry
            at = pl.ds(pl.multiple_of(x * PY, 8), PY)
            mine = (in_pitch >= 2 * x) & (in_pitch < 2 * x + 2) & in_mom
            packed = jnp.where(
                mine, pltpu.roll(mom_in[at, :], lax.rem(2 * x + shift, LANES), axis=1), packed
            )
            layer = mass_in[at, :]
            for group in range(3):
                start = PITCH * group
                here = (lane3 >= start + 2 * x) & (lane3 < start + 2 * x + 2)
                packed_mass = jnp.where(
                    here,
                    pltpu.roll(
                        layer[group * third : (group + 1) * third],
                        lax.rem(start + 2 * x + shift, LANES),
                        axis=1,
                    ),
                    packed_mass,
                )
            return packed, packed_mass

        packed, packed_mass = lax.fori_loop(
            0,
            PX,
            pack,
            (jnp.zeros((PY, LANES), jnp.float32), jnp.zeros((third, LANES), jnp.float32)),
        )
        z_send[side, :PY, :] = packed
        z_send[side, PY:, :] = packed_mass

    pl.semaphore_wait(barrier, 10)
    z_copies = [
        copy(z_send.at[side], z_recv.at[1 - side], side, z_steps[side]) for side in range(2)
    ]
    for c in z_copies:
        c.start()
    for c in z_copies:
        c.wait()

    low = (in_pitch < 2) & in_mom
    high = (in_pitch >= CZ) & (in_pitch < CZ + 2) & in_mom
    low3 = lane3 < 2
    high3 = (lane3 >= CZ) & (lane3 < CZ + 2)

    def unpack(x, carry):
        at = pl.ds(pl.multiple_of(x * PY, 8), PY)
        from_low = pltpu.roll(z_recv[0, :PY, :], lax.rem(LANES - 2 * x, LANES), axis=1)
        from_high = pltpu.roll(z_recv[1, :PY, :], lax.rem(LANES + CZ - 2 * x, LANES), axis=1)
        mom[at, :] = (
            mom_in[at, :] + jnp.where(low, from_low, 0.0) + jnp.where(high, from_high, 0.0)
        )
        for group in range(3):
            start = PITCH * group
            rows = pl.ds(pl.multiple_of(x * PY + group * third, 8), third)
            from_low = pltpu.roll(
                z_recv[0, PY:, :], lax.rem(2 * LANES - start - 2 * x, LANES), axis=1
            )
            from_high = pltpu.roll(
                z_recv[1, PY:, :], lax.rem(2 * LANES + CZ - start - 2 * x, LANES), axis=1
            )
            mass[rows, :] = (
                mass_in[rows, :]
                + jnp.where(low3, from_low, 0.0)
                + jnp.where(high3, from_high, 0.0)
            )
        return carry

    lax.fori_loop(0, PX, unpack, 0)

    firsts = (0, CX)
    y_firsts = (0, CY)
    copies = []
    for side in range(2):
        first = firsts[side] * PY
        xs_send[side] = mass[first : first + PY, :] + pltpu.roll(
            mass[first + PY : first + 2 * PY, :], 64, axis=1
        )
        copies.append(
            copy(
                mom.at[pl.ds(first, 2 * PY), :], xm_recv.at[1 - side], 2 + side, x_steps[side]
            )
        )
        copies.append(copy(xs_send.at[side], xs_recv.at[1 - side], 4 + side, x_steps[side]))
    for c in copies:
        c.start()
    more = []
    for side in range(2):
        y0 = y_firsts[side]
        y_send[side, 0:PX, :] = mom[pl.ds(y0, PX, stride=PY), :]
        y_send[side, 24 : 24 + PX, :] = mom[pl.ds(y0 + 1, PX, stride=PY), :]
        y_send[side, 48 : 48 + PX, :] = mass[pl.ds(y0, PX, stride=PY), :] + pltpu.roll(
            mass[pl.ds(y0 + 1, PX, stride=PY), :], 64, axis=1
        )
        y_send[side, PX:24, :] = jnp.zeros((24 - PX, LANES), jnp.float32)
        y_send[side, 24 + PX : 48, :] = jnp.zeros((24 - PX, LANES), jnp.float32)
        y_send[side, 48 + PX : 72, :] = jnp.zeros((24 - PX, LANES), jnp.float32)
        more.append(copy(y_send.at[side], y_recv.at[1 - side], 6 + side, y_steps[side]))
    for edge in range(4):
        x0, y0 = firsts[edge // 2], y_firsts[edge % 2]
        for layer in range(2):
            at = (x0 + layer) * PY + y0
            e_send[edge, 2 * layer : 2 * layer + 2, :] = mom[at : at + 2, :]
            e_send[edge, 4 + 2 * layer : 6 + 2 * layer, :] = mass[at : at + 2, :]
        more.append(copy(e_send.at[edge], e_recv.at[3 - edge], 8 + edge, e_steps[edge]))
    for c in more:
        c.start()
    for c in copies + more:
        c.wait()
    front = lane < 64
    front_x = lax.broadcasted_iota(jnp.int32, (PX, LANES), 1) < 64
    for side in range(2):
        first = firsts[side] * PY
        mom[first : first + 2 * PY, :] += xm_recv[side]
        got = xs_recv[side]
        mass[first : first + PY, :] += jnp.where(front, got, 0.0)
        mass[first + PY : first + 2 * PY, :] += jnp.where(
            front, pltpu.roll(got, 64, axis=1), 0.0
        )
    for side in range(2):
        y0 = y_firsts[side]
        got = y_recv[side, 48 : 48 + PX, :]
        at0 = pl.ds(y0, PX, stride=PY)
        at1 = pl.ds(y0 + 1, PX, stride=PY)
        mom[at0, :] = mom[at0, :] + y_recv[side, 0:PX, :]
        mom[at1, :] = mom[at1, :] + y_recv[side, 24 : 24 + PX, :]
        mass[at0, :] = mass[at0, :] + jnp.where(front_x, got, 0.0)
        mass[at1, :] = mass[at1, :] + jnp.where(front_x, pltpu.roll(got, 64, axis=1), 0.0)
    for edge in range(4):
        x0, y0 = firsts[edge // 2], y_firsts[edge % 2]
        for layer in range(2):
            at = (x0 + layer) * PY + y0
            mom[at : at + 2, :] += e_recv[edge, 2 * layer : 2 * layer + 2, :]
            mass[at : at + 2, :] += e_recv[edge, 4 + 2 * layer : 6 + 2 * layer, :]


def collect_kernel(
    tile_ref,
    mom_ref,
    mass_ref,
    shared_ref,
    new_velocity_ref,
    new_affine_ref,
    grid_velocity_ref,
    velocity,
    partial,
    final,
):
    blocks = tile_ref.shape[0]
    width_x = lax.axis_size("gx") * CX
    height_y = lax.axis_size("gy") * CY
    depth_z = lax.axis_size("gz") * CZ
    lane = lax.broadcasted_iota(jnp.int32, (PY, LANES), 1)
    row_index = lax.broadcasted_iota(jnp.int32, (PY, LANES), 0)
    first_z = lax.axis_index("gz") * CZ
    first_y = lax.axis_index("gy") * CY
    first_x = lax.axis_index("gx") * CX
    z_index = lax.rem(lane - 2 * PITCH - 1 + first_z + depth_z, depth_z)
    y_index = lax.rem(row_index - 1 + first_y + height_y, height_y)
    is_y = (lane >= PITCH) & (lane < 2 * PITCH)
    is_z = (lane >= 2 * PITCH) & (lane < 3 * PITCH)
    z_floor = is_z & (z_index < 2)
    z_top = is_z & (z_index >= depth_z - 2)
    y_floor = is_y & (y_index < 2)
    fall = jnp.where(is_y, time_step * gravity, 0.0)

    def layer(x):
        at = pl.ds(pl.multiple_of(x * PY, 8), PY)
        x_index = lax.rem(first_x + x - 1 + width_x, width_x)
        outlet = (x_index >= width_x // 4) & (x_index < width_x - width_x // 4)
        inverse = 1.0 / (mass_ref[at, :] + mass_floor)
        inverse = jnp.where(
            lane < PITCH,
            inverse,
            jnp.where(
                is_y, pltpu.roll(inverse, PITCH, axis=1), pltpu.roll(inverse, 2 * PITCH, axis=1)
            ),
        )
        values = mom_ref[at, :] * inverse - fall
        lifted = jnp.maximum(values, 0.0)
        values = jnp.where(
            z_floor | (y_floor & jnp.logical_not(outlet)), lifted, values
        )
        values = jnp.where(z_top, jnp.minimum(values, 0.0), values)
        velocity[at, :] = values

    def layers(step, carry):
        for member in range(3):
            layer(3 * step + member)
        return carry

    lax.fori_loop(0, PX // 3, layers, 0)

    def output(step, carry):
        for member in range(4):
            x = 4 * step + member
            turned = jnp.transpose(velocity[pl.ds((x + 1) * PY + 1, CY), :])
            for dim in range(3):
                grid_velocity_ref[dim, x] = turned[PITCH * dim + 1 : PITCH * dim + 1 + CZ]
        return carry

    lax.fori_loop(0, CX // 4, output, 0)

    lanes = lax.broadcasted_iota(jnp.int32, (8, LANES), 1)

    def row_of(block):
        def row(index):
            return jnp.broadcast_to(shared_ref[pl.ds(index * blocks + block, 1), :], (8, LANES))

        return row

    def gather(block):
        tile_x, tile_y, tile_z = tile_coords(tile_ref, block)
        planes = []
        for node in range(6):
            at = pl.ds(pl.multiple_of((4 * tile_x + node) * PY + 4 * tile_y, 4), 8)
            planes.append(velocity[at, :])
        rows = []
        for dim in range(3):
            merged = None
            for node in range(6):
                moved = pltpu.roll(
                    planes[node],
                    LANES + 8 * node - PITCH * dim - 4 * tile_z,
                    axis=1,
                )
                merged = moved if merged is None else jnp.where(lanes < 8 * node, merged, moved)
            rows.append(merged)
        return jnp.concatenate(rows, axis=0)

    def contract(block, left_side):
        row = row_of(block)
        wz, wzd = axis_weights(row, T_LZ, T_MZ, T_RZ, T_OZ, T_Z)
        wx = [row(T_WX + node) for node in range(6)]
        wxd = [row(T_WXD + node) for node in range(6)]
        right_side = jnp.concatenate(
            [
                jnp.concatenate([w * wz for w in wx], axis=0),
                jnp.concatenate([w * wz for w in wxd], axis=0),
                jnp.concatenate([w * wzd for w in wx], axis=0),
            ],
            axis=1,
        )
        left_high, left_low = split(left_side[:, :48])
        right_high, right_low = split(right_side)
        both = jnp.dot(
            jnp.concatenate([left_high, left_low], axis=0),
            right_high,
            preferred_element_type=jnp.float32,
        )
        return (
            both[:24]
            + both[24:]
            + jnp.dot(left_high, right_low, preferred_element_type=jnp.float32)
        )

    def weigh(block, sums):
        wy, wyd = axis_weights(row_of(block), T_LY, T_MY, T_RY, T_OY, T_Y)
        for dim in range(3):
            part = sums[8 * dim : 8 * dim + 8]
            terms = (
                (dim, wy * part[:, :128]),
                (3 + 3 * dim, wy * part[:, 128:256]),
                (4 + 3 * dim, wyd * part[:, :128]),
                (5 + 3 * dim, wy * part[:, 256:]),
            )
            for component, value in terms:
                at = pl.ds(pl.multiple_of(component * 8 * blocks + 8 * block, 8), 8)
                partial[at, :] = value

    def of_group(function, step, *values):
        return tuple(
            function(step * GROUP + member, *(value[member] for value in values))
            for member in range(GROUP)
        )

    def group(step, carry):
        left_sides, sums = carry
        following = of_group(gather, step + 2)
        products = of_group(contract, step + 1, left_sides)
        of_group(weigh, step, sums)
        return following, products

    steps = blocks // GROUP
    carry = of_group(gather, 1), of_group(contract, 0, of_group(gather, 0))
    left_sides, sums = lax.fori_loop(0, steps - 2, group, carry)
    of_group(weigh, steps - 2, sums)
    of_group(weigh, steps - 1, of_group(contract, steps - 1, left_sides))
    for component in range(12):
        total = partial[pl.ds(component * 8 * blocks, blocks, stride=8), :]
        for node in range(1, 6):
            total = total + partial[pl.ds(component * 8 * blocks + node, blocks, stride=8), :]
        if component >= 3:
            total = 4.0 * total
        final[component * blocks : (component + 1) * blocks, :] = total
    for block in range(blocks):
        cols = slice(block * BLOCK, (block + 1) * BLOCK)
        new_velocity_ref[:, cols] = final[pl.ds(block, 3, stride=blocks), :]
        new_affine_ref[:, cols] = final[pl.ds(3 * blocks + block, 9, stride=blocks), :]


def shards(
    point_frac,
    cell_offset,
    point_velocity,
    point_affine,
    point_stress,
    point_mass,
    block_tile,
    block_count,
):
    blocks = block_tile.shape[0]
    points = blocks * BLOCK
    vmem = pl.BlockSpec(memory_space=pltpu.VMEM)
    smem = pl.BlockSpec(memory_space=pltpu.SMEM)
    f32 = jnp.float32
    grid_shape = jax.ShapeDtypeStruct((ROWS, LANES), f32)
    new_stress, mom, mass, shared = pl.pallas_call(
        deposit_kernel,
        name="deposit",
        out_shape=(
            jax.ShapeDtypeStruct((6, points), f32),
            grid_shape,
            grid_shape,
            jax.ShapeDtypeStruct((T_SHARED * blocks, LANES), f32),
        ),
        in_specs=[smem, smem] + [vmem] * 6,
        out_specs=(vmem,) * 4,
        scratch_shapes=[
            pltpu.VMEM((48 * blocks, LANES), f32),
            pltpu.VMEM((T_ALL * blocks, LANES), f32),
            pltpu.VMEM((8 * blocks, LANES), f32),
        ],
        compiler_params=pltpu.CompilerParams(vmem_limit_bytes=VMEM_LIMIT),
    )(
        block_tile,
        block_count,
        point_frac,
        cell_offset,
        point_velocity,
        point_affine,
        point_stress,
        point_mass.reshape(blocks, BLOCK),
    )
    mom, mass = pl.pallas_call(
        exchange_kernel,
        name="exchange",
        out_shape=(grid_shape, grid_shape),
        in_specs=[vmem] * 2,
        out_specs=(vmem,) * 2,
        scratch_shapes=[
            pltpu.VMEM((2, PY + PY // 3, LANES), f32),
            pltpu.VMEM((2, PY + PY // 3, LANES), f32),
            pltpu.VMEM((2, 2 * PY, LANES), f32),
            pltpu.VMEM((2, PY, LANES), f32),
            pltpu.VMEM((2, PY, LANES), f32),
            pltpu.VMEM((2, 72, LANES), f32),
            pltpu.VMEM((2, 72, LANES), f32),
            pltpu.VMEM((4, 8, LANES), f32),
            pltpu.VMEM((4, 8, LANES), f32),
            pltpu.SemaphoreType.DMA((12,)),
            pltpu.SemaphoreType.DMA((12,)),
        ],
        compiler_params=pltpu.CompilerParams(
            collective_id=0, has_side_effects=True, vmem_limit_bytes=VMEM_LIMIT
        ),
    )(mom, mass)
    new_velocity, new_affine, grid_velocity = pl.pallas_call(
        collect_kernel,
        name="collect",
        out_shape=(
            jax.ShapeDtypeStruct((3, points), f32),
            jax.ShapeDtypeStruct((9, points), f32),
            jax.ShapeDtypeStruct((3, CX, CZ, CY), f32),
        ),
        in_specs=[smem] + [vmem] * 3,
        out_specs=(vmem,) * 3,
        scratch_shapes=[
            pltpu.VMEM((ROWS, LANES), f32),
            pltpu.VMEM((12 * 8 * blocks, LANES), f32),
            pltpu.VMEM((12 * blocks, LANES), f32),
        ],
        compiler_params=pltpu.CompilerParams(vmem_limit_bytes=VMEM_LIMIT),
    )(block_tile, mom, mass, shared)
    return (new_velocity, new_affine, new_stress, jnp.swapaxes(grid_velocity, 2, 3))


def solution(mesh):
    points = P(None, ("gx", "gy", "gz"))
    flat = P(("gx", "gy", "gz"))
    return jax.shard_map(
        shards,
        mesh=mesh,
        in_specs=(points,) * 5 + (flat,) * 3,
        out_specs=(points, points, points, P(None, "gx", "gy", "gz")),
        check_vma=False,
    )
```

```python
import jax
import jax.numpy as jnp
from jax import lax
from jax.experimental import pallas as pl
from jax.experimental.pallas import tpu as pltpu
from jax.sharding import PartitionSpec as P

CX = 16
CY = 64
CZ = 32
BLOCK = 128

time_step = 0.1
gravity = 1.0
shear_modulus = 2.0
bulk_modulus = 4.0
friction_static = 0.38
friction_limit = 0.64
inertial_ref = 0.28
grain_size = 0.5
grain_density = 1.0
pressure_floor = 0.5
shear_floor = 0.5
mass_floor = 0.05
stress_scale = 0.4
pair_index = ((0, 5, 4), (5, 1, 3), (4, 3, 2))
component_pairs = ((0, 0), (1, 1), (2, 2), (1, 2), (0, 2), (0, 1))

PX = CX + 2
PY = 72
PITCH = 40
LANES = 128
ROWS = PX * PY
GROUP = 4
VMEM_LIMIT = 16 * 1024 * 1024
MESH = pl.DeviceIdType.MESH

T_WX, T_WXD = 0, 6
T_LY, T_MY, T_RY, T_OY, T_Y = 12, 13, 14, 15, 16
T_LZ, T_MZ, T_RZ, T_OZ, T_Z = 17, 18, 19, 20, 21
T_SHARED = 22
T_MASS, T_MV, T_A = 22, 23, 26
T_ALL = 35


def stress_update(stress, affine):
    strain_rate = [
        [
            0.5 * (affine[3 * row_dim + col_dim] + affine[3 * col_dim + row_dim])
            for col_dim in range(3)
        ]
        for row_dim in range(3)
    ]
    volume_rate = strain_rate[0][0] + strain_rate[1][1] + strain_rate[2][2]
    deviator = [
        [
            strain_rate[row_dim][col_dim] - (volume_rate / 3.0 if row_dim == col_dim else 0.0)
            for col_dim in range(3)
        ]
        for row_dim in range(3)
    ]
    trial_stress = []
    for component in range(6):
        row_dim, col_dim = component_pairs[component]
        value = stress[component] + time_step * 2.0 * shear_modulus * deviator[row_dim][col_dim]
        if component < 3:
            value = value + time_step * bulk_modulus * volume_rate
        trial_stress.append(value)
    pressure = -(trial_stress[0] + trial_stress[1] + trial_stress[2]) / 3.0
    shear_part = [trial_stress[component] + pressure for component in range(3)] + trial_stress[3:]
    shear_stress = jnp.sqrt(
        0.5 * (shear_part[0] ** 2 + shear_part[1] ** 2 + shear_part[2] ** 2)
        + shear_part[3] ** 2
        + shear_part[4] ** 2
        + shear_part[5] ** 2
    )
    shear_rate = jnp.sqrt(
        2.0
        * (
            deviator[0][0] ** 2
            + deviator[1][1] ** 2
            + deviator[2][2] ** 2
            + 2.0 * (deviator[1][2] ** 2 + deviator[0][2] ** 2 + deviator[0][1] ** 2)
        )
    )
    inertial = (
        shear_rate * grain_size / jnp.sqrt(jnp.maximum(pressure, pressure_floor) / grain_density)
    )
    friction = friction_static + (friction_limit - friction_static) * inertial / (
        inertial_ref + inertial
    )
    support = jnp.maximum(pressure, 0.0)
    factor = jnp.minimum(1.0, friction * support / jnp.maximum(shear_stress, shear_floor))
    return [shear_part[component] * factor - support for component in range(3)] + [
        shear_part[component] * factor for component in range(3, 6)
    ]


def split(values):
    high = values.astype(jnp.bfloat16)
    low = (values - high.astype(jnp.float32)).astype(jnp.bfloat16)
    return high, low


def tile_coords(tile_ref, block):
    tile = tile_ref[block]
    return tile >> 7, (tile >> 3) & 15, tile & 7


def axis_weights(row, left, middle, right, offset, position):
    index = lax.broadcasted_iota(jnp.int32, (8, LANES), 0).astype(jnp.float32)
    shifted = index - row(offset)
    weight = jnp.where(
        shifted == 0.0,
        row(left),
        jnp.where(shifted == 1.0, row(middle), jnp.where(shifted == 2.0, row(right), 0.0)),
    )
    return weight, weight * (index - row(position))


def deposit_kernel(
    tile_hbm,
    count_hbm,
    frac_hbm,
    offset_hbm,
    velocity_hbm,
    affine_hbm,
    stress_hbm,
    mass_hbm,
    mom,
    mass,
    shared_ref,
    stress_out,
    tile_ref,
    count_ref,
    frac_ref,
    offset_ref,
    velocity_ref,
    affine_ref,
    stress_ref,
    mass_ref,
    gathered,
    table,
    placed_high,
    placed_low,
    z_send,
    z_recv,
    x_send,
    x_recv,
    y_send,
    y_recv,
    load_sem,
    send_sem,
    recv_sem,
):
    axes = ("gx", "gy", "gz")

    def device(dx, dy, dz):
        place = []
        for axis, step in zip(axes, (dx, dy, dz)):
            size = lax.axis_size(axis)
            moved = lax.axis_index(axis)
            if step:
                moved = moved + step
                moved = jnp.where(moved < 0, size - 1, jnp.where(moved >= size, 0, moved))
            place.append(moved)
        return tuple(place)

    z_sides = [device(0, 0, -1), device(0, 0, 1)]
    x_sides = [device(-1, 0, 0), device(1, 0, 0)]
    y_sides = [device(0, -1, 0), device(0, 1, 0)]
    barrier = pltpu.get_barrier_semaphore()
    for target in z_sides + x_sides + y_sides:
        pl.semaphore_signal(barrier, inc=1, device_id=target, device_id_type=MESH)
    loads = [
        pltpu.make_async_copy(source, target, load_sem.at[index])
        for index, (source, target) in enumerate(
            (
                (frac_hbm, frac_ref),
                (offset_hbm, offset_ref),
                (velocity_hbm, velocity_ref),
                (affine_hbm, affine_ref),
                (stress_hbm, stress_ref),
                (mass_hbm, mass_ref),
                (count_hbm, count_ref),
                (tile_hbm, tile_ref),
            )
        )
    ]
    for load in loads:
        load.start()

    blocks = mass_ref.shape[0]
    lane_row = lax.broadcasted_iota(jnp.int32, (1, LANES), 1)
    stride = 48
    for load in loads:
        load.wait()
    for block in range(blocks):
        cols = slice(block * BLOCK, (block + 1) * BLOCK)
        at = block * stride
        gathered[at : at + 3, :] = frac_ref[:, cols]
        gathered[at + 8 : at + 11, :] = offset_ref[:, cols].astype(jnp.float32)
        gathered[at + 16 : at + 19, :] = velocity_ref[:, cols]
        gathered[at + 24 : at + 33, :] = affine_ref[:, cols]
        gathered[at + 40 : at + 46, :] = stress_ref[:, cols]
        row = (T_MASS - T_SHARED) * blocks + block
        table[row : row + 1, :] = jnp.where(
            lane_row < count_ref[block], mass_ref[block : block + 1, :], 0.0
        )

    def dense(component):
        return gathered[pl.ds(component, blocks, stride=stride), :]

    def put(index, value):
        if index < T_SHARED:
            shared_ref[index * blocks : (index + 1) * blocks, :] = value
        else:
            start = (index - T_SHARED) * blocks
            table[start : start + blocks, :] = value

    affine = [dense(24 + component) for component in range(9)]
    stress = stress_update([dense(40 + component) for component in range(6)], affine)
    for component in range(6):
        stress_out[component * blocks : (component + 1) * blocks, :] = stress[component]
    live_mass = table[(T_MASS - T_SHARED) * blocks : (T_MASS - T_SHARED + 1) * blocks, :]
    for row_dim in range(3):
        put(T_MV + row_dim, live_mass * dense(16 + row_dim))
        for col_dim in range(3):
            put(
                T_A + 3 * row_dim + col_dim,
                live_mass
                * (
                    affine[3 * row_dim + col_dim]
                    - stress_scale * stress[pair_index[row_dim][col_dim]]
                ),
            )
    spline = []
    for dim in range(3):
        fraction = dense(dim)
        spline.append(
            (
                0.5 * (1.5 - fraction) ** 2,
                0.75 - (fraction - 1.0) ** 2,
                0.5 * (fraction - 0.5) ** 2,
                dense(8 + dim),
                dense(8 + dim) + fraction,
            )
        )
    left, middle, right, offset, position = spline[0]
    for node in range(6):
        shifted = float(node) - offset
        weight = jnp.where(
            shifted == 0.0,
            left,
            jnp.where(shifted == 1.0, middle, jnp.where(shifted == 2.0, right, 0.0)),
        )
        put(T_WX + node, weight)
        put(T_WXD + node, weight * (float(node) - position))
    for index in range(5):
        put(T_LY + index, spline[1][index])
        put(T_LZ + index, spline[2][index])

    lanes = lax.broadcasted_iota(jnp.int32, (8, 32), 1)
    channel = [(lanes >= 8 * index) & (lanes < 8 * index + 8) for index in range(4)]
    rest = jnp.zeros((8, LANES - 32), jnp.float32)
    blank = jnp.zeros((8, LANES), jnp.float32)

    def block_sums(block):
        def row(index):
            if index < T_SHARED:
                value = shared_ref[pl.ds(index * blocks + block, 1), :]
            else:
                value = table[pl.ds((index - T_SHARED) * blocks + block, 1), :]
            return jnp.broadcast_to(value, (8, LANES))

        wy, wyd = axis_weights(row, T_LY, T_MY, T_RY, T_OY, T_Y)
        wz, wzd = axis_weights(row, T_LZ, T_MZ, T_RZ, T_OZ, T_Z)
        wx = [row(T_WX + node) for node in range(6)]
        wxd = [row(T_WXD + node) for node in range(6)]
        left_side = jnp.concatenate(
            [
                jnp.concatenate([w * wy for w in wx], axis=0),
                jnp.concatenate([w * wy for w in wxd], axis=0),
                jnp.concatenate([w * wyd for w in wx], axis=0),
            ],
            axis=1,
        )
        value_rows = [
            wz * row(T_MV + dim) + wzd * row(T_A + 3 * dim + 2) for dim in range(3)
        ] + [wz * row(T_MASS)]
        x_rows = [wz * row(T_A + 3 * dim) for dim in range(3)] + [blank]
        y_rows = [wz * row(T_A + 3 * dim + 1) for dim in range(3)] + [blank]
        right_side = jnp.concatenate(
            [jnp.concatenate(r, axis=0) for r in (value_rows, x_rows, y_rows)], axis=1
        )
        left_high, left_low = split(left_side)
        right_high, right_low = split(right_side)

        def product(a, b):
            return lax.dot_general(
                a, b, (((1,), (1,)), ((), ())), preferred_element_type=jnp.float32
            )

        return (
            product(left_high, right_high)
            + product(left_high, right_low)
            + product(left_low, right_high)
        )

    starts = (0, PITCH - 8, 2 * PITCH - 16, LANES - 24)

    def group_place(step, sums):
        rows = pl.ds(pl.multiple_of(step * 8 * GROUP, 8 * GROUP), 8 * GROUP)
        heights = [4 * (tile_ref[step * GROUP + member] & 7) for member in range(GROUP)]
        for node in range(6):
            mom_rows, mass_rows = [], []
            for member in range(GROUP):
                part = sums[member][8 * node : 8 * node + 8]
                moved = [
                    pltpu.roll(
                        jnp.concatenate([jnp.where(channel[index], part, 0.0), rest], axis=1),
                        starts[index] + heights[member],
                        axis=1,
                    )
                    for index in range(4)
                ]
                mom_rows.append(moved[0] + moved[1] + moved[2])
                mass_rows.append(moved[3])
            for column, values in enumerate((mom_rows, mass_rows)):
                high, low = split(jnp.concatenate(values, axis=0))
                cols = slice(column * LANES, (column + 1) * LANES)
                placed_high[node, rows, cols] = high
                placed_low[node, rows, cols] = low

    def group_sums(step):
        return tuple(block_sums(step * GROUP + member) for member in range(GROUP))

    def group(step, sums):
        following = group_sums(step)
        group_place(step - 1, sums)
        return following

    steps = blocks // GROUP
    group_place(steps - 1, lax.fori_loop(1, steps, group, group_sums(0)))

    spots = 8 * blocks
    spot = lax.broadcasted_iota(jnp.int32, (8, spots), 1)
    owner = spot >> 3
    tiles = jnp.zeros((8, spots), jnp.int32)
    for block in range(blocks):
        tiles = jnp.where(owner == block, tile_ref[block], tiles)
    target = ((tiles >> 7) << 10) + (((tiles >> 3) & 15) << 2) + (spot & 7)
    y_row = lax.broadcasted_iota(jnp.int32, (8, spots), 0)
    chooser = jnp.concatenate(
        [
            jnp.where(target == y_row + (1024 * tile_x + start), 1.0, 0.0)
            for tile_x in range(CX // 4)
            for start in range(0, PY, 8)
        ],
        axis=0,
    ).astype(jnp.bfloat16)
    for node in range(6):
        layers = jnp.dot(
            chooser, placed_high[node], preferred_element_type=jnp.float32
        ) + jnp.dot(chooser, placed_low[node], preferred_element_type=jnp.float32)
        for tile_x in range(CX // 4):
            part = layers[tile_x * PY : (tile_x + 1) * PY]
            x = 4 * tile_x + node
            at = slice(x * PY, (x + 1) * PY)
            if node < 4 or x >= CX:
                mom[at, :] = part[:, :LANES]
                mass[at, :] = part[:, LANES:]
            else:
                mom[at, :] += part[:, :LANES]
                mass[at, :] += part[:, LANES:]

    def copy(src, dst, slot, target):
        return pltpu.make_async_remote_copy(
            src_ref=src,
            dst_ref=dst,
            send_sem=send_sem.at[slot],
            recv_sem=recv_sem.at[slot],
            device_id=target,
            device_id_type=MESH,
        )

    lane = lax.broadcasted_iota(jnp.int32, (PY, LANES), 1)
    in_mom = lane < 3 * PITCH
    in_pitch = lax.rem(lane, PITCH)
    third = PY // 3
    lane3 = lane[:third]

    def pack(step, carry):
        packed, packed_mass = list(carry[:2]), list(carry[2:])
        for member in range(3):
            x = 3 * step + member
            at = pl.ds(pl.multiple_of(x * PY, 8), PY)
            mine = (in_pitch >= 2 * x) & (in_pitch < 2 * x + 2) & in_mom
            for side, shift in enumerate((0, LANES - CZ)):
                packed[side] = jnp.where(
                    mine, pltpu.roll(mom[at, :], 2 * x + shift, axis=1), packed[side]
                )
                for part in range(3):
                    start = PITCH * part
                    rows = pl.ds(pl.multiple_of(x * PY + part * third, 8), third)
                    here = (lane3 >= start + 2 * x) & (lane3 < start + 2 * x + 2)
                    packed_mass[side] = jnp.where(
                        here,
                        pltpu.roll(mass[rows, :], start + 2 * x + shift, axis=1),
                        packed_mass[side],
                    )
        return tuple(packed + packed_mass)

    empty = jnp.zeros((PY, LANES), jnp.float32)
    packed = lax.fori_loop(0, PX // 3, pack, (empty, empty, empty[:third], empty[:third]))
    for side in range(2):
        z_send[side, :PY, :] = packed[side]
        z_send[side, PY:, :] = packed[2 + side]

    pl.semaphore_wait(barrier, 6)
    z_copies = [
        copy(z_send.at[side], z_recv.at[1 - side], side, z_sides[side]) for side in range(2)
    ]
    for c in z_copies:
        c.start()
    for c in z_copies:
        c.wait()

    low = (in_pitch < 2) & in_mom
    high = (in_pitch >= CZ) & (in_pitch < CZ + 2) & in_mom
    low3 = lane3 < 2
    high3 = (lane3 >= CZ) & (lane3 < CZ + 2)

    def unpack(step, carry):
        for member in range(3):
            x = 3 * step + member
            at = pl.ds(pl.multiple_of(x * PY, 8), PY)
            from_low = pltpu.roll(z_recv[0, :PY, :], LANES - 2 * x, axis=1)
            from_high = pltpu.roll(z_recv[1, :PY, :], LANES + CZ - 2 * x, axis=1)
            mom[at, :] += jnp.where(low, from_low, jnp.where(high, from_high, 0.0))
            for part in range(3):
                start = PITCH * part
                rows = pl.ds(pl.multiple_of(x * PY + part * third, 8), third)
                from_low = pltpu.roll(z_recv[0, PY:, :], 2 * LANES - start - 2 * x, axis=1)
                from_high = pltpu.roll(
                    z_recv[1, PY:, :], 2 * LANES + CZ - start - 2 * x, axis=1
                )
                mass[rows, :] += jnp.where(low3, from_low, jnp.where(high3, from_high, 0.0))
        return carry

    lax.fori_loop(0, PX // 3, unpack, 0)

    front = lane < 64
    firsts = (0, CX * PY)
    for side in range(2):
        first = firsts[side]
        x_send[side, : 2 * PY, :] = mom[first : first + 2 * PY, :]
        x_send[side, 2 * PY :, :] = mass[first : first + PY, :] + pltpu.roll(
            mass[first + PY : first + 2 * PY, :], 64, axis=1
        )
    x_copies = [
        copy(x_send.at[side], x_recv.at[1 - side], 2 + side, x_sides[side]) for side in range(2)
    ]
    for c in x_copies:
        c.start()
    for c in x_copies:
        c.wait()
    for side in range(2):
        first = firsts[side]
        mom[first : first + 2 * PY, :] += x_recv[side, : 2 * PY, :]
        got = x_recv[side, 2 * PY :, :]
        mass[first : first + PY, :] += jnp.where(front, got, 0.0)
        mass[first + PY : first + 2 * PY, :] += jnp.where(
            front, pltpu.roll(got, 64, axis=1), 0.0
        )

    y_firsts = (0, CY)
    for side in range(2):
        y0 = y_firsts[side]
        y_send[side, 0:PX, :] = mom[pl.ds(y0, PX, stride=PY), :]
        y_send[side, PX : 2 * PX, :] = mom[pl.ds(y0 + 1, PX, stride=PY), :]
        y_send[side, 2 * PX : 3 * PX, :] = mass[pl.ds(y0, PX, stride=PY), :] + pltpu.roll(
            mass[pl.ds(y0 + 1, PX, stride=PY), :], 64, axis=1
        )
        y_send[side, 3 * PX :, :] = jnp.zeros((2, LANES), jnp.float32)
    y_copies = [
        copy(y_send.at[side], y_recv.at[1 - side], 4 + side, y_sides[side]) for side in range(2)
    ]
    for c in y_copies:
        c.start()
    for c in y_copies:
        c.wait()
    for side in range(2):
        y0 = y_firsts[side]
        got = y_recv[side, 2 * PX : 3 * PX, :]
        at0 = pl.ds(y0, PX, stride=PY)
        at1 = pl.ds(y0 + 1, PX, stride=PY)
        mom[at0, :] = mom[at0, :] + y_recv[side, 0:PX, :]
        mom[at1, :] = mom[at1, :] + y_recv[side, PX : 2 * PX, :]
        mass[at0, :] = mass[at0, :] + jnp.where(front[:PX], got, 0.0)
        mass[at1, :] = mass[at1, :] + jnp.where(front[:PX], pltpu.roll(got, 64, axis=1), 0.0)


def collect_kernel(
    tile_hbm,
    mom_ref,
    mass_ref,
    shared_ref,
    stress_in,
    new_velocity_ref,
    new_affine_ref,
    new_stress_hbm,
    grid_velocity_hbm,
    tile_ref,
    new_stress_ref,
    grid_velocity_ref,
    velocity,
    partial,
    final,
    copy_sem,
):
    blocks = tile_hbm.shape[0]
    tile_copy = pltpu.make_async_copy(tile_hbm, tile_ref, copy_sem.at[0])
    tile_copy.start()
    for block in range(blocks):
        new_stress_ref[:, block * BLOCK : (block + 1) * BLOCK] = stress_in[
            pl.ds(block, 6, stride=blocks), :
        ]
    stress_copy = pltpu.make_async_copy(new_stress_ref, new_stress_hbm, copy_sem.at[1])
    stress_copy.start()
    width_x = lax.axis_size("gx") * CX
    height_y = lax.axis_size("gy") * CY
    depth_z = lax.axis_size("gz") * CZ
    lane = lax.broadcasted_iota(jnp.int32, (PY, LANES), 1)
    row_index = lax.broadcasted_iota(jnp.int32, (PY, LANES), 0)
    first_z = lax.axis_index("gz") * CZ
    first_y = lax.axis_index("gy") * CY
    first_x = lax.axis_index("gx") * CX
    z_index = lax.rem(lane - 2 * PITCH - 1 + first_z + depth_z, depth_z)
    y_index = lax.rem(row_index - 1 + first_y + height_y, height_y)
    is_y = (lane >= PITCH) & (lane < 2 * PITCH)
    is_z = (lane >= 2 * PITCH) & (lane < 3 * PITCH)
    z_floor = is_z & (z_index < 2)
    z_top = is_z & (z_index >= depth_z - 2)
    y_floor = is_y & (y_index < 2)
    fall = jnp.where(is_y, time_step * gravity, 0.0)

    def layer(x):
        at = pl.ds(pl.multiple_of(x * PY, 8), PY)
        x_index = lax.rem(first_x + x - 1 + width_x, width_x)
        outlet = (x_index >= width_x // 4) & (x_index < width_x - width_x // 4)
        inverse = 1.0 / (mass_ref[at, :] + mass_floor)
        inverse = jnp.where(
            lane < PITCH,
            inverse,
            jnp.where(
                is_y, pltpu.roll(inverse, PITCH, axis=1), pltpu.roll(inverse, 2 * PITCH, axis=1)
            ),
        )
        values = mom_ref[at, :] * inverse - fall
        lifted = jnp.maximum(values, 0.0)
        values = jnp.where(
            z_floor | (y_floor & jnp.logical_not(outlet)), lifted, values
        )
        values = jnp.where(z_top, jnp.minimum(values, 0.0), values)
        velocity[at, :] = values

    def layers(step, carry):
        for member in range(3):
            layer(3 * step + member)
        return carry

    lax.fori_loop(0, PX // 3, layers, 0)

    def output(step, carry):
        for member in range(4):
            x = 4 * step + member
            turned = jnp.transpose(velocity[pl.ds((x + 1) * PY + 1, CY), :])
            for dim in range(3):
                grid_velocity_ref[dim, x] = turned[PITCH * dim + 1 : PITCH * dim + 1 + CZ]
        return carry

    lax.fori_loop(0, CX // 4, output, 0)
    grid_copy = pltpu.make_async_copy(grid_velocity_ref, grid_velocity_hbm, copy_sem.at[2])
    grid_copy.start()
    tile_copy.wait()

    lanes = lax.broadcasted_iota(jnp.int32, (8, LANES), 1)

    def row_of(block):
        def row(index):
            return jnp.broadcast_to(shared_ref[pl.ds(index * blocks + block, 1), :], (8, LANES))

        return row

    def gather(block):
        tile_x, tile_y, tile_z = tile_coords(tile_ref, block)
        planes = []
        for node in range(6):
            at = pl.ds(pl.multiple_of((4 * tile_x + node) * PY + 4 * tile_y, 4), 8)
            planes.append(velocity[at, :])
        rows = []
        for dim in range(3):
            merged = None
            for node in range(6):
                moved = pltpu.roll(
                    planes[node],
                    LANES + 8 * node - PITCH * dim - 4 * tile_z,
                    axis=1,
                )
                merged = moved if merged is None else jnp.where(lanes < 8 * node, merged, moved)
            rows.append(merged)
        return jnp.concatenate(rows, axis=0)

    def contract(block, left_side):
        row = row_of(block)
        wz, wzd = axis_weights(row, T_LZ, T_MZ, T_RZ, T_OZ, T_Z)
        wx = [row(T_WX + node) for node in range(6)]
        wxd = [row(T_WXD + node) for node in range(6)]
        right_side = jnp.concatenate(
            [
                jnp.concatenate([w * wz for w in wx], axis=0),
                jnp.concatenate([w * wz for w in wxd], axis=0),
                jnp.concatenate([w * wzd for w in wx], axis=0),
            ],
            axis=1,
        )
        left_high, left_low = split(left_side[:, :48])
        right_high, right_low = split(right_side)
        both = jnp.dot(
            jnp.concatenate([left_high, left_low], axis=0),
            right_high,
            preferred_element_type=jnp.float32,
        )
        return (
            both[:24]
            + both[24:]
            + jnp.dot(left_high, right_low, preferred_element_type=jnp.float32)
        )

    def weigh(block, sums):
        wy, wyd = axis_weights(row_of(block), T_LY, T_MY, T_RY, T_OY, T_Y)
        for dim in range(3):
            part = sums[8 * dim : 8 * dim + 8]
            terms = (
                (dim, wy * part[:, :128]),
                (3 + 3 * dim, wy * part[:, 128:256]),
                (4 + 3 * dim, wyd * part[:, :128]),
                (5 + 3 * dim, wy * part[:, 256:]),
            )
            for component, value in terms:
                at = pl.ds(pl.multiple_of(component * 8 * blocks + 8 * block, 8), 8)
                partial[at, :] = value

    def of_group(function, step, *values):
        return tuple(
            function(step * GROUP + member, *(value[member] for value in values))
            for member in range(GROUP)
        )

    def group(step, carry):
        left_sides, sums = carry
        following = of_group(gather, step + 2)
        products = of_group(contract, step + 1, left_sides)
        of_group(weigh, step, sums)
        return following, products

    steps = blocks // GROUP
    carry = of_group(gather, 1), of_group(contract, 0, of_group(gather, 0))
    left_sides, sums = lax.fori_loop(0, steps - 2, group, carry)
    of_group(weigh, steps - 2, sums)
    of_group(weigh, steps - 1, of_group(contract, steps - 1, left_sides))
    for component in range(12):
        total = partial[pl.ds(component * 8 * blocks, blocks, stride=8), :]
        for node in range(1, 6):
            total = total + partial[pl.ds(component * 8 * blocks + node, blocks, stride=8), :]
        if component >= 3:
            total = 4.0 * total
        final[component * blocks : (component + 1) * blocks, :] = total
    for block in range(blocks):
        cols = slice(block * BLOCK, (block + 1) * BLOCK)
        new_velocity_ref[:, cols] = final[pl.ds(block, 3, stride=blocks), :]
        new_affine_ref[:, cols] = final[pl.ds(3 * blocks + block, 9, stride=blocks), :]
    stress_copy.wait()
    grid_copy.wait()


def shards(
    point_frac,
    cell_offset,
    point_velocity,
    point_affine,
    point_stress,
    point_mass,
    block_tile,
    block_count,
):
    blocks = block_tile.shape[0]
    points = blocks * BLOCK
    vmem = pl.BlockSpec(memory_space=pltpu.VMEM)
    hbm = pl.BlockSpec(memory_space=pltpu.HBM)
    f32 = jnp.float32
    grid_shape = jax.ShapeDtypeStruct((ROWS, LANES), f32)
    face = PY + PY // 3
    arguments = [
        pltpu.with_memory_space_constraint(value, pltpu.HBM)
        for value in (
            block_tile,
            block_count,
            point_frac,
            cell_offset,
            point_velocity,
            point_affine,
            point_stress,
            point_mass.reshape(blocks, BLOCK),
        )
    ]
    mom, mass, shared, stress = pl.pallas_call(
        deposit_kernel,
        name="deposit",
        out_shape=(
            grid_shape,
            grid_shape,
            jax.ShapeDtypeStruct((T_SHARED * blocks, LANES), f32),
            jax.ShapeDtypeStruct((6 * blocks, LANES), f32),
        ),
        in_specs=[hbm] * 8,
        out_specs=(vmem,) * 4,
        scratch_shapes=[
            pltpu.SMEM((blocks,), jnp.int32),
            pltpu.SMEM((blocks,), jnp.int32),
            pltpu.VMEM((3, points), f32),
            pltpu.VMEM((3, points), jnp.int32),
            pltpu.VMEM((3, points), f32),
            pltpu.VMEM((9, points), f32),
            pltpu.VMEM((6, points), f32),
            pltpu.VMEM((blocks, BLOCK), f32),
            pltpu.VMEM((48 * blocks, LANES), f32),
            pltpu.VMEM(((T_ALL - T_SHARED) * blocks, LANES), f32),
            pltpu.VMEM((6, 8 * blocks, 2 * LANES), jnp.bfloat16),
            pltpu.VMEM((6, 8 * blocks, 2 * LANES), jnp.bfloat16),
            pltpu.VMEM((2, face, LANES), f32),
            pltpu.VMEM((2, face, LANES), f32),
            pltpu.VMEM((2, 3 * PY, LANES), f32),
            pltpu.VMEM((2, 3 * PY, LANES), f32),
            pltpu.VMEM((2, 3 * PX + 2, LANES), f32),
            pltpu.VMEM((2, 3 * PX + 2, LANES), f32),
            pltpu.SemaphoreType.DMA((8,)),
            pltpu.SemaphoreType.DMA((6,)),
            pltpu.SemaphoreType.DMA((6,)),
        ],
        compiler_params=pltpu.CompilerParams(
            collective_id=0, has_side_effects=True, vmem_limit_bytes=VMEM_LIMIT
        ),
    )(*arguments)
    new_velocity, new_affine, new_stress, grid_velocity = pl.pallas_call(
        collect_kernel,
        name="collect",
        out_shape=(
            jax.ShapeDtypeStruct((3, points), f32),
            jax.ShapeDtypeStruct((9, points), f32),
            jax.ShapeDtypeStruct((6, points), f32),
            jax.ShapeDtypeStruct((3, CX, CZ, CY), f32),
        ),
        in_specs=[hbm] + [vmem] * 4,
        out_specs=(vmem, vmem, hbm, hbm),
        scratch_shapes=[
            pltpu.SMEM((blocks,), jnp.int32),
            pltpu.VMEM((6, points), f32),
            pltpu.VMEM((3, CX, CZ, CY), f32),
            pltpu.VMEM((ROWS, LANES), f32),
            pltpu.VMEM((12 * 8 * blocks, LANES), f32),
            pltpu.VMEM((12 * blocks, LANES), f32),
            pltpu.SemaphoreType.DMA((3,)),
        ],
        compiler_params=pltpu.CompilerParams(vmem_limit_bytes=VMEM_LIMIT),
    )(arguments[0], mom, mass, shared, stress)
    return (new_velocity, new_affine, new_stress, jnp.swapaxes(grid_velocity, 2, 3))


def solution(mesh):
    points = P(None, ("gx", "gy", "gz"))
    flat = P(("gx", "gy", "gz"))
    return jax.shard_map(
        shards,
        mesh=mesh,
        in_specs=(points,) * 5 + (flat,) * 3,
        out_specs=(points, points, points, P(None, "gx", "gy", "gz")),
        check_vma=False,
    )
```

```python
import jax
import jax.numpy as jnp
from jax import lax
from jax.experimental import pallas as pl
from jax.experimental.pallas import tpu as pltpu
from jax.sharding import PartitionSpec as P

CX = 16
CY = 64
CZ = 32
BLOCK = 128

time_step = 0.1
gravity = 1.0
shear_modulus = 2.0
bulk_modulus = 4.0
friction_static = 0.38
friction_limit = 0.64
inertial_ref = 0.28
grain_size = 0.5
grain_density = 1.0
pressure_floor = 0.5
shear_floor = 0.5
mass_floor = 0.05
stress_scale = 0.4
pair_index = ((0, 5, 4), (5, 1, 3), (4, 3, 2))
component_pairs = ((0, 0), (1, 1), (2, 2), (1, 2), (0, 2), (0, 1))

PX = CX + 2
PY = 72
PITCH = 40
LANES = 128
ROWS = PX * PY
GROUP = 4
UNROLL = 6
VMEM_LIMIT = 16 * 1024 * 1024
MESH = pl.DeviceIdType.MESH

T_WX, T_WXD = 0, 6
T_LY, T_MY, T_RY, T_OY, T_Y = 12, 13, 14, 15, 16
T_LZ, T_MZ, T_RZ, T_OZ, T_Z = 17, 18, 19, 20, 21
T_SHARED = 22
T_MASS, T_MV, T_A = 22, 23, 26
T_ALL = 35


def stress_update(stress, affine):
    strain_rate = [
        [
            0.5 * (affine[3 * row_dim + col_dim] + affine[3 * col_dim + row_dim])
            for col_dim in range(3)
        ]
        for row_dim in range(3)
    ]
    volume_rate = strain_rate[0][0] + strain_rate[1][1] + strain_rate[2][2]
    deviator = [
        [
            strain_rate[row_dim][col_dim] - (volume_rate / 3.0 if row_dim == col_dim else 0.0)
            for col_dim in range(3)
        ]
        for row_dim in range(3)
    ]
    trial_stress = []
    for component in range(6):
        row_dim, col_dim = component_pairs[component]
        value = stress[component] + time_step * 2.0 * shear_modulus * deviator[row_dim][col_dim]
        if component < 3:
            value = value + time_step * bulk_modulus * volume_rate
        trial_stress.append(value)
    pressure = -(trial_stress[0] + trial_stress[1] + trial_stress[2]) / 3.0
    shear_part = [trial_stress[component] + pressure for component in range(3)] + trial_stress[3:]
    shear_stress = jnp.sqrt(
        0.5 * (shear_part[0] ** 2 + shear_part[1] ** 2 + shear_part[2] ** 2)
        + shear_part[3] ** 2
        + shear_part[4] ** 2
        + shear_part[5] ** 2
    )
    shear_rate = jnp.sqrt(
        2.0
        * (
            deviator[0][0] ** 2
            + deviator[1][1] ** 2
            + deviator[2][2] ** 2
            + 2.0 * (deviator[1][2] ** 2 + deviator[0][2] ** 2 + deviator[0][1] ** 2)
        )
    )
    inertial = (
        shear_rate * grain_size / jnp.sqrt(jnp.maximum(pressure, pressure_floor) / grain_density)
    )
    friction = friction_static + (friction_limit - friction_static) * inertial / (
        inertial_ref + inertial
    )
    support = jnp.maximum(pressure, 0.0)
    factor = jnp.minimum(1.0, friction * support / jnp.maximum(shear_stress, shear_floor))
    return [shear_part[component] * factor - support for component in range(3)] + [
        shear_part[component] * factor for component in range(3, 6)
    ]


def split(values):
    high = values.astype(jnp.bfloat16)
    low = (values - high.astype(jnp.float32)).astype(jnp.bfloat16)
    return high, low


def tile_coords(tile_ref, block):
    tile = tile_ref[block]
    return tile >> 7, (tile >> 3) & 15, tile & 7


def axis_weights(row, left, middle, right, offset, position):
    index = lax.broadcasted_iota(jnp.int32, (8, LANES), 0).astype(jnp.float32)
    shifted = index - row(offset)
    weight = jnp.where(
        shifted == 0.0,
        row(left),
        jnp.where(shifted == 1.0, row(middle), jnp.where(shifted == 2.0, row(right), 0.0)),
    )
    return weight, weight * (index - row(position))


def deposit_kernel(
    tile_hbm,
    count_hbm,
    frac_hbm,
    offset_hbm,
    velocity_hbm,
    affine_hbm,
    stress_hbm,
    mass_hbm,
    mom,
    mass,
    shared_ref,
    stress_out,
    tile_ref,
    count_ref,
    frac_ref,
    offset_ref,
    velocity_ref,
    affine_ref,
    stress_ref,
    mass_ref,
    gathered,
    table,
    placed_high,
    placed_low,
    z_send,
    z_recv,
    x_send,
    x_recv,
    xz_send,
    xz_recv,
    y_send,
    y_recv,
    load_sem,
    send_sem,
    recv_sem,
):
    axes = ("gx", "gy", "gz")

    def device(dx, dy, dz):
        place = []
        for axis, step in zip(axes, (dx, dy, dz)):
            size = lax.axis_size(axis)
            moved = lax.axis_index(axis)
            if step:
                moved = moved + step
                moved = jnp.where(moved < 0, size - 1, jnp.where(moved >= size, 0, moved))
            place.append(moved)
        return tuple(place)

    z_sides = [device(0, 0, -1), device(0, 0, 1)]
    x_sides = [device(-1, 0, 0), device(1, 0, 0)]
    y_sides = [device(0, -1, 0), device(0, 1, 0)]
    xz_sides = [device(dx, 0, dz) for dx in (-1, 1) for dz in (-1, 1)]
    barrier = pltpu.get_barrier_semaphore()
    for target in x_sides + z_sides + xz_sides + y_sides:
        pl.semaphore_signal(barrier, inc=1, device_id=target, device_id_type=MESH)
    loads = [
        pltpu.make_async_copy(source, target, load_sem.at[index])
        for index, (source, target) in enumerate(
            (
                (frac_hbm, frac_ref),
                (offset_hbm, offset_ref),
                (velocity_hbm, velocity_ref),
                (affine_hbm, affine_ref),
                (stress_hbm, stress_ref),
                (mass_hbm, mass_ref),
                (count_hbm, count_ref),
                (tile_hbm, tile_ref),
            )
        )
    ]
    for load in loads:
        load.start()

    blocks = mass_ref.shape[0]
    lane_row = lax.broadcasted_iota(jnp.int32, (1, LANES), 1)
    stride = 48
    for load in loads:
        load.wait()
    for block in range(blocks):
        cols = slice(block * BLOCK, (block + 1) * BLOCK)
        at = block * stride
        gathered[at : at + 3, :] = frac_ref[:, cols]
        gathered[at + 8 : at + 11, :] = offset_ref[:, cols].astype(jnp.float32)
        gathered[at + 16 : at + 19, :] = velocity_ref[:, cols]
        gathered[at + 24 : at + 33, :] = affine_ref[:, cols]
        gathered[at + 40 : at + 46, :] = stress_ref[:, cols]
        row = (T_MASS - T_SHARED) * blocks + block
        table[row : row + 1, :] = jnp.where(
            lane_row < count_ref[block], mass_ref[block : block + 1, :], 0.0
        )

    def dense(component):
        return gathered[pl.ds(component, blocks, stride=stride), :]

    def put(index, value):
        if index < T_SHARED:
            shared_ref[index * blocks : (index + 1) * blocks, :] = value
        else:
            start = (index - T_SHARED) * blocks
            table[start : start + blocks, :] = value

    affine = [dense(24 + component) for component in range(9)]
    stress = stress_update([dense(40 + component) for component in range(6)], affine)
    for component in range(6):
        stress_out[component * blocks : (component + 1) * blocks, :] = stress[component]
    live_mass = table[(T_MASS - T_SHARED) * blocks : (T_MASS - T_SHARED + 1) * blocks, :]
    for row_dim in range(3):
        put(T_MV + row_dim, live_mass * dense(16 + row_dim))
        for col_dim in range(3):
            put(
                T_A + 3 * row_dim + col_dim,
                live_mass
                * (
                    affine[3 * row_dim + col_dim]
                    - stress_scale * stress[pair_index[row_dim][col_dim]]
                ),
            )
    spline = []
    for dim in range(3):
        fraction = dense(dim)
        spline.append(
            (
                0.5 * (1.5 - fraction) ** 2,
                0.75 - (fraction - 1.0) ** 2,
                0.5 * (fraction - 0.5) ** 2,
                dense(8 + dim),
                dense(8 + dim) + fraction,
            )
        )
    left, middle, right, offset, position = spline[0]
    for node in range(6):
        shifted = float(node) - offset
        weight = jnp.where(
            shifted == 0.0,
            left,
            jnp.where(shifted == 1.0, middle, jnp.where(shifted == 2.0, right, 0.0)),
        )
        put(T_WX + node, weight)
        put(T_WXD + node, weight * (float(node) - position))
    for index in range(5):
        put(T_LY + index, spline[1][index])
        put(T_LZ + index, spline[2][index])

    lanes = lax.broadcasted_iota(jnp.int32, (8, 32), 1)
    channel = [(lanes >= 8 * index) & (lanes < 8 * index + 8) for index in range(4)]
    rest = jnp.zeros((8, LANES - 32), jnp.float32)
    blank = jnp.zeros((8, LANES), jnp.float32)

    def block_sums(block):
        def row(index):
            if index < T_SHARED:
                value = shared_ref[pl.ds(index * blocks + block, 1), :]
            else:
                value = table[pl.ds((index - T_SHARED) * blocks + block, 1), :]
            return jnp.broadcast_to(value, (8, LANES))

        wy, wyd = axis_weights(row, T_LY, T_MY, T_RY, T_OY, T_Y)
        wz, wzd = axis_weights(row, T_LZ, T_MZ, T_RZ, T_OZ, T_Z)
        wx = [row(T_WX + node) for node in range(6)]
        wxd = [row(T_WXD + node) for node in range(6)]
        left_side = jnp.concatenate(
            [
                jnp.concatenate([w * wy for w in wx], axis=0),
                jnp.concatenate([w * wy for w in wxd], axis=0),
                jnp.concatenate([w * wyd for w in wx], axis=0),
            ],
            axis=1,
        )
        value_rows = [
            wz * row(T_MV + dim) + wzd * row(T_A + 3 * dim + 2) for dim in range(3)
        ] + [wz * row(T_MASS)]
        x_rows = [wz * row(T_A + 3 * dim) for dim in range(3)] + [blank]
        y_rows = [wz * row(T_A + 3 * dim + 1) for dim in range(3)] + [blank]
        right_side = jnp.concatenate(
            [jnp.concatenate(r, axis=0) for r in (value_rows, x_rows, y_rows)], axis=1
        )
        left_high, left_low = split(left_side)
        right_high, right_low = split(right_side)

        def product(a, b):
            return lax.dot_general(
                a, b, (((1,), (1,)), ((), ())), preferred_element_type=jnp.float32
            )

        return (
            product(left_high, right_high)
            + product(left_high, right_low)
            + product(left_low, right_high)
        )

    starts = (0, PITCH - 8, 2 * PITCH - 16, LANES - 24)

    def group_place(step, sums):
        rows = pl.ds(pl.multiple_of(step * 8 * GROUP, 8 * GROUP), 8 * GROUP)
        heights = [4 * (tile_ref[step * GROUP + member] & 7) for member in range(GROUP)]
        for node in range(6):
            mom_rows, mass_rows = [], []
            for member in range(GROUP):
                part = sums[member][8 * node : 8 * node + 8]
                moved = [
                    pltpu.roll(
                        jnp.concatenate([jnp.where(channel[index], part, 0.0), rest], axis=1),
                        starts[index] + heights[member],
                        axis=1,
                    )
                    for index in range(4)
                ]
                mom_rows.append(moved[0] + moved[1] + moved[2])
                mass_rows.append(moved[3])
            for column, values in enumerate((mom_rows, mass_rows)):
                high, low = split(jnp.concatenate(values, axis=0))
                cols = slice(column * LANES, (column + 1) * LANES)
                placed_high[node, rows, cols] = high
                placed_low[node, rows, cols] = low

    def group_sums(step):
        return tuple(block_sums(step * GROUP + member) for member in range(GROUP))

    def group(step, sums):
        following = group_sums(step)
        group_place(step - 1, sums)
        return following

    steps = blocks // GROUP
    group_place(steps - 1, lax.fori_loop(1, steps, group, group_sums(0)))

    spots = 8 * blocks
    spot = lax.broadcasted_iota(jnp.int32, (8, spots), 1)
    owner = spot >> 3
    tiles = jnp.zeros((8, spots), jnp.int32)
    for block in range(blocks):
        tiles = jnp.where(owner == block, tile_ref[block], tiles)
    target = ((tiles >> 7) << 10) + (((tiles >> 3) & 15) << 2) + (spot & 7)
    y_row = lax.broadcasted_iota(jnp.int32, (8, spots), 0)
    chooser = jnp.concatenate(
        [
            jnp.where(target == y_row + (1024 * tile_x + start), 1.0, 0.0)
            for tile_x in range(CX // 4)
            for start in range(0, PY, 8)
        ],
        axis=0,
    ).astype(jnp.bfloat16)
    for node in range(6):
        layers = jnp.dot(
            chooser, placed_high[node], preferred_element_type=jnp.float32
        ) + jnp.dot(chooser, placed_low[node], preferred_element_type=jnp.float32)
        for tile_x in range(CX // 4):
            part = layers[tile_x * PY : (tile_x + 1) * PY]
            x = 4 * tile_x + node
            at = slice(x * PY, (x + 1) * PY)
            if node < 4 or x >= CX:
                mom[at, :] = part[:, :LANES]
                mass[at, :] = part[:, LANES:]
            else:
                mom[at, :] += part[:, :LANES]
                mass[at, :] += part[:, LANES:]

    def copy(src, dst, slot, target):
        return pltpu.make_async_remote_copy(
            src_ref=src,
            dst_ref=dst,
            send_sem=send_sem.at[slot],
            recv_sem=recv_sem.at[slot],
            device_id=target,
            device_id_type=MESH,
        )

    lane = lax.broadcasted_iota(jnp.int32, (PY, LANES), 1)
    in_mom = lane < 3 * PITCH
    in_pitch = lax.rem(lane, PITCH)
    third = PY // 3
    lane3 = lane[:third]
    pl.semaphore_wait(barrier, 10)

    firsts = (0, CX * PY)
    for side in range(2):
        first = firsts[side]
        x_send[side, : 2 * PY, :] = mom[first : first + 2 * PY, :]
        for layer in range(2):
            start = first + layer * PY
            at = 2 * PY + layer * third
            x_send[side, at : at + third, :] = (
                mass[start : start + third, :]
                + pltpu.roll(mass[start + third : start + 2 * third, :], PITCH, axis=1)
                + pltpu.roll(mass[start + 2 * third : start + 3 * third, :], 2 * PITCH, axis=1)
            )
    x_copies = [
        copy(x_send.at[side], x_recv.at[1 - side], 2 + side, x_sides[side]) for side in range(2)
    ]
    for c in x_copies:
        c.start()

    def pack(step, carry):
        packed, packed_mass = list(carry[:2]), list(carry[2:])
        for member in range(UNROLL):
            x = UNROLL * step + member
            at = pl.ds(pl.multiple_of(x * PY, 8), PY)
            mine = (in_pitch >= 2 * x) & (in_pitch < 2 * x + 2) & in_mom
            for side, shift in enumerate((0, LANES - CZ)):
                packed[side] = jnp.where(
                    mine, pltpu.roll(mom[at, :], 2 * x + shift, axis=1), packed[side]
                )
                for part in range(3):
                    start = PITCH * part
                    rows = pl.ds(pl.multiple_of(x * PY + part * third, 8), third)
                    here = (lane3 >= start + 2 * x) & (lane3 < start + 2 * x + 2)
                    packed_mass[side] = jnp.where(
                        here,
                        pltpu.roll(mass[rows, :], start + 2 * x + shift, axis=1),
                        packed_mass[side],
                    )
        return tuple(packed + packed_mass)

    empty = jnp.zeros((PY, LANES), jnp.float32)
    packed = lax.fori_loop(0, PX // UNROLL, pack, (empty, empty, empty[:third], empty[:third]))
    for side in range(2):
        z_send[side, :PY, :] = packed[side]
        z_send[side, PY:, :] = packed[2 + side]
    z_copies = [
        copy(z_send.at[side], z_recv.at[1 - side], side, z_sides[side]) for side in range(2)
    ]
    for c in z_copies:
        c.start()

    quad = lax.broadcasted_iota(jnp.int32, (8, LANES), 1) >> 2
    for edge in range(4):
        x0, z_side = CX * (edge // 2), edge % 2
        result = [None, None]
        for tile in range(PY // 8):
            half, start = tile // 8, 16 * (tile % 8)
            rows = z_send[z_side, 8 * tile : 8 * tile + 8, :]
            mass_at = PY + 8 * (tile % 3)
            mass_rows = z_send[z_side, mass_at : mass_at + 8, :]
            for index in range(4):
                if index < 3:
                    source, at = rows, PITCH * index + 2 * x0
                else:
                    source, at = mass_rows, PITCH * (tile // 3) + 2 * x0
                to = start + 4 * index
                moved = pltpu.roll(source, (LANES + to - at) % LANES, axis=1)
                if result[half] is None:
                    result[half] = moved
                else:
                    result[half] = jnp.where(quad == to // 4, moved, result[half])
        xz_send[edge, :8, :] = result[0]
        xz_send[edge, 8:, :] = result[1]
    xz_copies = [
        copy(xz_send.at[edge], xz_recv.at[3 - edge], 6 + edge, xz_sides[edge])
        for edge in range(4)
    ]
    for c in xz_copies:
        c.start()

    for c in z_copies:
        c.wait()
    low = (in_pitch < 2) & in_mom
    high = (in_pitch >= CZ) & (in_pitch < CZ + 2) & in_mom
    low3 = lane3 < 2
    high3 = (lane3 >= CZ) & (lane3 < CZ + 2)

    def unpack(step, carry):
        for member in range(UNROLL):
            x = UNROLL * step + member
            at = pl.ds(pl.multiple_of(x * PY, 8), PY)
            from_low = pltpu.roll(z_recv[0, :PY, :], LANES - 2 * x, axis=1)
            from_high = pltpu.roll(z_recv[1, :PY, :], LANES + CZ - 2 * x, axis=1)
            mom[at, :] += jnp.where(low, from_low, jnp.where(high, from_high, 0.0))
            for part in range(3):
                start = PITCH * part
                rows = pl.ds(pl.multiple_of(x * PY + part * third, 8), third)
                from_low = pltpu.roll(z_recv[0, PY:, :], 2 * LANES - start - 2 * x, axis=1)
                from_high = pltpu.roll(
                    z_recv[1, PY:, :], 2 * LANES + CZ - start - 2 * x, axis=1
                )
                mass[rows, :] += jnp.where(low3, from_low, jnp.where(high3, from_high, 0.0))
        return carry

    lax.fori_loop(0, PX // UNROLL, unpack, 0)

    for c in xz_copies:
        c.wait()
    lane8 = lane[:8]
    for side in range(2):
        for layer in range(2):
            for tile in range(PY // 8):
                half, start = tile // 8, 16 * (tile % 8)
                mom_value, mass_value = 0.0, 0.0
                for z_side in range(2):
                    source = xz_recv[2 * side + z_side, 8 * half : 8 * half + 8, :]
                    for index in range(4):
                        to = (PITCH * index if index < 3 else 0) + CZ * z_side
                        at = start + 4 * index + 2 * layer
                        moved = pltpu.roll(source, (LANES + to - at) % LANES, axis=1)
                        here = (lane8 >= to) & (lane8 < to + 2)
                        if index < 3:
                            mom_value = jnp.where(here, moved, mom_value)
                        else:
                            mass_value = jnp.where(here, moved, mass_value)
                at = firsts[side] + layer * PY + 8 * tile
                mom[at : at + 8, :] += mom_value
                mass[at : at + 8, :] += mass_value

    for c in x_copies:
        c.wait()
    near3 = lane3 < PITCH
    for side in range(2):
        first = firsts[side]
        mom[first : first + 2 * PY, :] += x_recv[side, : 2 * PY, :]
        for layer in range(2):
            at = 2 * PY + layer * third
            got = x_recv[side, at : at + third, :]
            for part in range(3):
                start = first + layer * PY + part * third
                moved = pltpu.roll(got, (LANES - PITCH * part) % LANES, axis=1)
                mass[start : start + third, :] += jnp.where(near3, moved, 0.0)
    front = lane < 64

    y_firsts = (0, CY)
    for side in range(2):
        y0 = y_firsts[side]
        y_send[side, 0:PX, :] = mom[pl.ds(y0, PX, stride=PY), :]
        y_send[side, PX : 2 * PX, :] = mom[pl.ds(y0 + 1, PX, stride=PY), :]
        y_send[side, 2 * PX : 3 * PX, :] = mass[pl.ds(y0, PX, stride=PY), :] + pltpu.roll(
            mass[pl.ds(y0 + 1, PX, stride=PY), :], 64, axis=1
        )
        y_send[side, 3 * PX :, :] = jnp.zeros((2, LANES), jnp.float32)
    y_copies = [
        copy(y_send.at[side], y_recv.at[1 - side], 4 + side, y_sides[side]) for side in range(2)
    ]
    for c in y_copies:
        c.start()
    for c in y_copies:
        c.wait()
    for side in range(2):
        y0 = y_firsts[side]
        got = y_recv[side, 2 * PX : 3 * PX, :]
        at0 = pl.ds(y0, PX, stride=PY)
        at1 = pl.ds(y0 + 1, PX, stride=PY)
        mom[at0, :] = mom[at0, :] + y_recv[side, 0:PX, :]
        mom[at1, :] = mom[at1, :] + y_recv[side, PX : 2 * PX, :]
        mass[at0, :] = mass[at0, :] + jnp.where(front[:PX], got, 0.0)
        mass[at1, :] = mass[at1, :] + jnp.where(front[:PX], pltpu.roll(got, 64, axis=1), 0.0)


def collect_kernel(
    tile_hbm,
    mom_ref,
    mass_ref,
    shared_ref,
    stress_in,
    new_velocity_ref,
    new_affine_ref,
    new_stress_hbm,
    grid_velocity_hbm,
    tile_ref,
    new_stress_ref,
    grid_velocity_ref,
    velocity,
    partial,
    final,
    copy_sem,
):
    blocks = tile_hbm.shape[0]
    tile_copy = pltpu.make_async_copy(tile_hbm, tile_ref, copy_sem.at[0])
    tile_copy.start()
    for block in range(blocks):
        new_stress_ref[:, block * BLOCK : (block + 1) * BLOCK] = stress_in[
            pl.ds(block, 6, stride=blocks), :
        ]
    stress_copy = pltpu.make_async_copy(new_stress_ref, new_stress_hbm, copy_sem.at[1])
    stress_copy.start()
    width_x = lax.axis_size("gx") * CX
    height_y = lax.axis_size("gy") * CY
    depth_z = lax.axis_size("gz") * CZ
    lane = lax.broadcasted_iota(jnp.int32, (PY, LANES), 1)
    row_index = lax.broadcasted_iota(jnp.int32, (PY, LANES), 0)
    first_z = lax.axis_index("gz") * CZ
    first_y = lax.axis_index("gy") * CY
    first_x = lax.axis_index("gx") * CX
    z_index = lax.rem(lane - 2 * PITCH - 1 + first_z + depth_z, depth_z)
    y_index = lax.rem(row_index - 1 + first_y + height_y, height_y)
    is_y = (lane >= PITCH) & (lane < 2 * PITCH)
    is_z = (lane >= 2 * PITCH) & (lane < 3 * PITCH)
    z_floor = is_z & (z_index < 2)
    z_top = is_z & (z_index >= depth_z - 2)
    y_floor = is_y & (y_index < 2)
    fall = jnp.where(is_y, time_step * gravity, 0.0)

    def layer(x):
        at = pl.ds(pl.multiple_of(x * PY, 8), PY)
        x_index = lax.rem(first_x + x - 1 + width_x, width_x)
        outlet = (x_index >= width_x // 4) & (x_index < width_x - width_x // 4)
        inverse = 1.0 / (mass_ref[at, :] + mass_floor)
        inverse = jnp.where(
            lane < PITCH,
            inverse,
            jnp.where(
                is_y, pltpu.roll(inverse, PITCH, axis=1), pltpu.roll(inverse, 2 * PITCH, axis=1)
            ),
        )
        values = mom_ref[at, :] * inverse - fall
        lifted = jnp.maximum(values, 0.0)
        values = jnp.where(
            z_floor | (y_floor & jnp.logical_not(outlet)), lifted, values
        )
        values = jnp.where(z_top, jnp.minimum(values, 0.0), values)
        velocity[at, :] = values

    def layers(step, carry):
        for member in range(3):
            layer(3 * step + member)
        return carry

    lax.fori_loop(0, PX // 3, layers, 0)

    def output(step, carry):
        for member in range(4):
            x = 4 * step + member
            turned = jnp.transpose(velocity[pl.ds((x + 1) * PY + 1, CY), :])
            for dim in range(3):
                grid_velocity_ref[dim, x] = turned[PITCH * dim + 1 : PITCH * dim + 1 + CZ]
        return carry

    lax.fori_loop(0, CX // 4, output, 0)
    grid_copy = pltpu.make_async_copy(grid_velocity_ref, grid_velocity_hbm, copy_sem.at[2])
    grid_copy.start()
    tile_copy.wait()

    lanes = lax.broadcasted_iota(jnp.int32, (8, LANES), 1)

    def row_of(block):
        def row(index):
            return jnp.broadcast_to(shared_ref[pl.ds(index * blocks + block, 1), :], (8, LANES))

        return row

    def gather(block):
        tile_x, tile_y, tile_z = tile_coords(tile_ref, block)
        planes = []
        for node in range(6):
            at = pl.ds(pl.multiple_of((4 * tile_x + node) * PY + 4 * tile_y, 4), 8)
            planes.append(velocity[at, :])
        rows = []
        for dim in range(3):
            merged = None
            for node in range(6):
                moved = pltpu.roll(
                    planes[node],
                    LANES + 8 * node - PITCH * dim - 4 * tile_z,
                    axis=1,
                )
                merged = moved if merged is None else jnp.where(lanes < 8 * node, merged, moved)
            rows.append(merged)
        return jnp.concatenate(rows, axis=0)

    def contract(block, left_side):
        row = row_of(block)
        wz, wzd = axis_weights(row, T_LZ, T_MZ, T_RZ, T_OZ, T_Z)
        wx = [row(T_WX + node) for node in range(6)]
        wxd = [row(T_WXD + node) for node in range(6)]
        right_side = jnp.concatenate(
            [
                jnp.concatenate([w * wz for w in wx], axis=0),
                jnp.concatenate([w * wz for w in wxd], axis=0),
                jnp.concatenate([w * wzd for w in wx], axis=0),
            ],
            axis=1,
        )
        left_high, left_low = split(left_side[:, :48])
        right_high, right_low = split(right_side)
        both = jnp.dot(
            jnp.concatenate([left_high, left_low], axis=0),
            right_high,
            preferred_element_type=jnp.float32,
        )
        return (
            both[:24]
            + both[24:]
            + jnp.dot(left_high, right_low, preferred_element_type=jnp.float32)
        )

    def weigh(block, sums):
        wy, wyd = axis_weights(row_of(block), T_LY, T_MY, T_RY, T_OY, T_Y)
        for dim in range(3):
            part = sums[8 * dim : 8 * dim + 8]
            terms = (
                (dim, wy * part[:, :128]),
                (3 + 3 * dim, wy * part[:, 128:256]),
                (4 + 3 * dim, wyd * part[:, :128]),
                (5 + 3 * dim, wy * part[:, 256:]),
            )
            for component, value in terms:
                at = pl.ds(pl.multiple_of(component * 8 * blocks + 8 * block, 8), 8)
                partial[at, :] = value

    def of_group(function, step, *values):
        return tuple(
            function(step * GROUP + member, *(value[member] for value in values))
            for member in range(GROUP)
        )

    def group(step, carry):
        left_sides, sums = carry
        following = of_group(gather, step + 2)
        products = of_group(contract, step + 1, left_sides)
        of_group(weigh, step, sums)
        return following, products

    steps = blocks // GROUP
    carry = of_group(gather, 1), of_group(contract, 0, of_group(gather, 0))
    left_sides, sums = lax.fori_loop(0, steps - 2, group, carry)
    of_group(weigh, steps - 2, sums)
    of_group(weigh, steps - 1, of_group(contract, steps - 1, left_sides))
    for component in range(12):
        total = partial[pl.ds(component * 8 * blocks, blocks, stride=8), :]
        for node in range(1, 6):
            total = total + partial[pl.ds(component * 8 * blocks + node, blocks, stride=8), :]
        if component >= 3:
            total = 4.0 * total
        final[component * blocks : (component + 1) * blocks, :] = total
    for block in range(blocks):
        cols = slice(block * BLOCK, (block + 1) * BLOCK)
        new_velocity_ref[:, cols] = final[pl.ds(block, 3, stride=blocks), :]
        new_affine_ref[:, cols] = final[pl.ds(3 * blocks + block, 9, stride=blocks), :]
    stress_copy.wait()
    grid_copy.wait()


def shards(
    point_frac,
    cell_offset,
    point_velocity,
    point_affine,
    point_stress,
    point_mass,
    block_tile,
    block_count,
):
    blocks = block_tile.shape[0]
    points = blocks * BLOCK
    vmem = pl.BlockSpec(memory_space=pltpu.VMEM)
    hbm = pl.BlockSpec(memory_space=pltpu.HBM)
    f32 = jnp.float32
    grid_shape = jax.ShapeDtypeStruct((ROWS, LANES), f32)
    face = PY + PY // 3
    arguments = [
        pltpu.with_memory_space_constraint(value, pltpu.HBM)
        for value in (
            block_tile,
            block_count,
            point_frac,
            cell_offset,
            point_velocity,
            point_affine,
            point_stress,
            point_mass.reshape(blocks, BLOCK),
        )
    ]
    mom, mass, shared, stress = pl.pallas_call(
        deposit_kernel,
        name="deposit",
        out_shape=(
            grid_shape,
            grid_shape,
            jax.ShapeDtypeStruct((T_SHARED * blocks, LANES), f32),
            jax.ShapeDtypeStruct((6 * blocks, LANES), f32),
        ),
        in_specs=[hbm] * 8,
        out_specs=(vmem,) * 4,
        scratch_shapes=[
            pltpu.SMEM((blocks,), jnp.int32),
            pltpu.SMEM((blocks,), jnp.int32),
            pltpu.VMEM((3, points), f32),
            pltpu.VMEM((3, points), jnp.int32),
            pltpu.VMEM((3, points), f32),
            pltpu.VMEM((9, points), f32),
            pltpu.VMEM((6, points), f32),
            pltpu.VMEM((blocks, BLOCK), f32),
            pltpu.VMEM((48 * blocks, LANES), f32),
            pltpu.VMEM(((T_ALL - T_SHARED) * blocks, LANES), f32),
            pltpu.VMEM((6, 8 * blocks, 2 * LANES), jnp.bfloat16),
            pltpu.VMEM((6, 8 * blocks, 2 * LANES), jnp.bfloat16),
            pltpu.VMEM((2, face, LANES), f32),
            pltpu.VMEM((2, face, LANES), f32),
            pltpu.VMEM((2, 2 * face, LANES), f32),
            pltpu.VMEM((2, 2 * face, LANES), f32),
            pltpu.VMEM((4, 16, LANES), f32),
            pltpu.VMEM((4, 16, LANES), f32),
            pltpu.VMEM((2, 3 * PX + 2, LANES), f32),
            pltpu.VMEM((2, 3 * PX + 2, LANES), f32),
            pltpu.SemaphoreType.DMA((8,)),
            pltpu.SemaphoreType.DMA((10,)),
            pltpu.SemaphoreType.DMA((10,)),
        ],
        compiler_params=pltpu.CompilerParams(
            collective_id=0, has_side_effects=True, vmem_limit_bytes=VMEM_LIMIT
        ),
    )(*arguments)
    new_velocity, new_affine, new_stress, grid_velocity = pl.pallas_call(
        collect_kernel,
        name="collect",
        out_shape=(
            jax.ShapeDtypeStruct((3, points), f32),
            jax.ShapeDtypeStruct((9, points), f32),
            jax.ShapeDtypeStruct((6, points), f32),
            jax.ShapeDtypeStruct((3, CX, CZ, CY), f32),
        ),
        in_specs=[hbm] + [vmem] * 4,
        out_specs=(vmem, vmem, hbm, hbm),
        scratch_shapes=[
            pltpu.SMEM((blocks,), jnp.int32),
            pltpu.VMEM((6, points), f32),
            pltpu.VMEM((3, CX, CZ, CY), f32),
            pltpu.VMEM((ROWS, LANES), f32),
            pltpu.VMEM((12 * 8 * blocks, LANES), f32),
            pltpu.VMEM((12 * blocks, LANES), f32),
            pltpu.SemaphoreType.DMA((3,)),
        ],
        compiler_params=pltpu.CompilerParams(vmem_limit_bytes=VMEM_LIMIT),
    )(arguments[0], mom, mass, shared, stress)
    return (new_velocity, new_affine, new_stress, jnp.swapaxes(grid_velocity, 2, 3))


def solution(mesh):
    points = P(None, ("gx", "gy", "gz"))
    flat = P(("gx", "gy", "gz"))
    return jax.shard_map(
        shards,
        mesh=mesh,
        in_specs=(points,) * 5 + (flat,) * 3,
        out_specs=(points, points, points, P(None, "gx", "gy", "gz")),
        check_vma=False,
    )
```

```python
import jax
import jax.numpy as jnp
from jax import lax
from jax.experimental import pallas as pl
from jax.experimental.pallas import tpu as pltpu
from jax.sharding import PartitionSpec as P

CX = 16
CY = 64
CZ = 32
BLOCK = 128

time_step = 0.1
gravity = 1.0
shear_modulus = 2.0
bulk_modulus = 4.0
friction_static = 0.38
friction_limit = 0.64
inertial_ref = 0.28
grain_size = 0.5
grain_density = 1.0
pressure_floor = 0.5
shear_floor = 0.5
mass_floor = 0.05
stress_scale = 0.4
pair_index = ((0, 5, 4), (5, 1, 3), (4, 3, 2))
component_pairs = ((0, 0), (1, 1), (2, 2), (1, 2), (0, 2), (0, 1))

PX = CX + 2
PY = 72
PITCH = 40
LANES = 128
ROWS = PX * PY
GROUP = 4
VMEM_LIMIT = 16 * 1024 * 1024
MESH = pl.DeviceIdType.MESH

T_WX, T_WXD = 0, 6
T_LY, T_MY, T_RY, T_OY, T_Y = 12, 13, 14, 15, 16
T_LZ, T_MZ, T_RZ, T_OZ, T_Z = 17, 18, 19, 20, 21
T_SHARED = 22
T_MASS, T_MV, T_A = 22, 23, 26
T_ALL = 35


def stress_update(stress, affine):
    strain_rate = [
        [
            0.5 * (affine[3 * row_dim + col_dim] + affine[3 * col_dim + row_dim])
            for col_dim in range(3)
        ]
        for row_dim in range(3)
    ]
    volume_rate = strain_rate[0][0] + strain_rate[1][1] + strain_rate[2][2]
    deviator = [
        [
            strain_rate[row_dim][col_dim] - (volume_rate / 3.0 if row_dim == col_dim else 0.0)
            for col_dim in range(3)
        ]
        for row_dim in range(3)
    ]
    trial_stress = []
    for component in range(6):
        row_dim, col_dim = component_pairs[component]
        value = stress[component] + time_step * 2.0 * shear_modulus * deviator[row_dim][col_dim]
        if component < 3:
            value = value + time_step * bulk_modulus * volume_rate
        trial_stress.append(value)
    pressure = -(trial_stress[0] + trial_stress[1] + trial_stress[2]) / 3.0
    shear_part = [trial_stress[component] + pressure for component in range(3)] + trial_stress[3:]
    shear_stress = jnp.sqrt(
        0.5 * (shear_part[0] ** 2 + shear_part[1] ** 2 + shear_part[2] ** 2)
        + shear_part[3] ** 2
        + shear_part[4] ** 2
        + shear_part[5] ** 2
    )
    shear_rate = jnp.sqrt(
        2.0
        * (
            deviator[0][0] ** 2
            + deviator[1][1] ** 2
            + deviator[2][2] ** 2
            + 2.0 * (deviator[1][2] ** 2 + deviator[0][2] ** 2 + deviator[0][1] ** 2)
        )
    )
    inertial = (
        shear_rate * grain_size / jnp.sqrt(jnp.maximum(pressure, pressure_floor) / grain_density)
    )
    friction = friction_static + (friction_limit - friction_static) * inertial / (
        inertial_ref + inertial
    )
    support = jnp.maximum(pressure, 0.0)
    factor = jnp.minimum(1.0, friction * support / jnp.maximum(shear_stress, shear_floor))
    return [shear_part[component] * factor - support for component in range(3)] + [
        shear_part[component] * factor for component in range(3, 6)
    ]


def split(values):
    high = values.astype(jnp.bfloat16)
    low = (values - high.astype(jnp.float32)).astype(jnp.bfloat16)
    return high, low


def tile_coords(tile_ref, block):
    tile = tile_ref[block]
    return tile >> 7, (tile >> 3) & 15, tile & 7


def axis_weights(row, left, middle, right, offset, position):
    index = lax.broadcasted_iota(jnp.int32, (8, LANES), 0).astype(jnp.float32)
    shifted = index - row(offset)
    weight = jnp.where(
        shifted == 0.0,
        row(left),
        jnp.where(shifted == 1.0, row(middle), jnp.where(shifted == 2.0, row(right), 0.0)),
    )
    return weight, weight * (index - row(position))


def deposit_kernel(
    tile_hbm,
    count_hbm,
    frac_hbm,
    offset_hbm,
    velocity_hbm,
    affine_hbm,
    stress_hbm,
    mass_hbm,
    mom,
    mass,
    shared_ref,
    stress_out,
    tile_ref,
    count_ref,
    frac_ref,
    offset_ref,
    velocity_ref,
    affine_ref,
    stress_ref,
    mass_ref,
    gathered,
    table,
    placed_high,
    placed_low,
    z_send,
    z_recv,
    x_send,
    x_recv,
    xz_send,
    xz_recv,
    y_send,
    y_recv,
    xy_send,
    xy_recv,
    load_sem,
    send_sem,
    recv_sem,
):
    axes = ("gx", "gy", "gz")

    def device(dx, dy, dz):
        place = []
        for axis, step in zip(axes, (dx, dy, dz)):
            size = lax.axis_size(axis)
            moved = lax.axis_index(axis)
            if step:
                moved = moved + step
                moved = jnp.where(moved < 0, size - 1, jnp.where(moved >= size, 0, moved))
            place.append(moved)
        return tuple(place)

    loads = [
        pltpu.make_async_copy(source, target, load_sem.at[index])
        for index, (source, target) in enumerate(
            (
                (frac_hbm, frac_ref),
                (offset_hbm, offset_ref),
                (velocity_hbm, velocity_ref),
                (affine_hbm, affine_ref),
                (stress_hbm, stress_ref),
                (mass_hbm, mass_ref),
                (count_hbm, count_ref),
                (tile_hbm, tile_ref),
            )
        )
    ]
    for load in loads:
        load.start()
    z_sides = [device(0, 0, -1), device(0, 0, 1)]
    x_sides = [device(-1, 0, 0), device(1, 0, 0)]
    y_sides = [device(0, -1, 0), device(0, 1, 0)]
    xz_sides = [device(dx, 0, dz) for dx in (-1, 1) for dz in (-1, 1)]
    xy_sides = [device(dx, dy, 0) for dx in (-1, 1) for dy in (-1, 1)]
    barrier = pltpu.get_barrier_semaphore()
    for target in z_sides + x_sides + xz_sides + y_sides + xy_sides:
        pl.semaphore_signal(barrier, inc=1, device_id=target, device_id_type=MESH)

    blocks = mass_ref.shape[0]
    lane_row = lax.broadcasted_iota(jnp.int32, (1, LANES), 1)
    stride = 48
    for load in loads:
        load.wait()
    for block in range(blocks):
        cols = slice(block * BLOCK, (block + 1) * BLOCK)
        at = block * stride
        gathered[at : at + 3, :] = frac_ref[:, cols]
        gathered[at + 8 : at + 11, :] = offset_ref[:, cols].astype(jnp.float32)
        gathered[at + 16 : at + 19, :] = velocity_ref[:, cols]
        gathered[at + 24 : at + 33, :] = affine_ref[:, cols]
        gathered[at + 40 : at + 46, :] = stress_ref[:, cols]
        row = (T_MASS - T_SHARED) * blocks + block
        table[row : row + 1, :] = jnp.where(
            lane_row < count_ref[block], mass_ref[block : block + 1, :], 0.0
        )

    def dense(component):
        return gathered[pl.ds(component, blocks, stride=stride), :]

    def put(index, value):
        if index < T_SHARED:
            shared_ref[index * blocks : (index + 1) * blocks, :] = value
        else:
            start = (index - T_SHARED) * blocks
            table[start : start + blocks, :] = value

    affine = [dense(24 + component) for component in range(9)]
    stress = stress_update([dense(40 + component) for component in range(6)], affine)
    for component in range(6):
        stress_out[component * blocks : (component + 1) * blocks, :] = stress[component]
    live_mass = table[(T_MASS - T_SHARED) * blocks : (T_MASS - T_SHARED + 1) * blocks, :]
    for row_dim in range(3):
        put(T_MV + row_dim, live_mass * dense(16 + row_dim))
        for col_dim in range(3):
            put(
                T_A + 3 * row_dim + col_dim,
                live_mass
                * (
                    affine[3 * row_dim + col_dim]
                    - stress_scale * stress[pair_index[row_dim][col_dim]]
                ),
            )
    spline = []
    for dim in range(3):
        fraction = dense(dim)
        spline.append(
            (
                0.5 * (1.5 - fraction) ** 2,
                0.75 - (fraction - 1.0) ** 2,
                0.5 * (fraction - 0.5) ** 2,
                dense(8 + dim),
                dense(8 + dim) + fraction,
            )
        )
    left, middle, right, offset, position = spline[0]
    for node in range(6):
        shifted = float(node) - offset
        weight = jnp.where(
            shifted == 0.0,
            left,
            jnp.where(shifted == 1.0, middle, jnp.where(shifted == 2.0, right, 0.0)),
        )
        put(T_WX + node, weight)
        put(T_WXD + node, weight * (float(node) - position))
    for index in range(5):
        put(T_LY + index, spline[1][index])
        put(T_LZ + index, spline[2][index])

    lanes = lax.broadcasted_iota(jnp.int32, (8, 32), 1)
    channel = [(lanes >= 8 * index) & (lanes < 8 * index + 8) for index in range(4)]
    rest = jnp.zeros((8, LANES - 32), jnp.float32)
    blank = jnp.zeros((8, LANES), jnp.float32)

    def block_sums(block):
        def row(index):
            if index < T_SHARED:
                value = shared_ref[pl.ds(index * blocks + block, 1), :]
            else:
                value = table[pl.ds((index - T_SHARED) * blocks + block, 1), :]
            return jnp.broadcast_to(value, (8, LANES))

        wy, wyd = axis_weights(row, T_LY, T_MY, T_RY, T_OY, T_Y)
        wz, wzd = axis_weights(row, T_LZ, T_MZ, T_RZ, T_OZ, T_Z)
        wx = [row(T_WX + node) for node in range(6)]
        wxd = [row(T_WXD + node) for node in range(6)]
        left_side = jnp.concatenate(
            [
                jnp.concatenate([w * wy for w in wx], axis=0),
                jnp.concatenate([w * wy for w in wxd], axis=0),
                jnp.concatenate([w * wyd for w in wx], axis=0),
            ],
            axis=1,
        )
        value_rows = [
            wz * row(T_MV + dim) + wzd * row(T_A + 3 * dim + 2) for dim in range(3)
        ] + [wz * row(T_MASS)]
        x_rows = [wz * row(T_A + 3 * dim) for dim in range(3)] + [blank]
        y_rows = [wz * row(T_A + 3 * dim + 1) for dim in range(3)] + [blank]
        right_side = jnp.concatenate(
            [jnp.concatenate(r, axis=0) for r in (value_rows, x_rows, y_rows)], axis=1
        )
        left_high, left_low = split(left_side)
        right_high, right_low = split(right_side)

        return lax.dot_general(
            jnp.concatenate([left_high, left_high, left_low], axis=1),
            jnp.concatenate([right_high, right_low, right_high], axis=1),
            (((1,), (1,)), ((), ())),
            preferred_element_type=jnp.float32,
        )

    starts = (0, PITCH - 8, 2 * PITCH - 16, LANES - 24)

    def group_place(step, sums):
        rows = pl.ds(pl.multiple_of(step * 8 * GROUP, 8 * GROUP), 8 * GROUP)
        heights = [4 * (tile_ref[step * GROUP + member] & 7) for member in range(GROUP)]
        for node in range(6):
            mom_rows, mass_rows = [], []
            for member in range(GROUP):
                part = sums[member][8 * node : 8 * node + 8]
                moved = [
                    pltpu.roll(
                        jnp.concatenate([jnp.where(channel[index], part, 0.0), rest], axis=1),
                        starts[index] + heights[member],
                        axis=1,
                    )
                    for index in range(4)
                ]
                mom_rows.append(moved[0] + moved[1] + moved[2])
                mass_rows.append(moved[3])
            for column, values in enumerate((mom_rows, mass_rows)):
                high, low = split(jnp.concatenate(values, axis=0))
                cols = slice(column * LANES, (column + 1) * LANES)
                placed_high[node, rows, cols] = high
                placed_low[node, rows, cols] = low

    def group_sums(step):
        return tuple(block_sums(step * GROUP + member) for member in range(GROUP))

    def group(step, sums):
        following = group_sums(step)
        group_place(step - 1, sums)
        return following

    steps = blocks // GROUP
    group_place(steps - 1, lax.fori_loop(1, steps, group, group_sums(0)))

    spots = 8 * blocks
    spot = lax.broadcasted_iota(jnp.int32, (8, spots), 1)
    owner = spot >> 3
    tiles = jnp.zeros((8, spots), jnp.int32)
    for block in range(blocks):
        tiles = jnp.where(owner == block, tile_ref[block], tiles)
    target = ((tiles >> 7) << 10) + (((tiles >> 3) & 15) << 2) + (spot & 7)
    y_row = lax.broadcasted_iota(jnp.int32, (8, spots), 0)
    chooser = jnp.concatenate(
        [
            jnp.where(target == y_row + (1024 * tile_x + start), 1.0, 0.0)
            for tile_x in range(CX // 4)
            for start in range(0, PY, 8)
        ],
        axis=0,
    ).astype(jnp.bfloat16)
    for node in range(6):
        layers = jnp.dot(
            chooser, placed_high[node], preferred_element_type=jnp.float32
        ) + jnp.dot(chooser, placed_low[node], preferred_element_type=jnp.float32)
        for tile_x in range(CX // 4):
            part = layers[tile_x * PY : (tile_x + 1) * PY]
            x = 4 * tile_x + node
            at = slice(x * PY, (x + 1) * PY)
            if node < 4 or x >= CX:
                mom[at, :] = part[:, :LANES]
                mass[at, :] = part[:, LANES:]
            else:
                mom[at, :] += part[:, :LANES]
                mass[at, :] += part[:, LANES:]

    def copy(src, dst, slot, target):
        return pltpu.make_async_remote_copy(
            src_ref=src,
            dst_ref=dst,
            send_sem=send_sem.at[slot],
            recv_sem=recv_sem.at[slot],
            device_id=target,
            device_id_type=MESH,
        )

    lane = lax.broadcasted_iota(jnp.int32, (PY, LANES), 1)
    in_mom = lane < 3 * PITCH
    in_pitch = lax.rem(lane, PITCH)
    third = PY // 3
    lane3 = lane[:third]
    pl.semaphore_wait(barrier, 14)

    firsts = (0, CX * PY)
    for side in range(2):
        first = firsts[side]
        x_send[side, : 2 * PY, :] = mom[first : first + 2 * PY, :]
        for layer in range(2):
            start = first + layer * PY
            at = 2 * PY + layer * third
            x_send[side, at : at + third, :] = (
                mass[start : start + third, :]
                + pltpu.roll(mass[start + third : start + 2 * third, :], PITCH, axis=1)
                + pltpu.roll(mass[start + 2 * third : start + 3 * third, :], 2 * PITCH, axis=1)
            )
    x_copies = [
        copy(x_send.at[side], x_recv.at[1 - side], 2 + side, x_sides[side]) for side in range(2)
    ]
    for c in x_copies:
        c.start()

    pair = jnp.where(in_mom, in_pitch >> 1, -1)
    far = lax.rem(lane + (LANES - CZ), LANES)
    far_pair = jnp.where(far < 3 * PITCH, lax.rem(far, PITCH) >> 1, -1)
    pair3 = lane3 >> 1
    far_pair3 = far[:third] >> 1
    packed, packed_mass = [None, None], [None, None]
    for x in range(PX):
        at = slice(x * PY, (x + 1) * PY)
        moved = pltpu.roll(mom[at, :], 2 * x, axis=1) if x else mom[at, :]
        for side, which in enumerate((pair, far_pair)):
            packed[side] = jnp.where(which == x, moved, packed[side] if x else 0.0)
        for part in range(3):
            start = PITCH * part
            rows = slice(x * PY + part * third, x * PY + (part + 1) * third)
            moved = mass[rows, :]
            if start + 2 * x:
                moved = pltpu.roll(moved, start + 2 * x, axis=1)
            for side, which in enumerate((pair3, far_pair3)):
                packed_mass[side] = jnp.where(
                    which == start // 2 + x, moved, packed_mass[side] if start + x else 0.0
                )
    for side in range(2):
        z_send[side, :PY, :] = packed[side]
        z_send[side, PY:, :] = packed_mass[side]
    z_copies = [
        copy(z_send.at[side], z_recv.at[1 - side], side, z_sides[side]) for side in range(2)
    ]
    for c in z_copies:
        c.start()

    quad = lax.broadcasted_iota(jnp.int32, (8, LANES), 1) >> 2
    for edge in range(4):
        x0, z_side = CX * (edge // 2), edge % 2
        result = [None, None]
        for tile in range(PY // 8):
            half, start = tile // 8, 16 * (tile % 8)
            rows = z_send[z_side, 8 * tile : 8 * tile + 8, :]
            mass_at = PY + 8 * (tile % 3)
            mass_rows = z_send[z_side, mass_at : mass_at + 8, :]
            for index in range(4):
                if index < 3:
                    source, at = rows, PITCH * index + 2 * x0 + CZ * z_side
                else:
                    source, at = mass_rows, PITCH * (tile // 3) + 2 * x0 + CZ * z_side
                to = start + 4 * index
                moved = pltpu.roll(source, (2 * LANES + to - at) % LANES, axis=1)
                if result[half] is None:
                    result[half] = moved
                else:
                    result[half] = jnp.where(quad == to // 4, moved, result[half])
        xz_send[edge, :8, :] = result[0]
        xz_send[edge, 8:, :] = result[1]
    xz_copies = [
        copy(xz_send.at[edge], xz_recv.at[3 - edge], 6 + edge, xz_sides[edge])
        for edge in range(4)
    ]
    for c in xz_copies:
        c.start()

    for c in z_copies:
        c.wait()
    rim = in_mom & ((in_pitch < 2) | ((in_pitch >= CZ) & (in_pitch < CZ + 2)))
    rim3 = (lane3 < 2) | ((lane3 >= CZ) & (lane3 < CZ + 2))
    from_low = pltpu.roll(z_recv[0], 64, axis=1)
    from_high = z_recv[1]
    for x in range(PX):
        at = slice(x * PY, (x + 1) * PY)
        joined = jnp.where(pair == x, from_high[:PY], from_low[:PY])
        moved = pltpu.roll(joined, (LANES + CZ - 2 * x) % LANES, axis=1)
        mom[at, :] += jnp.where(rim, moved, 0.0)
        for part in range(3):
            start = PITCH * part
            rows = slice(x * PY + part * third, x * PY + (part + 1) * third)
            joined = jnp.where(pair3 == start // 2 + x, from_high[PY:], from_low[PY:])
            moved = pltpu.roll(joined, (2 * LANES + CZ - start - 2 * x) % LANES, axis=1)
            mass[rows, :] += jnp.where(rim3, moved, 0.0)

    y_firsts = (0, CY)
    for side in range(2):
        y0 = y_firsts[side]
        y_send[side, 0:PX, :] = mom[pl.ds(y0, PX, stride=PY), :]
        y_send[side, PX : 2 * PX, :] = mom[pl.ds(y0 + 1, PX, stride=PY), :]
        y_send[side, 2 * PX : 3 * PX, :] = mass[pl.ds(y0, PX, stride=PY), :] + pltpu.roll(
            mass[pl.ds(y0 + 1, PX, stride=PY), :], 64, axis=1
        )
        y_send[side, 3 * PX :, :] = jnp.zeros((2, LANES), jnp.float32)
    y_copies = [
        copy(y_send.at[side], y_recv.at[1 - side], 4 + side, y_sides[side]) for side in range(2)
    ]
    for edge in range(4):
        x0, y0 = CX * (edge // 2), y_firsts[edge % 2]
        for layer in range(2):
            at = (x0 + layer) * PY + y0
            xy_send[edge, 2 * layer : 2 * layer + 2, :] = mom[at : at + 2, :]
            xy_send[edge, 4 + 2 * layer : 6 + 2 * layer, :] = mass[at : at + 2, :]
        y_copies.append(copy(xy_send.at[edge], xy_recv.at[3 - edge], 10 + edge, xy_sides[edge]))
    for c in y_copies:
        c.start()

    for c in xz_copies:
        c.wait()
    lane8 = lane[:8]
    for side in range(2):
        for layer in range(2):
            for tile in range(PY // 8):
                half, start = tile // 8, 16 * (tile % 8)
                mom_value, mass_value = 0.0, 0.0
                for z_side in range(2):
                    source = xz_recv[2 * side + z_side, 8 * half : 8 * half + 8, :]
                    for index in range(4):
                        to = (PITCH * index if index < 3 else 0) + CZ * z_side
                        at = start + 4 * index + 2 * layer
                        moved = pltpu.roll(source, (LANES + to - at) % LANES, axis=1)
                        here = (lane8 >= to) & (lane8 < to + 2)
                        if index < 3:
                            mom_value = jnp.where(here, moved, mom_value)
                        else:
                            mass_value = jnp.where(here, moved, mass_value)
                at = firsts[side] + layer * PY + 8 * tile
                mom[at : at + 8, :] += mom_value
                mass[at : at + 8, :] += mass_value

    for c in x_copies:
        c.wait()
    near3 = lane3 < PITCH
    for side in range(2):
        first = firsts[side]
        mom[first : first + 2 * PY, :] += x_recv[side, : 2 * PY, :]
        for layer in range(2):
            at = 2 * PY + layer * third
            got = x_recv[side, at : at + third, :]
            for part in range(3):
                start = first + layer * PY + part * third
                moved = pltpu.roll(got, (LANES - PITCH * part) % LANES, axis=1)
                mass[start : start + third, :] += jnp.where(near3, moved, 0.0)
    front = lane < 64
    for c in y_copies:
        c.wait()
    for side in range(2):
        y0 = y_firsts[side]
        got = y_recv[side, 2 * PX : 3 * PX, :]
        at0 = pl.ds(y0, PX, stride=PY)
        at1 = pl.ds(y0 + 1, PX, stride=PY)
        mom[at0, :] = mom[at0, :] + y_recv[side, 0:PX, :]
        mom[at1, :] = mom[at1, :] + y_recv[side, PX : 2 * PX, :]
        mass[at0, :] = mass[at0, :] + jnp.where(front[:PX], got, 0.0)
        mass[at1, :] = mass[at1, :] + jnp.where(front[:PX], pltpu.roll(got, 64, axis=1), 0.0)
    for edge in range(4):
        x0, y0 = CX * (edge // 2), y_firsts[edge % 2]
        for layer in range(2):
            at = (x0 + layer) * PY + y0
            mom[at : at + 2, :] += xy_recv[edge, 2 * layer : 2 * layer + 2, :]
            mass[at : at + 2, :] += xy_recv[edge, 4 + 2 * layer : 6 + 2 * layer, :]


def collect_kernel(
    tile_hbm,
    mom_ref,
    mass_ref,
    shared_ref,
    stress_in,
    new_velocity_ref,
    new_affine_ref,
    new_stress_hbm,
    grid_velocity_hbm,
    tile_ref,
    new_stress_ref,
    grid_velocity_ref,
    velocity,
    partial,
    final,
    copy_sem,
):
    blocks = tile_hbm.shape[0]
    tile_copy = pltpu.make_async_copy(tile_hbm, tile_ref, copy_sem.at[0])
    tile_copy.start()
    for block in range(blocks):
        new_stress_ref[:, block * BLOCK : (block + 1) * BLOCK] = stress_in[
            pl.ds(block, 6, stride=blocks), :
        ]
    stress_copy = pltpu.make_async_copy(new_stress_ref, new_stress_hbm, copy_sem.at[1])
    stress_copy.start()
    width_x = lax.axis_size("gx") * CX
    height_y = lax.axis_size("gy") * CY
    depth_z = lax.axis_size("gz") * CZ
    lane = lax.broadcasted_iota(jnp.int32, (PY, LANES), 1)
    row_index = lax.broadcasted_iota(jnp.int32, (PY, LANES), 0)
    first_z = lax.axis_index("gz") * CZ
    first_y = lax.axis_index("gy") * CY
    first_x = lax.axis_index("gx") * CX
    z_index = lax.rem(lane - 2 * PITCH - 1 + first_z + depth_z, depth_z)
    y_index = lax.rem(row_index - 1 + first_y + height_y, height_y)
    is_y = (lane >= PITCH) & (lane < 2 * PITCH)
    is_z = (lane >= 2 * PITCH) & (lane < 3 * PITCH)
    z_floor = is_z & (z_index < 2)
    z_top = is_z & (z_index >= depth_z - 2)
    y_floor = is_y & (y_index < 2)
    fall = jnp.where(is_y, time_step * gravity, 0.0)

    def layer(x):
        at = pl.ds(pl.multiple_of(x * PY, 8), PY)
        x_index = lax.rem(first_x + x - 1 + width_x, width_x)
        outlet = (x_index >= width_x // 4) & (x_index < width_x - width_x // 4)
        inverse = 1.0 / (mass_ref[at, :] + mass_floor)
        inverse = jnp.where(
            lane < PITCH,
            inverse,
            jnp.where(
                is_y, pltpu.roll(inverse, PITCH, axis=1), pltpu.roll(inverse, 2 * PITCH, axis=1)
            ),
        )
        values = mom_ref[at, :] * inverse - fall
        lifted = jnp.maximum(values, 0.0)
        values = jnp.where(
            z_floor | (y_floor & jnp.logical_not(outlet)), lifted, values
        )
        values = jnp.where(z_top, jnp.minimum(values, 0.0), values)
        velocity[at, :] = values

    def layers(step, carry):
        for member in range(3):
            layer(3 * step + member)
        return carry

    lax.fori_loop(0, PX // 3, layers, 0)

    def output(step, carry):
        for member in range(4):
            x = 4 * step + member
            turned = jnp.transpose(velocity[pl.ds((x + 1) * PY + 1, CY), :])
            for dim in range(3):
                grid_velocity_ref[dim, x] = turned[PITCH * dim + 1 : PITCH * dim + 1 + CZ]
        return carry

    lax.fori_loop(0, CX // 4, output, 0)
    grid_copy = pltpu.make_async_copy(grid_velocity_ref, grid_velocity_hbm, copy_sem.at[2])
    grid_copy.start()
    tile_copy.wait()

    lanes = lax.broadcasted_iota(jnp.int32, (8, LANES), 1)

    def row_of(block):
        def row(index):
            return jnp.broadcast_to(shared_ref[pl.ds(index * blocks + block, 1), :], (8, LANES))

        return row

    def gather(block):
        tile_x, tile_y, tile_z = tile_coords(tile_ref, block)
        planes = []
        for node in range(6):
            at = pl.ds(pl.multiple_of((4 * tile_x + node) * PY + 4 * tile_y, 4), 8)
            planes.append(velocity[at, :])
        rows = []
        for dim in range(3):
            merged = None
            for node in range(6):
                moved = pltpu.roll(
                    planes[node],
                    LANES + 8 * node - PITCH * dim - 4 * tile_z,
                    axis=1,
                )
                merged = moved if merged is None else jnp.where(lanes < 8 * node, merged, moved)
            rows.append(merged)
        return jnp.concatenate(rows, axis=0)

    def contract(block, left_side):
        row = row_of(block)
        wz, wzd = axis_weights(row, T_LZ, T_MZ, T_RZ, T_OZ, T_Z)
        wx = [row(T_WX + node) for node in range(6)]
        wxd = [row(T_WXD + node) for node in range(6)]
        right_side = jnp.concatenate(
            [
                jnp.concatenate([w * wz for w in wx], axis=0),
                jnp.concatenate([w * wz for w in wxd], axis=0),
                jnp.concatenate([w * wzd for w in wx], axis=0),
            ],
            axis=1,
        )
        left_high, left_low = split(left_side[:, :48])
        right_high, right_low = split(right_side)
        both = jnp.dot(
            jnp.concatenate([left_high, left_low], axis=0),
            right_high,
            preferred_element_type=jnp.float32,
        )
        return (
            both[:24]
            + both[24:]
            + jnp.dot(left_high, right_low, preferred_element_type=jnp.float32)
        )

    def weigh(block, sums):
        wy, wyd = axis_weights(row_of(block), T_LY, T_MY, T_RY, T_OY, T_Y)
        for dim in range(3):
            part = sums[8 * dim : 8 * dim + 8]
            terms = (
                (dim, wy * part[:, :128]),
                (3 + 3 * dim, wy * part[:, 128:256]),
                (4 + 3 * dim, wyd * part[:, :128]),
                (5 + 3 * dim, wy * part[:, 256:]),
            )
            for component, value in terms:
                at = pl.ds(pl.multiple_of(component * 8 * blocks + 8 * block, 8), 8)
                partial[at, :] = value

    def of_group(function, step, *values):
        return tuple(
            function(step * GROUP + member, *(value[member] for value in values))
            for member in range(GROUP)
        )

    def group(step, carry):
        left_sides, sums = carry
        following = of_group(gather, step + 2)
        products = of_group(contract, step + 1, left_sides)
        of_group(weigh, step, sums)
        return following, products

    steps = blocks // GROUP
    carry = of_group(gather, 1), of_group(contract, 0, of_group(gather, 0))
    left_sides, sums = lax.fori_loop(0, steps - 2, group, carry)
    of_group(weigh, steps - 2, sums)
    of_group(weigh, steps - 1, of_group(contract, steps - 1, left_sides))
    for component in range(12):
        total = partial[pl.ds(component * 8 * blocks, blocks, stride=8), :]
        for node in range(1, 6):
            total = total + partial[pl.ds(component * 8 * blocks + node, blocks, stride=8), :]
        if component >= 3:
            total = 4.0 * total
        final[component * blocks : (component + 1) * blocks, :] = total
    for block in range(blocks):
        cols = slice(block * BLOCK, (block + 1) * BLOCK)
        new_velocity_ref[:, cols] = final[pl.ds(block, 3, stride=blocks), :]
        new_affine_ref[:, cols] = final[pl.ds(3 * blocks + block, 9, stride=blocks), :]
    stress_copy.wait()
    grid_copy.wait()


def shards(
    point_frac,
    cell_offset,
    point_velocity,
    point_affine,
    point_stress,
    point_mass,
    block_tile,
    block_count,
):
    blocks = block_tile.shape[0]
    points = blocks * BLOCK
    vmem = pl.BlockSpec(memory_space=pltpu.VMEM)
    hbm = pl.BlockSpec(memory_space=pltpu.HBM)
    f32 = jnp.float32
    grid_shape = jax.ShapeDtypeStruct((ROWS, LANES), f32)
    face = PY + PY // 3
    arguments = [
        pltpu.with_memory_space_constraint(value, pltpu.HBM)
        for value in (
            block_tile,
            block_count,
            point_frac,
            cell_offset,
            point_velocity,
            point_affine,
            point_stress,
            point_mass.reshape(blocks, BLOCK),
        )
    ]
    mom, mass, shared, stress = pl.pallas_call(
        deposit_kernel,
        name="deposit",
        out_shape=(
            grid_shape,
            grid_shape,
            jax.ShapeDtypeStruct((T_SHARED * blocks, LANES), f32),
            jax.ShapeDtypeStruct((6 * blocks, LANES), f32),
        ),
        in_specs=[hbm] * 8,
        out_specs=(vmem,) * 4,
        scratch_shapes=[
            pltpu.SMEM((blocks,), jnp.int32),
            pltpu.SMEM((blocks,), jnp.int32),
            pltpu.VMEM((3, points), f32),
            pltpu.VMEM((3, points), jnp.int32),
            pltpu.VMEM((3, points), f32),
            pltpu.VMEM((9, points), f32),
            pltpu.VMEM((6, points), f32),
            pltpu.VMEM((blocks, BLOCK), f32),
            pltpu.VMEM((48 * blocks, LANES), f32),
            pltpu.VMEM(((T_ALL - T_SHARED) * blocks, LANES), f32),
            pltpu.VMEM((6, 8 * blocks, 2 * LANES), jnp.bfloat16),
            pltpu.VMEM((6, 8 * blocks, 2 * LANES), jnp.bfloat16),
            pltpu.VMEM((2, face, LANES), f32),
            pltpu.VMEM((2, face, LANES), f32),
            pltpu.VMEM((2, 2 * face, LANES), f32),
            pltpu.VMEM((2, 2 * face, LANES), f32),
            pltpu.VMEM((4, 16, LANES), f32),
            pltpu.VMEM((4, 16, LANES), f32),
            pltpu.VMEM((2, 3 * PX + 2, LANES), f32),
            pltpu.VMEM((2, 3 * PX + 2, LANES), f32),
            pltpu.VMEM((4, 8, LANES), f32),
            pltpu.VMEM((4, 8, LANES), f32),
            pltpu.SemaphoreType.DMA((8,)),
            pltpu.SemaphoreType.DMA((14,)),
            pltpu.SemaphoreType.DMA((14,)),
        ],
        compiler_params=pltpu.CompilerParams(
            collective_id=0, has_side_effects=True, vmem_limit_bytes=VMEM_LIMIT
        ),
    )(*arguments)
    new_velocity, new_affine, new_stress, grid_velocity = pl.pallas_call(
        collect_kernel,
        name="collect",
        out_shape=(
            jax.ShapeDtypeStruct((3, points), f32),
            jax.ShapeDtypeStruct((9, points), f32),
            jax.ShapeDtypeStruct((6, points), f32),
            jax.ShapeDtypeStruct((3, CX, CZ, CY), f32),
        ),
        in_specs=[hbm] + [vmem] * 4,
        out_specs=(vmem, vmem, hbm, hbm),
        scratch_shapes=[
            pltpu.SMEM((blocks,), jnp.int32),
            pltpu.VMEM((6, points), f32),
            pltpu.VMEM((3, CX, CZ, CY), f32),
            pltpu.VMEM((ROWS, LANES), f32),
            pltpu.VMEM((12 * 8 * blocks, LANES), f32),
            pltpu.VMEM((12 * blocks, LANES), f32),
            pltpu.SemaphoreType.DMA((3,)),
        ],
        compiler_params=pltpu.CompilerParams(vmem_limit_bytes=VMEM_LIMIT),
    )(arguments[0], mom, mass, shared, stress)
    return (new_velocity, new_affine, new_stress, jnp.swapaxes(grid_velocity, 2, 3))


def solution(mesh):
    points = P(None, ("gx", "gy", "gz"))
    flat = P(("gx", "gy", "gz"))
    return jax.shard_map(
        shards,
        mesh=mesh,
        in_specs=(points,) * 5 + (flat,) * 3,
        out_specs=(points, points, points, P(None, "gx", "gy", "gz")),
        check_vma=False,
    )
```

```python
import jax
import jax.numpy as jnp
from jax import lax
from jax.experimental import pallas as pl
from jax.experimental.pallas import tpu as pltpu
from jax.sharding import PartitionSpec as P

CX = 16
CY = 64
CZ = 32
BLOCK = 128

time_step = 0.1
gravity = 1.0
shear_modulus = 2.0
bulk_modulus = 4.0
friction_static = 0.38
friction_limit = 0.64
inertial_ref = 0.28
grain_size = 0.5
grain_density = 1.0
pressure_floor = 0.5
shear_floor = 0.5
mass_floor = 0.05
stress_scale = 0.4
pair_index = ((0, 5, 4), (5, 1, 3), (4, 3, 2))
component_pairs = ((0, 0), (1, 1), (2, 2), (1, 2), (0, 2), (0, 1))

PX = CX + 2
PY = 72
PITCH = 40
LANES = 128
ROWS = PX * PY
GROUP = 4
VMEM_LIMIT = 16 * 1024 * 1024
MESH = pl.DeviceIdType.MESH

T_WX, T_WXD = 0, 6
T_LY, T_MY, T_RY, T_OY, T_Y = 12, 13, 14, 15, 16
T_LZ, T_MZ, T_RZ, T_OZ, T_Z = 17, 18, 19, 20, 21
T_SHARED = 22
T_MASS, T_MV, T_A = 22, 23, 26
T_ALL = 35


def stress_update(stress, affine):
    strain_rate = [
        [
            0.5 * (affine[3 * row_dim + col_dim] + affine[3 * col_dim + row_dim])
            for col_dim in range(3)
        ]
        for row_dim in range(3)
    ]
    volume_rate = strain_rate[0][0] + strain_rate[1][1] + strain_rate[2][2]
    deviator = [
        [
            strain_rate[row_dim][col_dim] - (volume_rate / 3.0 if row_dim == col_dim else 0.0)
            for col_dim in range(3)
        ]
        for row_dim in range(3)
    ]
    trial_stress = []
    for component in range(6):
        row_dim, col_dim = component_pairs[component]
        value = stress[component] + time_step * 2.0 * shear_modulus * deviator[row_dim][col_dim]
        if component < 3:
            value = value + time_step * bulk_modulus * volume_rate
        trial_stress.append(value)
    pressure = -(trial_stress[0] + trial_stress[1] + trial_stress[2]) / 3.0
    shear_part = [trial_stress[component] + pressure for component in range(3)] + trial_stress[3:]
    shear_stress = jnp.sqrt(
        0.5 * (shear_part[0] ** 2 + shear_part[1] ** 2 + shear_part[2] ** 2)
        + shear_part[3] ** 2
        + shear_part[4] ** 2
        + shear_part[5] ** 2
    )
    shear_rate = jnp.sqrt(
        2.0
        * (
            deviator[0][0] ** 2
            + deviator[1][1] ** 2
            + deviator[2][2] ** 2
            + 2.0 * (deviator[1][2] ** 2 + deviator[0][2] ** 2 + deviator[0][1] ** 2)
        )
    )
    inertial = (
        shear_rate * grain_size / jnp.sqrt(jnp.maximum(pressure, pressure_floor) / grain_density)
    )
    friction = friction_static + (friction_limit - friction_static) * inertial / (
        inertial_ref + inertial
    )
    support = jnp.maximum(pressure, 0.0)
    factor = jnp.minimum(1.0, friction * support / jnp.maximum(shear_stress, shear_floor))
    return [shear_part[component] * factor - support for component in range(3)] + [
        shear_part[component] * factor for component in range(3, 6)
    ]


def split(values):
    high = values.astype(jnp.bfloat16)
    low = (values - high.astype(jnp.float32)).astype(jnp.bfloat16)
    return high, low


def tile_coords(tile_ref, block):
    tile = tile_ref[block]
    return tile >> 7, (tile >> 3) & 15, tile & 7


def axis_weights(row, left, middle, right, offset, position):
    index = lax.broadcasted_iota(jnp.int32, (8, LANES), 0).astype(jnp.float32)
    shifted = index - row(offset)
    weight = jnp.where(
        shifted == 0.0,
        row(left),
        jnp.where(shifted == 1.0, row(middle), jnp.where(shifted == 2.0, row(right), 0.0)),
    )
    return weight, weight * (index - row(position))


def deposit_kernel(
    tile_hbm,
    count_hbm,
    frac_hbm,
    offset_hbm,
    velocity_hbm,
    affine_hbm,
    stress_hbm,
    mass_hbm,
    velocity_out,
    collect_high,
    collect_low,
    y_table,
    stress_out,
    mom,
    mass,
    shared_ref,
    tile_ref,
    count_ref,
    frac_ref,
    offset_ref,
    velocity_ref,
    affine_ref,
    stress_ref,
    mass_ref,
    gathered,
    table,
    placed_high,
    placed_low,
    z_send,
    z_recv,
    x_send,
    x_recv,
    xz_send,
    xz_recv,
    y_send,
    y_recv,
    xy_send,
    xy_recv,
    load_sem,
    send_sem,
    recv_sem,
):
    axes = ("gx", "gy", "gz")

    def device(dx, dy, dz):
        place = []
        for axis, step in zip(axes, (dx, dy, dz)):
            size = lax.axis_size(axis)
            moved = lax.axis_index(axis)
            if step and size & (size - 1) == 0:
                moved = (moved + size + step) & (size - 1)
            elif step:
                moved = lax.rem(moved + size + step, size)
            place.append(moved)
        return tuple(place)

    loads = [
        pltpu.make_async_copy(source, target, load_sem.at[index])
        for index, (source, target) in enumerate(
            (
                (frac_hbm, frac_ref),
                (offset_hbm, offset_ref),
                (velocity_hbm, velocity_ref),
                (affine_hbm, affine_ref),
                (stress_hbm, stress_ref),
                (mass_hbm, mass_ref),
                (count_hbm, count_ref),
                (tile_hbm, tile_ref),
            )
        )
    ]
    for load in loads:
        load.start()
    z_sides = [device(0, 0, -1), device(0, 0, 1)]
    x_sides = [device(-1, 0, 0), device(1, 0, 0)]
    y_sides = [device(0, -1, 0), device(0, 1, 0)]
    xz_sides = [device(dx, 0, dz) for dx in (-1, 1) for dz in (-1, 1)]
    xy_sides = [device(dx, dy, 0) for dx in (-1, 1) for dy in (-1, 1)]
    barrier = pltpu.get_barrier_semaphore()
    for target in z_sides + x_sides + xz_sides + y_sides + xy_sides:
        pl.semaphore_signal(barrier, inc=1, device_id=target, device_id_type=MESH)

    blocks = mass_ref.shape[0]
    lane_row = lax.broadcasted_iota(jnp.int32, (1, LANES), 1)
    stride = 48
    for load in loads:
        load.wait()
    for block in range(blocks):
        cols = slice(block * BLOCK, (block + 1) * BLOCK)
        at = block * stride
        gathered[at : at + 3, :] = frac_ref[:, cols]
        gathered[at + 8 : at + 11, :] = offset_ref[:, cols].astype(jnp.float32)
        gathered[at + 16 : at + 19, :] = velocity_ref[:, cols]
        gathered[at + 24 : at + 33, :] = affine_ref[:, cols]
        gathered[at + 40 : at + 46, :] = stress_ref[:, cols]
        row = (T_MASS - T_SHARED) * blocks + block
        table[row : row + 1, :] = jnp.where(
            lane_row < count_ref[block], mass_ref[block : block + 1, :], 0.0
        )

    def dense(component):
        return gathered[pl.ds(component, blocks, stride=stride), :]

    def put(index, value):
        if index < T_SHARED:
            shared_ref[index * blocks : (index + 1) * blocks, :] = value
        else:
            start = (index - T_SHARED) * blocks
            table[start : start + blocks, :] = value

    affine = [dense(24 + component) for component in range(9)]
    stress = stress_update([dense(40 + component) for component in range(6)], affine)
    for component in range(6):
        stress_out[component * blocks : (component + 1) * blocks, :] = stress[component]
    live_mass = table[(T_MASS - T_SHARED) * blocks : (T_MASS - T_SHARED + 1) * blocks, :]
    for row_dim in range(3):
        put(T_MV + row_dim, live_mass * dense(16 + row_dim))
        for col_dim in range(3):
            put(
                T_A + 3 * row_dim + col_dim,
                live_mass
                * (
                    affine[3 * row_dim + col_dim]
                    - stress_scale * stress[pair_index[row_dim][col_dim]]
                ),
            )
    spline = []
    for dim in range(3):
        fraction = dense(dim)
        spline.append(
            (
                0.5 * (1.5 - fraction) ** 2,
                0.75 - (fraction - 1.0) ** 2,
                0.5 * (fraction - 0.5) ** 2,
                dense(8 + dim),
                dense(8 + dim) + fraction,
            )
        )
    left, middle, right, offset, position = spline[0]
    for node in range(6):
        shifted = float(node) - offset
        weight = jnp.where(
            shifted == 0.0,
            left,
            jnp.where(shifted == 1.0, middle, jnp.where(shifted == 2.0, right, 0.0)),
        )
        put(T_WX + node, weight)
        put(T_WXD + node, weight * (float(node) - position))
    for index in range(5):
        put(T_LY + index, spline[1][index])
        put(T_LZ + index, spline[2][index])
        y_table[index * blocks : (index + 1) * blocks, :] = spline[1][index]

    lanes = lax.broadcasted_iota(jnp.int32, (8, 32), 1)
    channel = [(lanes >= 8 * index) & (lanes < 8 * index + 8) for index in range(4)]
    rest = jnp.zeros((8, LANES - 32), jnp.float32)
    blank = jnp.zeros((8, LANES), jnp.float32)

    def row_of(block):
        def row(index):
            if index < T_SHARED:
                value = shared_ref[pl.ds(index * blocks + block, 1), :]
            else:
                value = table[pl.ds((index - T_SHARED) * blocks + block, 1), :]
            return jnp.broadcast_to(value, (8, LANES))

        return row

    def block_sums(block):
        row = row_of(block)
        wy, wyd = axis_weights(row, T_LY, T_MY, T_RY, T_OY, T_Y)
        wz, wzd = axis_weights(row, T_LZ, T_MZ, T_RZ, T_OZ, T_Z)
        wx = [row(T_WX + node) for node in range(6)]
        wxd = [row(T_WXD + node) for node in range(6)]
        left_side = jnp.concatenate(
            [
                jnp.concatenate([w * wy for w in wx], axis=0),
                jnp.concatenate([w * wy for w in wxd], axis=0),
                jnp.concatenate([w * wyd for w in wx], axis=0),
            ],
            axis=1,
        )
        value_rows = [
            wz * row(T_MV + dim) + wzd * row(T_A + 3 * dim + 2) for dim in range(3)
        ] + [wz * row(T_MASS)]
        x_rows = [wz * row(T_A + 3 * dim) for dim in range(3)] + [blank]
        y_rows = [wz * row(T_A + 3 * dim + 1) for dim in range(3)] + [blank]
        right_side = jnp.concatenate(
            [jnp.concatenate(r, axis=0) for r in (value_rows, x_rows, y_rows)], axis=1
        )
        left_high, left_low = split(left_side)
        right_high, right_low = split(right_side)

        return lax.dot_general(
            jnp.concatenate([left_high, left_high, left_low], axis=1),
            jnp.concatenate([right_high, right_low, right_high], axis=1),
            (((1,), (1,)), ((), ())),
            preferred_element_type=jnp.float32,
        )

    starts = (0, PITCH - 8, 2 * PITCH - 16, LANES - 24)

    def group_place(step, sums):
        rows = pl.ds(pl.multiple_of(step * 8 * GROUP, 8 * GROUP), 8 * GROUP)
        heights = [4 * (tile_ref[step * GROUP + member] & 7) for member in range(GROUP)]
        for node in range(6):
            mom_rows, mass_rows = [], []
            for member in range(GROUP):
                part = sums[member][8 * node : 8 * node + 8]
                moved = [
                    pltpu.roll(
                        jnp.concatenate([jnp.where(channel[index], part, 0.0), rest], axis=1),
                        starts[index] + heights[member],
                        axis=1,
                    )
                    for index in range(4)
                ]
                mom_rows.append(moved[0] + moved[1] + moved[2])
                mass_rows.append(moved[3])
            for column, values in enumerate((mom_rows, mass_rows)):
                high, low = split(jnp.concatenate(values, axis=0))
                cols = slice(column * LANES, (column + 1) * LANES)
                placed_high[node, rows, cols] = high
                placed_low[node, rows, cols] = low

    def group_sums(step):
        return tuple(block_sums(step * GROUP + member) for member in range(GROUP))

    def group(step, sums):
        following = group_sums(step)
        group_place(step - 1, sums)
        return following

    steps = blocks // GROUP
    group_place(steps - 1, lax.fori_loop(1, steps, group, group_sums(0)))

    spots = 8 * blocks
    spot = lax.broadcasted_iota(jnp.int32, (8, spots), 1)
    owner = spot >> 3
    tiles = jnp.zeros((8, spots), jnp.int32)
    for block in range(blocks):
        tiles = jnp.where(owner == block, tile_ref[block], tiles)
    target = ((tiles >> 7) << 10) + (((tiles >> 3) & 15) << 2) + (spot & 7)
    y_row = lax.broadcasted_iota(jnp.int32, (8, spots), 0)
    chooser = jnp.concatenate(
        [
            jnp.where(target == y_row + (1024 * tile_x + start), 1.0, 0.0)
            for tile_x in range(CX // 4)
            for start in range(0, PY, 8)
        ],
        axis=0,
    ).astype(jnp.bfloat16)
    for node in range(6):
        layers = jnp.dot(
            chooser, placed_high[node], preferred_element_type=jnp.float32
        ) + jnp.dot(chooser, placed_low[node], preferred_element_type=jnp.float32)
        for tile_x in range(CX // 4):
            part = layers[tile_x * PY : (tile_x + 1) * PY]
            x = 4 * tile_x + node
            at = slice(x * PY, (x + 1) * PY)
            if node < 4 or x >= CX:
                mom[at, :] = part[:, :LANES]
                mass[at, :] = part[:, LANES:]
            else:
                mom[at, :] += part[:, :LANES]
                mass[at, :] += part[:, LANES:]

    def copy(src, dst, slot, target):
        return pltpu.make_async_remote_copy(
            src_ref=src,
            dst_ref=dst,
            send_sem=send_sem.at[slot],
            recv_sem=recv_sem.at[slot],
            device_id=target,
            device_id_type=MESH,
        )

    lane = lax.broadcasted_iota(jnp.int32, (PY, LANES), 1)
    in_mom = lane < 3 * PITCH
    in_pitch = lax.rem(lane, PITCH)
    third = PY // 3
    lane3 = lane[:third]
    pl.semaphore_wait(barrier, 14)

    firsts = (0, CX * PY)
    for side in range(2):
        first = firsts[side]
        x_send[side, : 2 * PY, :] = mom[first : first + 2 * PY, :]
        for layer in range(2):
            start = first + layer * PY
            at = 2 * PY + layer * third
            x_send[side, at : at + third, :] = (
                mass[start : start + third, :]
                + pltpu.roll(mass[start + third : start + 2 * third, :], PITCH, axis=1)
                + pltpu.roll(mass[start + 2 * third : start + 3 * third, :], 2 * PITCH, axis=1)
            )
    x_copies = [
        copy(x_send.at[side], x_recv.at[1 - side], 2 + side, x_sides[side]) for side in range(2)
    ]
    for c in x_copies:
        c.start()

    pair = jnp.where(in_mom, in_pitch >> 1, -1)
    far = lax.rem(lane + (LANES - CZ), LANES)
    far_pair = jnp.where(far < 3 * PITCH, lax.rem(far, PITCH) >> 1, -1)
    pair3 = lane3 >> 1
    far_pair3 = far[:third] >> 1
    packed, packed_mass = [None, None], [None, None]
    for x in range(PX):
        at = slice(x * PY, (x + 1) * PY)
        moved = pltpu.roll(mom[at, :], 2 * x, axis=1) if x else mom[at, :]
        for side, which in enumerate((pair, far_pair)):
            packed[side] = jnp.where(which == x, moved, packed[side] if x else 0.0)
        for part in range(3):
            start = PITCH * part
            rows = slice(x * PY + part * third, x * PY + (part + 1) * third)
            moved = mass[rows, :]
            if start + 2 * x:
                moved = pltpu.roll(moved, start + 2 * x, axis=1)
            for side, which in enumerate((pair3, far_pair3)):
                packed_mass[side] = jnp.where(
                    which == start // 2 + x, moved, packed_mass[side] if start + x else 0.0
                )
    for side in range(2):
        z_send[side, :PY, :] = packed[side]
        z_send[side, PY:, :] = packed_mass[side]
    z_copies = [
        copy(z_send.at[side], z_recv.at[1 - side], side, z_sides[side]) for side in range(2)
    ]
    for c in z_copies:
        c.start()

    quad = lax.broadcasted_iota(jnp.int32, (8, LANES), 1) >> 2
    for edge in range(4):
        x0, z_side = CX * (edge // 2), edge % 2
        result = [None, None]
        for tile in range(PY // 8):
            half, start = tile // 8, 16 * (tile % 8)
            rows = z_send[z_side, 8 * tile : 8 * tile + 8, :]
            mass_at = PY + 8 * (tile % 3)
            mass_rows = z_send[z_side, mass_at : mass_at + 8, :]
            for index in range(4):
                if index < 3:
                    source, at = rows, PITCH * index + 2 * x0 + CZ * z_side
                else:
                    source, at = mass_rows, PITCH * (tile // 3) + 2 * x0 + CZ * z_side
                to = start + 4 * index
                moved = pltpu.roll(source, (2 * LANES + to - at) % LANES, axis=1)
                if result[half] is None:
                    result[half] = moved
                else:
                    result[half] = jnp.where(quad == to // 4, moved, result[half])
        xz_send[edge, :8, :] = result[0]
        xz_send[edge, 8:, :] = result[1]
    xz_copies = [
        copy(xz_send.at[edge], xz_recv.at[3 - edge], 6 + edge, xz_sides[edge])
        for edge in range(4)
    ]
    for c in xz_copies:
        c.start()

    for c in z_copies:
        c.wait()
    rim = in_mom & ((in_pitch < 2) | ((in_pitch >= CZ) & (in_pitch < CZ + 2)))
    rim3 = (lane3 < 2) | ((lane3 >= CZ) & (lane3 < CZ + 2))
    from_low = pltpu.roll(z_recv[0], 64, axis=1)
    from_high = z_recv[1]
    for x in range(PX):
        at = slice(x * PY, (x + 1) * PY)
        joined = jnp.where(pair == x, from_high[:PY], from_low[:PY])
        moved = pltpu.roll(joined, (LANES + CZ - 2 * x) % LANES, axis=1)
        mom[at, :] += jnp.where(rim, moved, 0.0)
        for part in range(3):
            start = PITCH * part
            rows = slice(x * PY + part * third, x * PY + (part + 1) * third)
            joined = jnp.where(pair3 == start // 2 + x, from_high[PY:], from_low[PY:])
            moved = pltpu.roll(joined, (2 * LANES + CZ - start - 2 * x) % LANES, axis=1)
            mass[rows, :] += jnp.where(rim3, moved, 0.0)

    y_firsts = (0, CY)
    for side in range(2):
        y0 = y_firsts[side]
        y_send[side, 0:PX, :] = mom[pl.ds(y0, PX, stride=PY), :]
        y_send[side, PX : 2 * PX, :] = mom[pl.ds(y0 + 1, PX, stride=PY), :]
        y_send[side, 2 * PX : 3 * PX, :] = mass[pl.ds(y0, PX, stride=PY), :] + pltpu.roll(
            mass[pl.ds(y0 + 1, PX, stride=PY), :], 64, axis=1
        )
        y_send[side, 3 * PX :, :] = jnp.zeros((2, LANES), jnp.float32)
    y_copies = [
        copy(y_send.at[side], y_recv.at[1 - side], 4 + side, y_sides[side]) for side in range(2)
    ]
    for edge in range(4):
        x0, y0 = CX * (edge // 2), y_firsts[edge % 2]
        for layer in range(2):
            at = (x0 + layer) * PY + y0
            xy_send[edge, 2 * layer : 2 * layer + 2, :] = mom[at : at + 2, :]
            xy_send[edge, 4 + 2 * layer : 6 + 2 * layer, :] = mass[at : at + 2, :]
        y_copies.append(copy(xy_send.at[edge], xy_recv.at[3 - edge], 10 + edge, xy_sides[edge]))
    for c in y_copies:
        c.start()

    width_x = lax.axis_size("gx") * CX
    height_y = lax.axis_size("gy") * CY
    depth_z = lax.axis_size("gz") * CZ
    first_z = lax.axis_index("gz") * CZ
    first_y = lax.axis_index("gy") * CY
    first_x = lax.axis_index("gx") * CX
    z_index = lax.rem(lane - 2 * PITCH - 1 + first_z + depth_z, depth_z)
    is_y = (lane >= PITCH) & (lane < 2 * PITCH)
    is_z = (lane >= 2 * PITCH) & (lane < 3 * PITCH)
    z_floor = is_z & (z_index < 2)
    z_top = is_z & (z_index >= depth_z - 2)
    fall = jnp.where(is_y, time_step * gravity, 0.0)
    row_index = lax.broadcasted_iota(jnp.int32, (PY, LANES), 0)
    y_floor = is_y & (lax.rem(row_index - 1 + first_y + height_y, height_y) < 2)

    def update(mom_values, mass_values, floor, count):
        inverse = 1.0 / (mass_values + mass_floor)
        inverse = jnp.where(
            lane[:count] < PITCH,
            inverse,
            jnp.where(
                is_y[:count],
                pltpu.roll(inverse, PITCH, axis=1),
                pltpu.roll(inverse, 2 * PITCH, axis=1),
            ),
        )
        values = mom_values * inverse - fall[:count]
        values = jnp.where(z_floor[:count] | floor, jnp.maximum(values, 0.0), values)
        return jnp.where(z_top[:count], jnp.minimum(values, 0.0), values)

    def off_outlet(x):
        x_index = lax.rem(first_x + x - 1 + width_x, width_x)
        return (x_index < width_x // 4) | (x_index >= width_x - width_x // 4)

    def update_layer(x):
        at = pl.ds(pl.multiple_of(x * PY, 8), PY)
        velocity_out[at, :] = update(mom[at, :], mass[at, :], y_floor & off_outlet(x), PY)

    def layers(step, carry):
        for member in range(7):
            update_layer(2 + 7 * step + member)
        return carry

    lax.fori_loop(0, 2, layers, 0)

    def right_sides(step, carry):
        for member in range(2):
            block = 2 * step + member
            row = row_of(block)
            wz, wzd = axis_weights(row, T_LZ, T_MZ, T_RZ, T_OZ, T_Z)
            wx = [row(T_WX + node) for node in range(6)]
            wxd = [row(T_WXD + node) for node in range(6)]
            at = pl.ds(pl.multiple_of(48 * block, 16), 48)
            for index, (along_x, along_z) in enumerate(((wx, wz), (wxd, wz), (wx, wzd))):
                high, low = split(jnp.concatenate([w * along_z for w in along_x], axis=0))
                cols = slice(index * LANES, (index + 1) * LANES)
                collect_high[at, cols] = high
                collect_low[at, cols] = low
        return carry

    lax.fori_loop(0, blocks // 2, right_sides, 0)

    for c in xz_copies:
        c.wait()
    lane8 = lane[:8]
    for side in range(2):
        for layer in range(2):
            for tile in range(PY // 8):
                half, start = tile // 8, 16 * (tile % 8)
                mom_value, mass_value = 0.0, 0.0
                for z_side in range(2):
                    source = xz_recv[2 * side + z_side, 8 * half : 8 * half + 8, :]
                    for index in range(4):
                        to = (PITCH * index if index < 3 else 0) + CZ * z_side
                        at = start + 4 * index + 2 * layer
                        moved = pltpu.roll(source, (LANES + to - at) % LANES, axis=1)
                        here = (lane8 >= to) & (lane8 < to + 2)
                        if index < 3:
                            mom_value = jnp.where(here, moved, mom_value)
                        else:
                            mass_value = jnp.where(here, moved, mass_value)
                at = firsts[side] + layer * PY + 8 * tile
                mom[at : at + 8, :] += mom_value
                mass[at : at + 8, :] += mass_value

    for c in x_copies:
        c.wait()
    near3 = lane3 < PITCH
    for side in range(2):
        first = firsts[side]
        mom[first : first + 2 * PY, :] += x_recv[side, : 2 * PY, :]
        for layer in range(2):
            at = 2 * PY + layer * third
            got = x_recv[side, at : at + third, :]
            for part in range(3):
                start = first + layer * PY + part * third
                moved = pltpu.roll(got, (LANES - PITCH * part) % LANES, axis=1)
                mass[start : start + third, :] += jnp.where(near3, moved, 0.0)
    for x in (0, 1, CX, CX + 1):
        update_layer(x)
    front = lane < 64
    for c in y_copies:
        c.wait()
    for side in range(2):
        y0 = y_firsts[side]
        got = y_recv[side, 2 * PX : 3 * PX, :]
        at0 = pl.ds(y0, PX, stride=PY)
        at1 = pl.ds(y0 + 1, PX, stride=PY)
        mom[at0, :] = mom[at0, :] + y_recv[side, 0:PX, :]
        mom[at1, :] = mom[at1, :] + y_recv[side, PX : 2 * PX, :]
        mass[at0, :] = mass[at0, :] + jnp.where(front[:PX], got, 0.0)
        mass[at1, :] = mass[at1, :] + jnp.where(front[:PX], pltpu.roll(got, 64, axis=1), 0.0)
    for edge in range(4):
        x0, y0 = CX * (edge // 2), y_firsts[edge % 2]
        for layer in range(2):
            at = (x0 + layer) * PY + y0
            mom[at : at + 2, :] += xy_recv[edge, 2 * layer : 2 * layer + 2, :]
            mass[at : at + 2, :] += xy_recv[edge, 4 + 2 * layer : 6 + 2 * layer, :]
    x_rows = lax.broadcasted_iota(jnp.int32, (PX, LANES), 0)
    outside = off_outlet(x_rows)
    for y in (0, 1, CY, CY + 1):
        at = pl.ds(y, PX, stride=PY)
        on_floor = lax.rem(first_y + (y - 1 + height_y), height_y) < 2
        velocity_out[at, :] = update(
            mom[at, :], mass[at, :], is_y[:PX] & outside & on_floor, PX
        )


def collect_kernel(
    tile_hbm,
    velocity,
    right_high,
    right_low,
    y_table,
    stress_in,
    new_velocity_ref,
    new_affine_ref,
    new_stress_hbm,
    grid_velocity_hbm,
    tile_ref,
    new_stress_ref,
    grid_velocity_ref,
    partial,
    final,
    copy_sem,
):
    blocks = tile_hbm.shape[0]
    tile_copy = pltpu.make_async_copy(tile_hbm, tile_ref, copy_sem.at[0])
    tile_copy.start()
    for block in range(blocks):
        new_stress_ref[:, block * BLOCK : (block + 1) * BLOCK] = stress_in[
            pl.ds(block, 6, stride=blocks), :
        ]
    stress_copy = pltpu.make_async_copy(new_stress_ref, new_stress_hbm, copy_sem.at[1])
    stress_copy.start()
    def output(step, carry):
        for member in range(4):
            x = 4 * step + member
            turned = jnp.transpose(velocity[pl.ds((x + 1) * PY + 1, CY), :])
            for dim in range(3):
                grid_velocity_ref[dim, x] = turned[PITCH * dim + 1 : PITCH * dim + 1 + CZ]
        return carry

    lax.fori_loop(0, CX // 4, output, 0)
    grid_copy = pltpu.make_async_copy(grid_velocity_ref, grid_velocity_hbm, copy_sem.at[2])
    grid_copy.start()
    tile_copy.wait()

    lanes = lax.broadcasted_iota(jnp.int32, (8, LANES), 1)

    def gather(block):
        tile_x, tile_y, tile_z = tile_coords(tile_ref, block)
        planes = []
        for node in range(6):
            at = pl.ds(pl.multiple_of((4 * tile_x + node) * PY + 4 * tile_y, 4), 8)
            planes.append(velocity[at, :])
        rows = []
        for dim in range(3):
            merged = None
            for node in range(6):
                moved = pltpu.roll(
                    planes[node],
                    LANES + 8 * node - PITCH * dim - 4 * tile_z,
                    axis=1,
                )
                merged = moved if merged is None else jnp.where(lanes < 8 * node, merged, moved)
            rows.append(merged)
        return jnp.concatenate(rows, axis=0)

    def contract(block, left_side):
        left_high, left_low = split(left_side[:, :48])
        at = pl.ds(pl.multiple_of(48 * block, 16), 48)
        both = jnp.dot(
            jnp.concatenate([left_high, left_low], axis=0),
            right_high[at, :],
            preferred_element_type=jnp.float32,
        )
        return (
            both[:24]
            + both[24:]
            + jnp.dot(left_high, right_low[at, :], preferred_element_type=jnp.float32)
        )

    def weigh(block, sums):
        def row(index):
            return jnp.broadcast_to(y_table[pl.ds(index * blocks + block, 1), :], (8, LANES))

        wy, wyd = axis_weights(row, 0, 1, 2, 3, 4)
        for dim in range(3):
            part = sums[8 * dim : 8 * dim + 8]
            terms = (
                (dim, wy * part[:, :128]),
                (3 + 3 * dim, wy * part[:, 128:256]),
                (4 + 3 * dim, wyd * part[:, :128]),
                (5 + 3 * dim, wy * part[:, 256:]),
            )
            for component, value in terms:
                at = pl.ds(pl.multiple_of(component * 8 * blocks + 8 * block, 8), 8)
                partial[at, :] = value

    def of_group(function, step, *values):
        return tuple(
            function(step * GROUP + member, *(value[member] for value in values))
            for member in range(GROUP)
        )

    def group(step, carry):
        left_sides, sums = carry
        following = of_group(gather, step + 2)
        products = of_group(contract, step + 1, left_sides)
        of_group(weigh, step, sums)
        return following, products

    steps = blocks // GROUP
    carry = of_group(gather, 1), of_group(contract, 0, of_group(gather, 0))
    left_sides, sums = lax.fori_loop(0, steps - 2, group, carry)
    of_group(weigh, steps - 2, sums)
    of_group(weigh, steps - 1, of_group(contract, steps - 1, left_sides))
    for component in range(12):
        total = partial[pl.ds(component * 8 * blocks, blocks, stride=8), :]
        for node in range(1, 6):
            total = total + partial[pl.ds(component * 8 * blocks + node, blocks, stride=8), :]
        if component >= 3:
            total = 4.0 * total
        final[component * blocks : (component + 1) * blocks, :] = total
    for block in range(blocks):
        cols = slice(block * BLOCK, (block + 1) * BLOCK)
        new_velocity_ref[:, cols] = final[pl.ds(block, 3, stride=blocks), :]
        new_affine_ref[:, cols] = final[pl.ds(3 * blocks + block, 9, stride=blocks), :]
    stress_copy.wait()
    grid_copy.wait()


def shards(
    point_frac,
    cell_offset,
    point_velocity,
    point_affine,
    point_stress,
    point_mass,
    block_tile,
    block_count,
):
    blocks = block_tile.shape[0]
    points = blocks * BLOCK
    vmem = pl.BlockSpec(memory_space=pltpu.VMEM)
    hbm = pl.BlockSpec(memory_space=pltpu.HBM)
    f32 = jnp.float32
    grid_shape = jax.ShapeDtypeStruct((ROWS, LANES), f32)
    face = PY + PY // 3
    arguments = [
        pltpu.with_memory_space_constraint(value, pltpu.HBM)
        for value in (
            block_tile,
            block_count,
            point_frac,
            cell_offset,
            point_velocity,
            point_affine,
            point_stress,
            point_mass.reshape(blocks, BLOCK),
        )
    ]
    right_shape = jax.ShapeDtypeStruct((48 * blocks, 3 * LANES), jnp.bfloat16)
    velocity, right_high, right_low, y_table, stress = pl.pallas_call(
        deposit_kernel,
        name="deposit",
        out_shape=(
            grid_shape,
            right_shape,
            right_shape,
            jax.ShapeDtypeStruct((5 * blocks, LANES), f32),
            jax.ShapeDtypeStruct((6 * blocks, LANES), f32),
        ),
        in_specs=[hbm] * 8,
        out_specs=(vmem,) * 5,
        scratch_shapes=[
            pltpu.VMEM((ROWS, LANES), f32),
            pltpu.VMEM((ROWS, LANES), f32),
            pltpu.VMEM((T_SHARED * blocks, LANES), f32),
            pltpu.SMEM((blocks,), jnp.int32),
            pltpu.SMEM((blocks,), jnp.int32),
            pltpu.VMEM((3, points), f32),
            pltpu.VMEM((3, points), jnp.int32),
            pltpu.VMEM((3, points), f32),
            pltpu.VMEM((9, points), f32),
            pltpu.VMEM((6, points), f32),
            pltpu.VMEM((blocks, BLOCK), f32),
            pltpu.VMEM((48 * blocks, LANES), f32),
            pltpu.VMEM(((T_ALL - T_SHARED) * blocks, LANES), f32),
            pltpu.VMEM((6, 8 * blocks, 2 * LANES), jnp.bfloat16),
            pltpu.VMEM((6, 8 * blocks, 2 * LANES), jnp.bfloat16),
            pltpu.VMEM((2, face, LANES), f32),
            pltpu.VMEM((2, face, LANES), f32),
            pltpu.VMEM((2, 2 * face, LANES), f32),
            pltpu.VMEM((2, 2 * face, LANES), f32),
            pltpu.VMEM((4, 16, LANES), f32),
            pltpu.VMEM((4, 16, LANES), f32),
            pltpu.VMEM((2, 3 * PX + 2, LANES), f32),
            pltpu.VMEM((2, 3 * PX + 2, LANES), f32),
            pltpu.VMEM((4, 8, LANES), f32),
            pltpu.VMEM((4, 8, LANES), f32),
            pltpu.SemaphoreType.DMA((8,)),
            pltpu.SemaphoreType.DMA((14,)),
            pltpu.SemaphoreType.DMA((14,)),
        ],
        compiler_params=pltpu.CompilerParams(
            collective_id=0, has_side_effects=True, vmem_limit_bytes=VMEM_LIMIT
        ),
    )(*arguments)
    new_velocity, new_affine, new_stress, grid_velocity = pl.pallas_call(
        collect_kernel,
        name="collect",
        out_shape=(
            jax.ShapeDtypeStruct((3, points), f32),
            jax.ShapeDtypeStruct((9, points), f32),
            jax.ShapeDtypeStruct((6, points), f32),
            jax.ShapeDtypeStruct((3, CX, CZ, CY), f32),
        ),
        in_specs=[hbm] + [vmem] * 5,
        out_specs=(vmem, vmem, hbm, hbm),
        scratch_shapes=[
            pltpu.SMEM((blocks,), jnp.int32),
            pltpu.VMEM((6, points), f32),
            pltpu.VMEM((3, CX, CZ, CY), f32),
            pltpu.VMEM((12 * 8 * blocks, LANES), f32),
            pltpu.VMEM((12 * blocks, LANES), f32),
            pltpu.SemaphoreType.DMA((3,)),
        ],
        compiler_params=pltpu.CompilerParams(vmem_limit_bytes=VMEM_LIMIT),
    )(arguments[0], velocity, right_high, right_low, y_table, stress)
    return (new_velocity, new_affine, new_stress, jnp.swapaxes(grid_velocity, 2, 3))


def solution(mesh):
    points = P(None, ("gx", "gy", "gz"))
    flat = P(("gx", "gy", "gz"))
    return jax.shard_map(
        shards,
        mesh=mesh,
        in_specs=(points,) * 5 + (flat,) * 3,
        out_specs=(points, points, points, P(None, "gx", "gy", "gz")),
        check_vma=False,
    )
```

```python
import jax
import jax.numpy as jnp
from jax import lax
from jax.experimental import pallas as pl
from jax.experimental.pallas import tpu as pltpu
from jax.sharding import PartitionSpec as P

CX = 16
CY = 64
CZ = 32
BLOCK = 128

time_step = 0.1
gravity = 1.0
shear_modulus = 2.0
bulk_modulus = 4.0
friction_static = 0.38
friction_limit = 0.64
inertial_ref = 0.28
grain_size = 0.5
grain_density = 1.0
pressure_floor = 0.5
shear_floor = 0.5
mass_floor = 0.05
stress_scale = 0.4
pair_index = ((0, 5, 4), (5, 1, 3), (4, 3, 2))
component_pairs = ((0, 0), (1, 1), (2, 2), (1, 2), (0, 2), (0, 1))

PX = CX + 2
PY = 72
PITCH = 40
LANES = 128
ROWS = PX * PY
GROUP = 16
VMEM_LIMIT = 16 * 1024 * 1024
MESH = pl.DeviceIdType.MESH

T_WX, T_WXD = 0, 6
T_LY, T_MY, T_RY, T_OY, T_Y = 12, 13, 14, 15, 16
T_LZ, T_MZ, T_RZ, T_OZ, T_Z = 17, 18, 19, 20, 21
T_SHARED = 22
T_MASS, T_MV, T_A = 22, 23, 26
T_ALL = 35


def stress_update(stress, affine):
    strain_rate = [
        [
            0.5 * (affine[3 * row_dim + col_dim] + affine[3 * col_dim + row_dim])
            for col_dim in range(3)
        ]
        for row_dim in range(3)
    ]
    volume_rate = strain_rate[0][0] + strain_rate[1][1] + strain_rate[2][2]
    deviator = [
        [
            strain_rate[row_dim][col_dim] - (volume_rate / 3.0 if row_dim == col_dim else 0.0)
            for col_dim in range(3)
        ]
        for row_dim in range(3)
    ]
    trial_stress = []
    for component in range(6):
        row_dim, col_dim = component_pairs[component]
        value = stress[component] + time_step * 2.0 * shear_modulus * deviator[row_dim][col_dim]
        if component < 3:
            value = value + time_step * bulk_modulus * volume_rate
        trial_stress.append(value)
    pressure = -(trial_stress[0] + trial_stress[1] + trial_stress[2]) / 3.0
    shear_part = [trial_stress[component] + pressure for component in range(3)] + trial_stress[3:]
    shear_stress = jnp.sqrt(
        0.5 * (shear_part[0] ** 2 + shear_part[1] ** 2 + shear_part[2] ** 2)
        + shear_part[3] ** 2
        + shear_part[4] ** 2
        + shear_part[5] ** 2
    )
    shear_rate = jnp.sqrt(
        2.0
        * (
            deviator[0][0] ** 2
            + deviator[1][1] ** 2
            + deviator[2][2] ** 2
            + 2.0 * (deviator[1][2] ** 2 + deviator[0][2] ** 2 + deviator[0][1] ** 2)
        )
    )
    inertial = (
        shear_rate * grain_size / jnp.sqrt(jnp.maximum(pressure, pressure_floor) / grain_density)
    )
    friction = friction_static + (friction_limit - friction_static) * inertial / (
        inertial_ref + inertial
    )
    support = jnp.maximum(pressure, 0.0)
    factor = jnp.minimum(1.0, friction * support / jnp.maximum(shear_stress, shear_floor))
    return [shear_part[component] * factor - support for component in range(3)] + [
        shear_part[component] * factor for component in range(3, 6)
    ]


def split(values):
    high = values.astype(jnp.bfloat16)
    low = (values - high.astype(jnp.float32)).astype(jnp.bfloat16)
    return high, low


def tile_coords(tile_ref, block):
    tile = tile_ref[block]
    return tile >> 7, (tile >> 3) & 15, tile & 7


def axis_weights(row, left, middle, right, offset, position):
    index = lax.broadcasted_iota(jnp.int32, (8, LANES), 0).astype(jnp.float32)
    shifted = index - row(offset)
    weight = jnp.where(
        shifted == 0.0,
        row(left),
        jnp.where(shifted == 1.0, row(middle), jnp.where(shifted == 2.0, row(right), 0.0)),
    )
    return weight, weight * (index - row(position))


def deposit_kernel(
    tile_hbm,
    count_hbm,
    frac_hbm,
    offset_hbm,
    velocity_hbm,
    affine_hbm,
    stress_hbm,
    mass_hbm,
    velocity_out,
    collect_high,
    collect_low,
    y_table,
    stress_out,
    mom,
    mass,
    shared_ref,
    tile_ref,
    count_ref,
    frac_ref,
    offset_ref,
    velocity_ref,
    affine_ref,
    stress_ref,
    mass_ref,
    gathered,
    table,
    placed_high,
    placed_low,
    z_send,
    z_recv,
    x_send,
    x_recv,
    xz_send,
    xz_recv,
    y_send,
    y_recv,
    xy_send,
    xy_recv,
    load_sem,
    send_sem,
    recv_sem,
):
    axes = ("gx", "gy", "gz")

    def device(dx, dy, dz):
        place = []
        for axis, step in zip(axes, (dx, dy, dz)):
            size = lax.axis_size(axis)
            moved = lax.axis_index(axis)
            if step and size & (size - 1) == 0:
                moved = (moved + size + step) & (size - 1)
            elif step:
                moved = lax.rem(moved + size + step, size)
            place.append(moved)
        return tuple(place)

    loads = [
        pltpu.make_async_copy(source, target, load_sem.at[index])
        for index, (source, target) in enumerate(
            (
                (frac_hbm, frac_ref),
                (offset_hbm, offset_ref),
                (velocity_hbm, velocity_ref),
                (affine_hbm, affine_ref),
                (stress_hbm, stress_ref),
                (mass_hbm, mass_ref),
                (count_hbm, count_ref),
                (tile_hbm, tile_ref),
            )
        )
    ]
    for load in loads:
        load.start()
    z_sides = [device(0, 0, -1), device(0, 0, 1)]
    x_sides = [device(-1, 0, 0), device(1, 0, 0)]
    y_sides = [device(0, -1, 0), device(0, 1, 0)]
    xz_sides = [device(dx, 0, dz) for dx in (-1, 1) for dz in (-1, 1)]
    xy_sides = [device(dx, dy, 0) for dx in (-1, 1) for dy in (-1, 1)]
    barrier = pltpu.get_barrier_semaphore()
    for target in z_sides + x_sides + xz_sides + y_sides + xy_sides:
        pl.semaphore_signal(barrier, inc=1, device_id=target, device_id_type=MESH)

    blocks = mass_ref.shape[0]
    lane_row = lax.broadcasted_iota(jnp.int32, (1, LANES), 1)
    stride = 48
    for load in loads:
        load.wait()
    for block in range(blocks):
        cols = slice(block * BLOCK, (block + 1) * BLOCK)
        at = block * stride
        gathered[at : at + 3, :] = frac_ref[:, cols]
        gathered[at + 8 : at + 11, :] = offset_ref[:, cols].astype(jnp.float32)
        gathered[at + 16 : at + 19, :] = velocity_ref[:, cols]
        gathered[at + 24 : at + 33, :] = affine_ref[:, cols]
        gathered[at + 40 : at + 46, :] = stress_ref[:, cols]
        row = (T_MASS - T_SHARED) * blocks + block
        table[row : row + 1, :] = jnp.where(
            lane_row < count_ref[block], mass_ref[block : block + 1, :], 0.0
        )

    def dense(component):
        return gathered[pl.ds(component, blocks, stride=stride), :]

    def put(index, value):
        if index < T_SHARED:
            shared_ref[index * blocks : (index + 1) * blocks, :] = value
        else:
            start = (index - T_SHARED) * blocks
            table[start : start + blocks, :] = value

    affine = [dense(24 + component) for component in range(9)]
    stress = stress_update([dense(40 + component) for component in range(6)], affine)
    for component in range(6):
        stress_out[component * blocks : (component + 1) * blocks, :] = stress[component]
    live_mass = table[(T_MASS - T_SHARED) * blocks : (T_MASS - T_SHARED + 1) * blocks, :]
    for row_dim in range(3):
        put(T_MV + row_dim, live_mass * dense(16 + row_dim))
        for col_dim in range(3):
            put(
                T_A + 3 * row_dim + col_dim,
                live_mass
                * (
                    affine[3 * row_dim + col_dim]
                    - stress_scale * stress[pair_index[row_dim][col_dim]]
                ),
            )
    spline = []
    for dim in range(3):
        fraction = dense(dim)
        spline.append(
            (
                0.5 * (1.5 - fraction) ** 2,
                0.75 - (fraction - 1.0) ** 2,
                0.5 * (fraction - 0.5) ** 2,
                dense(8 + dim),
                dense(8 + dim) + fraction,
            )
        )
    left, middle, right, offset, position = spline[0]
    for node in range(6):
        shifted = float(node) - offset
        weight = jnp.where(
            shifted == 0.0,
            left,
            jnp.where(shifted == 1.0, middle, jnp.where(shifted == 2.0, right, 0.0)),
        )
        put(T_WX + node, weight)
        put(T_WXD + node, weight * (float(node) - position))
    for index in range(5):
        put(T_LY + index, spline[1][index])
        put(T_LZ + index, spline[2][index])
        y_table[index * blocks : (index + 1) * blocks, :] = spline[1][index]

    lanes = lax.broadcasted_iota(jnp.int32, (8, 32), 1)
    channel = [(lanes >= 8 * index) & (lanes < 8 * index + 8) for index in range(4)]
    rest = jnp.zeros((8, LANES - 32), jnp.float32)
    blank = jnp.zeros((8, LANES), jnp.float32)

    def row_of(block):
        def row(index):
            if index < T_SHARED:
                value = shared_ref[pl.ds(index * blocks + block, 1), :]
            else:
                value = table[pl.ds((index - T_SHARED) * blocks + block, 1), :]
            return jnp.broadcast_to(value, (8, LANES))

        return row

    def block_sums(block):
        row = row_of(block)
        wy, wyd = axis_weights(row, T_LY, T_MY, T_RY, T_OY, T_Y)
        wz, wzd = axis_weights(row, T_LZ, T_MZ, T_RZ, T_OZ, T_Z)
        wx = [row(T_WX + node) for node in range(6)]
        wxd = [row(T_WXD + node) for node in range(6)]
        left_side = jnp.concatenate(
            [
                jnp.concatenate([w * wy for w in wx], axis=0),
                jnp.concatenate([w * wy for w in wxd], axis=0),
                jnp.concatenate([w * wyd for w in wx], axis=0),
            ],
            axis=1,
        )
        value_rows = [
            wz * row(T_MV + dim) + wzd * row(T_A + 3 * dim + 2) for dim in range(3)
        ] + [wz * row(T_MASS)]
        x_rows = [wz * row(T_A + 3 * dim) for dim in range(3)] + [blank]
        y_rows = [wz * row(T_A + 3 * dim + 1) for dim in range(3)] + [blank]
        right_side = jnp.concatenate(
            [jnp.concatenate(r, axis=0) for r in (value_rows, x_rows, y_rows)], axis=1
        )
        left_high, left_low = split(left_side)
        right_high, right_low = split(right_side)

        return lax.dot_general(
            jnp.concatenate([left_high, left_high, left_low], axis=1),
            jnp.concatenate([right_high, right_low, right_high], axis=1),
            (((1,), (1,)), ((), ())),
            preferred_element_type=jnp.float32,
        )

    starts = (0, PITCH - 8, 2 * PITCH - 16, LANES - 24)

    def group_place(step, sums):
        rows = pl.ds(pl.multiple_of(step * 8 * GROUP, 8 * GROUP), 8 * GROUP)
        heights = [4 * (tile_ref[step * GROUP + member] & 7) for member in range(GROUP)]
        for node in range(6):
            mom_rows, mass_rows = [], []
            for member in range(GROUP):
                part = sums[member][8 * node : 8 * node + 8]
                moved = [
                    pltpu.roll(
                        jnp.concatenate([jnp.where(channel[index], part, 0.0), rest], axis=1),
                        starts[index] + heights[member],
                        axis=1,
                    )
                    for index in range(4)
                ]
                mom_rows.append(moved[0] + moved[1] + moved[2])
                mass_rows.append(moved[3])
            for column, values in enumerate((mom_rows, mass_rows)):
                high, low = split(jnp.concatenate(values, axis=0))
                cols = slice(column * LANES, (column + 1) * LANES)
                placed_high[node, rows, cols] = high
                placed_low[node, rows, cols] = low

    def group_sums(step):
        return tuple(block_sums(step * GROUP + member) for member in range(GROUP))

    def group(step, sums):
        following = group_sums(step)
        group_place(step - 1, sums)
        return following

    steps = blocks // GROUP
    group_place(steps - 1, lax.fori_loop(1, steps, group, group_sums(0)))

    spots = 8 * blocks
    spot = lax.broadcasted_iota(jnp.int32, (8, spots), 1)
    owner = spot >> 3
    tiles = jnp.zeros((8, spots), jnp.int32)
    for block in range(blocks):
        tiles = jnp.where(owner == block, tile_ref[block], tiles)
    target = ((tiles >> 7) << 10) + (((tiles >> 3) & 15) << 2) + (spot & 7)
    y_row = lax.broadcasted_iota(jnp.int32, (8, spots), 0)
    chooser = jnp.concatenate(
        [
            jnp.where(target == y_row + (1024 * tile_x + start), 1.0, 0.0)
            for tile_x in range(CX // 4)
            for start in range(0, PY, 8)
        ],
        axis=0,
    ).astype(jnp.bfloat16)
    for node in range(6):
        layers = jnp.dot(
            chooser, placed_high[node], preferred_element_type=jnp.float32
        ) + jnp.dot(chooser, placed_low[node], preferred_element_type=jnp.float32)
        for tile_x in range(CX // 4):
            part = layers[tile_x * PY : (tile_x + 1) * PY]
            x = 4 * tile_x + node
            at = slice(x * PY, (x + 1) * PY)
            if node < 4 or x >= CX:
                mom[at, :] = part[:, :LANES]
                mass[at, :] = part[:, LANES:]
            else:
                mom[at, :] += part[:, :LANES]
                mass[at, :] += part[:, LANES:]

    def copy(src, dst, slot, target):
        return pltpu.make_async_remote_copy(
            src_ref=src,
            dst_ref=dst,
            send_sem=send_sem.at[slot],
            recv_sem=recv_sem.at[slot],
            device_id=target,
            device_id_type=MESH,
        )

    lane = lax.broadcasted_iota(jnp.int32, (PY, LANES), 1)
    in_mom = lane < 3 * PITCH
    in_pitch = lax.rem(lane, PITCH)
    third = PY // 3
    lane3 = lane[:third]
    pl.semaphore_wait(barrier, 14)

    firsts = (0, CX * PY)
    for side in range(2):
        first = firsts[side]
        x_send[side, : 2 * PY, :] = mom[first : first + 2 * PY, :]
        for layer in range(2):
            start = first + layer * PY
            at = 2 * PY + layer * third
            x_send[side, at : at + third, :] = (
                mass[start : start + third, :]
                + pltpu.roll(mass[start + third : start + 2 * third, :], PITCH, axis=1)
                + pltpu.roll(mass[start + 2 * third : start + 3 * third, :], 2 * PITCH, axis=1)
            )
    x_copies = [
        copy(x_send.at[side], x_recv.at[1 - side], 2 + side, x_sides[side]) for side in range(2)
    ]
    for c in x_copies:
        c.start()

    pair = jnp.where(in_mom, in_pitch >> 1, -1)
    far = lax.rem(lane + (LANES - CZ), LANES)
    far_pair = jnp.where(far < 3 * PITCH, lax.rem(far, PITCH) >> 1, -1)
    pair3 = lane3 >> 1
    far_pair3 = far[:third] >> 1
    packed, packed_mass = [None, None], [None, None]
    for x in range(PX):
        at = slice(x * PY, (x + 1) * PY)
        moved = pltpu.roll(mom[at, :], 2 * x, axis=1) if x else mom[at, :]
        for side, which in enumerate((pair, far_pair)):
            packed[side] = jnp.where(which == x, moved, packed[side] if x else 0.0)
        for part in range(3):
            start = PITCH * part
            rows = slice(x * PY + part * third, x * PY + (part + 1) * third)
            moved = mass[rows, :]
            if start + 2 * x:
                moved = pltpu.roll(moved, start + 2 * x, axis=1)
            for side, which in enumerate((pair3, far_pair3)):
                packed_mass[side] = jnp.where(
                    which == start // 2 + x, moved, packed_mass[side] if start + x else 0.0
                )
    for side in range(2):
        z_send[side, :PY, :] = packed[side]
        z_send[side, PY:, :] = packed_mass[side]
    z_copies = [
        copy(z_send.at[side], z_recv.at[1 - side], side, z_sides[side]) for side in range(2)
    ]
    for c in z_copies:
        c.start()

    quad = lax.broadcasted_iota(jnp.int32, (8, LANES), 1) >> 2
    for edge in range(4):
        x0, z_side = CX * (edge // 2), edge % 2
        result = [None, None]
        for tile in range(PY // 8):
            half, start = tile // 8, 16 * (tile % 8)
            rows = z_send[z_side, 8 * tile : 8 * tile + 8, :]
            mass_at = PY + 8 * (tile % 3)
            mass_rows = z_send[z_side, mass_at : mass_at + 8, :]
            for index in range(4):
                if index < 3:
                    source, at = rows, PITCH * index + 2 * x0 + CZ * z_side
                else:
                    source, at = mass_rows, PITCH * (tile // 3) + 2 * x0 + CZ * z_side
                to = start + 4 * index
                moved = pltpu.roll(source, (2 * LANES + to - at) % LANES, axis=1)
                if result[half] is None:
                    result[half] = moved
                else:
                    result[half] = jnp.where(quad == to // 4, moved, result[half])
        xz_send[edge, :8, :] = result[0]
        xz_send[edge, 8:, :] = result[1]
    xz_copies = [
        copy(xz_send.at[edge], xz_recv.at[3 - edge], 6 + edge, xz_sides[edge])
        for edge in range(4)
    ]
    for c in xz_copies:
        c.start()

    for c in z_copies:
        c.wait()
    rim = in_mom & ((in_pitch < 2) | ((in_pitch >= CZ) & (in_pitch < CZ + 2)))
    rim3 = (lane3 < 2) | ((lane3 >= CZ) & (lane3 < CZ + 2))
    from_low = pltpu.roll(z_recv[0], 64, axis=1)
    from_high = z_recv[1]
    for x in range(PX):
        at = slice(x * PY, (x + 1) * PY)
        joined = jnp.where(pair == x, from_high[:PY], from_low[:PY])
        moved = pltpu.roll(joined, (LANES + CZ - 2 * x) % LANES, axis=1)
        mom[at, :] += jnp.where(rim, moved, 0.0)
        for part in range(3):
            start = PITCH * part
            rows = slice(x * PY + part * third, x * PY + (part + 1) * third)
            joined = jnp.where(pair3 == start // 2 + x, from_high[PY:], from_low[PY:])
            moved = pltpu.roll(joined, (2 * LANES + CZ - start - 2 * x) % LANES, axis=1)
            mass[rows, :] += jnp.where(rim3, moved, 0.0)

    y_firsts = (0, CY)
    for side in range(2):
        y0 = y_firsts[side]
        y_send[side, 0:PX, :] = mom[pl.ds(y0, PX, stride=PY), :]
        y_send[side, PX : 2 * PX, :] = mom[pl.ds(y0 + 1, PX, stride=PY), :]
        y_send[side, 2 * PX : 3 * PX, :] = mass[pl.ds(y0, PX, stride=PY), :] + pltpu.roll(
            mass[pl.ds(y0 + 1, PX, stride=PY), :], 64, axis=1
        )
        y_send[side, 3 * PX :, :] = jnp.zeros((2, LANES), jnp.float32)
    y_copies = [
        copy(y_send.at[side], y_recv.at[1 - side], 4 + side, y_sides[side]) for side in range(2)
    ]
    for edge in range(4):
        x0, y0 = CX * (edge // 2), y_firsts[edge % 2]
        for layer in range(2):
            at = (x0 + layer) * PY + y0
            xy_send[edge, 2 * layer : 2 * layer + 2, :] = mom[at : at + 2, :]
            xy_send[edge, 4 + 2 * layer : 6 + 2 * layer, :] = mass[at : at + 2, :]
        y_copies.append(copy(xy_send.at[edge], xy_recv.at[3 - edge], 10 + edge, xy_sides[edge]))
    for c in y_copies:
        c.start()

    width_x = lax.axis_size("gx") * CX
    height_y = lax.axis_size("gy") * CY
    depth_z = lax.axis_size("gz") * CZ
    first_z = lax.axis_index("gz") * CZ
    first_y = lax.axis_index("gy") * CY
    first_x = lax.axis_index("gx") * CX
    z_index = lax.rem(lane - 2 * PITCH - 1 + first_z + depth_z, depth_z)
    is_y = (lane >= PITCH) & (lane < 2 * PITCH)
    is_z = (lane >= 2 * PITCH) & (lane < 3 * PITCH)
    z_floor = is_z & (z_index < 2)
    z_top = is_z & (z_index >= depth_z - 2)
    fall = jnp.where(is_y, time_step * gravity, 0.0)
    row_index = lax.broadcasted_iota(jnp.int32, (PY, LANES), 0)
    y_floor = is_y & (lax.rem(row_index - 1 + first_y + height_y, height_y) < 2)

    def update(mom_values, mass_values, floor, count):
        inverse = 1.0 / (mass_values + mass_floor)
        inverse = jnp.where(
            lane[:count] < PITCH,
            inverse,
            jnp.where(
                is_y[:count],
                pltpu.roll(inverse, PITCH, axis=1),
                pltpu.roll(inverse, 2 * PITCH, axis=1),
            ),
        )
        values = mom_values * inverse - fall[:count]
        values = jnp.where(z_floor[:count] | floor, jnp.maximum(values, 0.0), values)
        return jnp.where(z_top[:count], jnp.minimum(values, 0.0), values)

    def off_outlet(x):
        x_index = lax.rem(first_x + x - 1 + width_x, width_x)
        return (x_index < width_x // 4) | (x_index >= width_x - width_x // 4)

    def update_layer(x):
        at = pl.ds(pl.multiple_of(x * PY, 8), PY)
        velocity_out[at, :] = update(mom[at, :], mass[at, :], y_floor & off_outlet(x), PY)

    def layers(step, carry):
        for member in range(7):
            update_layer(2 + 7 * step + member)
        return carry

    lax.fori_loop(0, 2, layers, 0)

    def right_sides(step, carry):
        for member in range(2):
            block = 2 * step + member
            row = row_of(block)
            wz, wzd = axis_weights(row, T_LZ, T_MZ, T_RZ, T_OZ, T_Z)
            wx = [row(T_WX + node) for node in range(6)]
            wxd = [row(T_WXD + node) for node in range(6)]
            at = pl.ds(pl.multiple_of(48 * block, 16), 48)
            for index, (along_x, along_z) in enumerate(((wx, wz), (wxd, wz), (wx, wzd))):
                high, low = split(jnp.concatenate([w * along_z for w in along_x], axis=0))
                cols = slice(index * LANES, (index + 1) * LANES)
                collect_high[at, cols] = high
                collect_low[at, cols] = low
        return carry

    lax.fori_loop(0, blocks // 2, right_sides, 0)

    for c in xz_copies:
        c.wait()
    lane8 = lane[:8]
    for side in range(2):
        for layer in range(2):
            for tile in range(PY // 8):
                half, start = tile // 8, 16 * (tile % 8)
                mom_value, mass_value = 0.0, 0.0
                for z_side in range(2):
                    source = xz_recv[2 * side + z_side, 8 * half : 8 * half + 8, :]
                    for index in range(4):
                        to = (PITCH * index if index < 3 else 0) + CZ * z_side
                        at = start + 4 * index + 2 * layer
                        moved = pltpu.roll(source, (LANES + to - at) % LANES, axis=1)
                        here = (lane8 >= to) & (lane8 < to + 2)
                        if index < 3:
                            mom_value = jnp.where(here, moved, mom_value)
                        else:
                            mass_value = jnp.where(here, moved, mass_value)
                at = firsts[side] + layer * PY + 8 * tile
                mom[at : at + 8, :] += mom_value
                mass[at : at + 8, :] += mass_value

    for c in x_copies:
        c.wait()
    near3 = lane3 < PITCH
    for side in range(2):
        first = firsts[side]
        mom[first : first + 2 * PY, :] += x_recv[side, : 2 * PY, :]
        for layer in range(2):
            at = 2 * PY + layer * third
            got = x_recv[side, at : at + third, :]
            for part in range(3):
                start = first + layer * PY + part * third
                moved = pltpu.roll(got, (LANES - PITCH * part) % LANES, axis=1)
                mass[start : start + third, :] += jnp.where(near3, moved, 0.0)
    for x in (0, 1, CX, CX + 1):
        update_layer(x)
    front = lane < 64
    for c in y_copies:
        c.wait()
    for side in range(2):
        y0 = y_firsts[side]
        got = y_recv[side, 2 * PX : 3 * PX, :]
        at0 = pl.ds(y0, PX, stride=PY)
        at1 = pl.ds(y0 + 1, PX, stride=PY)
        mom[at0, :] = mom[at0, :] + y_recv[side, 0:PX, :]
        mom[at1, :] = mom[at1, :] + y_recv[side, PX : 2 * PX, :]
        mass[at0, :] = mass[at0, :] + jnp.where(front[:PX], got, 0.0)
        mass[at1, :] = mass[at1, :] + jnp.where(front[:PX], pltpu.roll(got, 64, axis=1), 0.0)
    for edge in range(4):
        x0, y0 = CX * (edge // 2), y_firsts[edge % 2]
        for layer in range(2):
            at = (x0 + layer) * PY + y0
            mom[at : at + 2, :] += xy_recv[edge, 2 * layer : 2 * layer + 2, :]
            mass[at : at + 2, :] += xy_recv[edge, 4 + 2 * layer : 6 + 2 * layer, :]
    x_rows = lax.broadcasted_iota(jnp.int32, (PX, LANES), 0)
    outside = off_outlet(x_rows)
    for y in (0, 1, CY, CY + 1):
        at = pl.ds(y, PX, stride=PY)
        on_floor = lax.rem(first_y + (y - 1 + height_y), height_y) < 2
        velocity_out[at, :] = update(
            mom[at, :], mass[at, :], is_y[:PX] & outside & on_floor, PX
        )


def collect_kernel(
    tile_hbm,
    velocity,
    right_high,
    right_low,
    y_table,
    stress_in,
    new_velocity_ref,
    new_affine_ref,
    new_stress_hbm,
    grid_velocity_hbm,
    tile_ref,
    new_stress_ref,
    grid_velocity_ref,
    partial,
    final,
    copy_sem,
):
    blocks = tile_hbm.shape[0]
    tile_copy = pltpu.make_async_copy(tile_hbm, tile_ref, copy_sem.at[0])
    tile_copy.start()
    for block in range(blocks):
        new_stress_ref[:, block * BLOCK : (block + 1) * BLOCK] = stress_in[
            pl.ds(block, 6, stride=blocks), :
        ]
    stress_copy = pltpu.make_async_copy(new_stress_ref, new_stress_hbm, copy_sem.at[1])
    stress_copy.start()
    def output(step, carry):
        for member in range(4):
            x = 4 * step + member
            turned = jnp.transpose(velocity[pl.ds((x + 1) * PY + 1, CY), :])
            for dim in range(3):
                grid_velocity_ref[dim, x] = turned[PITCH * dim + 1 : PITCH * dim + 1 + CZ]
        return carry

    lax.fori_loop(0, CX // 4, output, 0)
    grid_copy = pltpu.make_async_copy(grid_velocity_ref, grid_velocity_hbm, copy_sem.at[2])
    grid_copy.start()
    tile_copy.wait()

    lanes = lax.broadcasted_iota(jnp.int32, (8, LANES), 1)

    def gather(block):
        tile_x, tile_y, tile_z = tile_coords(tile_ref, block)
        planes = []
        for node in range(6):
            at = pl.ds(pl.multiple_of((4 * tile_x + node) * PY + 4 * tile_y, 4), 8)
            planes.append(velocity[at, :])
        rows = []
        for dim in range(3):
            merged = None
            for node in range(6):
                moved = pltpu.roll(
                    planes[node],
                    LANES + 8 * node - PITCH * dim - 4 * tile_z,
                    axis=1,
                )
                merged = moved if merged is None else jnp.where(lanes < 8 * node, merged, moved)
            rows.append(merged)
        return jnp.concatenate(rows, axis=0)

    def contract(block, left_side):
        left_high, left_low = split(left_side[:, :48])
        at = pl.ds(pl.multiple_of(48 * block, 16), 48)
        both = jnp.dot(
            jnp.concatenate([left_high, left_low], axis=0),
            right_high[at, :],
            preferred_element_type=jnp.float32,
        )
        return (
            both[:24]
            + both[24:]
            + jnp.dot(left_high, right_low[at, :], preferred_element_type=jnp.float32)
        )

    def weigh(block, sums):
        def row(index):
            return jnp.broadcast_to(y_table[pl.ds(index * blocks + block, 1), :], (8, LANES))

        wy, wyd = axis_weights(row, 0, 1, 2, 3, 4)
        for dim in range(3):
            part = sums[8 * dim : 8 * dim + 8]
            terms = (
                (dim, wy * part[:, :128]),
                (3 + 3 * dim, wy * part[:, 128:256]),
                (4 + 3 * dim, wyd * part[:, :128]),
                (5 + 3 * dim, wy * part[:, 256:]),
            )
            for component, value in terms:
                at = pl.ds(pl.multiple_of(component * 8 * blocks + 8 * block, 8), 8)
                partial[at, :] = value

    def of_group(function, step, *values):
        return tuple(
            function(step * GROUP + member, *(value[member] for value in values))
            for member in range(GROUP)
        )

    def group(step, carry):
        left_sides, sums = carry
        following = of_group(gather, step + 2)
        products = of_group(contract, step + 1, left_sides)
        of_group(weigh, step, sums)
        return following, products

    steps = blocks // GROUP
    carry = of_group(gather, 1), of_group(contract, 0, of_group(gather, 0))
    left_sides, sums = lax.fori_loop(0, steps - 2, group, carry)
    of_group(weigh, steps - 2, sums)
    of_group(weigh, steps - 1, of_group(contract, steps - 1, left_sides))
    for component in range(12):
        total = partial[pl.ds(component * 8 * blocks, blocks, stride=8), :]
        for node in range(1, 6):
            total = total + partial[pl.ds(component * 8 * blocks + node, blocks, stride=8), :]
        if component >= 3:
            total = 4.0 * total
        final[component * blocks : (component + 1) * blocks, :] = total
    for block in range(blocks):
        cols = slice(block * BLOCK, (block + 1) * BLOCK)
        new_velocity_ref[:, cols] = final[pl.ds(block, 3, stride=blocks), :]
        new_affine_ref[:, cols] = final[pl.ds(3 * blocks + block, 9, stride=blocks), :]
    stress_copy.wait()
    grid_copy.wait()


def shards(
    point_frac,
    cell_offset,
    point_velocity,
    point_affine,
    point_stress,
    point_mass,
    block_tile,
    block_count,
):
    blocks = block_tile.shape[0]
    points = blocks * BLOCK
    vmem = pl.BlockSpec(memory_space=pltpu.VMEM)
    hbm = pl.BlockSpec(memory_space=pltpu.HBM)
    f32 = jnp.float32
    grid_shape = jax.ShapeDtypeStruct((ROWS, LANES), f32)
    face = PY + PY // 3
    arguments = [
        pltpu.with_memory_space_constraint(value, pltpu.HBM)
        for value in (
            block_tile,
            block_count,
            point_frac,
            cell_offset,
            point_velocity,
            point_affine,
            point_stress,
            point_mass.reshape(blocks, BLOCK),
        )
    ]
    right_shape = jax.ShapeDtypeStruct((48 * blocks, 3 * LANES), jnp.bfloat16)
    velocity, right_high, right_low, y_table, stress = pl.pallas_call(
        deposit_kernel,
        name="deposit",
        out_shape=(
            grid_shape,
            right_shape,
            right_shape,
            jax.ShapeDtypeStruct((5 * blocks, LANES), f32),
            jax.ShapeDtypeStruct((6 * blocks, LANES), f32),
        ),
        in_specs=[hbm] * 8,
        out_specs=(vmem,) * 5,
        scratch_shapes=[
            pltpu.VMEM((ROWS, LANES), f32),
            pltpu.VMEM((ROWS, LANES), f32),
            pltpu.VMEM((T_SHARED * blocks, LANES), f32),
            pltpu.SMEM((blocks,), jnp.int32),
            pltpu.SMEM((blocks,), jnp.int32),
            pltpu.VMEM((3, points), f32),
            pltpu.VMEM((3, points), jnp.int32),
            pltpu.VMEM((3, points), f32),
            pltpu.VMEM((9, points), f32),
            pltpu.VMEM((6, points), f32),
            pltpu.VMEM((blocks, BLOCK), f32),
            pltpu.VMEM((48 * blocks, LANES), f32),
            pltpu.VMEM(((T_ALL - T_SHARED) * blocks, LANES), f32),
            pltpu.VMEM((6, 8 * blocks, 2 * LANES), jnp.bfloat16),
            pltpu.VMEM((6, 8 * blocks, 2 * LANES), jnp.bfloat16),
            pltpu.VMEM((2, face, LANES), f32),
            pltpu.VMEM((2, face, LANES), f32),
            pltpu.VMEM((2, 2 * face, LANES), f32),
            pltpu.VMEM((2, 2 * face, LANES), f32),
            pltpu.VMEM((4, 16, LANES), f32),
            pltpu.VMEM((4, 16, LANES), f32),
            pltpu.VMEM((2, 3 * PX + 2, LANES), f32),
            pltpu.VMEM((2, 3 * PX + 2, LANES), f32),
            pltpu.VMEM((4, 8, LANES), f32),
            pltpu.VMEM((4, 8, LANES), f32),
            pltpu.SemaphoreType.DMA((8,)),
            pltpu.SemaphoreType.DMA((14,)),
            pltpu.SemaphoreType.DMA((14,)),
        ],
        compiler_params=pltpu.CompilerParams(
            collective_id=0, has_side_effects=True, vmem_limit_bytes=VMEM_LIMIT
        ),
    )(*arguments)
    new_velocity, new_affine, new_stress, grid_velocity = pl.pallas_call(
        collect_kernel,
        name="collect",
        out_shape=(
            jax.ShapeDtypeStruct((3, points), f32),
            jax.ShapeDtypeStruct((9, points), f32),
            jax.ShapeDtypeStruct((6, points), f32),
            jax.ShapeDtypeStruct((3, CX, CZ, CY), f32),
        ),
        in_specs=[hbm] + [vmem] * 5,
        out_specs=(vmem, vmem, hbm, hbm),
        scratch_shapes=[
            pltpu.SMEM((blocks,), jnp.int32),
            pltpu.VMEM((6, points), f32),
            pltpu.VMEM((3, CX, CZ, CY), f32),
            pltpu.VMEM((12 * 8 * blocks, LANES), f32),
            pltpu.VMEM((12 * blocks, LANES), f32),
            pltpu.SemaphoreType.DMA((3,)),
        ],
        compiler_params=pltpu.CompilerParams(vmem_limit_bytes=VMEM_LIMIT),
    )(arguments[0], velocity, right_high, right_low, y_table, stress)
    return (new_velocity, new_affine, new_stress, jnp.swapaxes(grid_velocity, 2, 3))


def solution(mesh):
    points = P(None, ("gx", "gy", "gz"))
    flat = P(("gx", "gy", "gz"))
    return jax.shard_map(
        shards,
        mesh=mesh,
        in_specs=(points,) * 5 + (flat,) * 3,
        out_specs=(points, points, points, P(None, "gx", "gy", "gz")),
        check_vma=False,
    )
```

```python
import jax
import jax.numpy as jnp
from jax import lax
from jax.experimental import pallas as pl
from jax.experimental.pallas import tpu as pltpu
from jax.sharding import PartitionSpec as P

CX = 16
CY = 64
CZ = 32
BLOCK = 128

time_step = 0.1
gravity = 1.0
shear_modulus = 2.0
bulk_modulus = 4.0
friction_static = 0.38
friction_limit = 0.64
inertial_ref = 0.28
grain_size = 0.5
grain_density = 1.0
pressure_floor = 0.5
shear_floor = 0.5
mass_floor = 0.05
stress_scale = 0.4
pair_index = ((0, 5, 4), (5, 1, 3), (4, 3, 2))
component_pairs = ((0, 0), (1, 1), (2, 2), (1, 2), (0, 2), (0, 1))

PX = CX + 2
PY = 72
PITCH = 40
LANES = 128
ROWS = PX * PY
GROUP = 16
VMEM_LIMIT = 16 * 1024 * 1024
MESH = pl.DeviceIdType.MESH

T_WX, T_WXD = 0, 6
T_LY, T_MY, T_RY, T_OY, T_Y = 12, 13, 14, 15, 16
T_LZ, T_MZ, T_RZ, T_OZ, T_Z = 17, 18, 19, 20, 21
T_SHARED = 22
T_MASS, T_MV, T_A = 22, 23, 26
T_ALL = 35


def stress_update(stress, affine):
    strain_rate = [
        [
            0.5 * (affine[3 * row_dim + col_dim] + affine[3 * col_dim + row_dim])
            for col_dim in range(3)
        ]
        for row_dim in range(3)
    ]
    volume_rate = strain_rate[0][0] + strain_rate[1][1] + strain_rate[2][2]
    deviator = [
        [
            strain_rate[row_dim][col_dim] - (volume_rate / 3.0 if row_dim == col_dim else 0.0)
            for col_dim in range(3)
        ]
        for row_dim in range(3)
    ]
    trial_stress = []
    for component in range(6):
        row_dim, col_dim = component_pairs[component]
        value = stress[component] + time_step * 2.0 * shear_modulus * deviator[row_dim][col_dim]
        if component < 3:
            value = value + time_step * bulk_modulus * volume_rate
        trial_stress.append(value)
    pressure = -(trial_stress[0] + trial_stress[1] + trial_stress[2]) / 3.0
    shear_part = [trial_stress[component] + pressure for component in range(3)] + trial_stress[3:]
    shear_stress = jnp.sqrt(
        0.5 * (shear_part[0] ** 2 + shear_part[1] ** 2 + shear_part[2] ** 2)
        + shear_part[3] ** 2
        + shear_part[4] ** 2
        + shear_part[5] ** 2
    )
    shear_rate = jnp.sqrt(
        2.0
        * (
            deviator[0][0] ** 2
            + deviator[1][1] ** 2
            + deviator[2][2] ** 2
            + 2.0 * (deviator[1][2] ** 2 + deviator[0][2] ** 2 + deviator[0][1] ** 2)
        )
    )
    inertial = (
        shear_rate * grain_size / jnp.sqrt(jnp.maximum(pressure, pressure_floor) / grain_density)
    )
    friction = friction_static + (friction_limit - friction_static) * inertial / (
        inertial_ref + inertial
    )
    support = jnp.maximum(pressure, 0.0)
    factor = jnp.minimum(1.0, friction * support / jnp.maximum(shear_stress, shear_floor))
    return [shear_part[component] * factor - support for component in range(3)] + [
        shear_part[component] * factor for component in range(3, 6)
    ]


def split(values):
    high = values.astype(jnp.bfloat16)
    low = (values - high.astype(jnp.float32)).astype(jnp.bfloat16)
    return high, low


def tile_coords(tile_ref, block):
    tile = tile_ref[block]
    return tile >> 7, (tile >> 3) & 15, tile & 7


def axis_weights(row, left, middle, right, offset, position):
    index = lax.broadcasted_iota(jnp.int32, (8, LANES), 0).astype(jnp.float32)
    shifted = index - row(offset)
    weight = jnp.where(
        shifted == 0.0,
        row(left),
        jnp.where(shifted == 1.0, row(middle), jnp.where(shifted == 2.0, row(right), 0.0)),
    )
    return weight, weight * (index - row(position))


def deposit_kernel(
    tile_hbm,
    count_hbm,
    frac_hbm,
    offset_hbm,
    velocity_hbm,
    affine_hbm,
    stress_hbm,
    mass_hbm,
    velocity_out,
    collect_high,
    collect_low,
    y_table,
    stress_out,
    mom,
    mass,
    shared_ref,
    tile_ref,
    count_ref,
    frac_ref,
    offset_ref,
    velocity_ref,
    affine_ref,
    stress_ref,
    mass_ref,
    gathered,
    table,
    placed_high,
    placed_low,
    za_send,
    za_recv,
    zb_send,
    zb_recv,
    x_send,
    x_recv,
    xz_send,
    xz_recv,
    y_send,
    y_recv,
    xy_send,
    xy_recv,
    load_sem,
    send_sem,
    recv_sem,
):
    axes = ("gx", "gy", "gz")

    def device(dx, dy, dz):
        place = []
        for axis, step in zip(axes, (dx, dy, dz)):
            size = lax.axis_size(axis)
            moved = lax.axis_index(axis)
            if step and size & (size - 1) == 0:
                moved = (moved + size + step) & (size - 1)
            elif step:
                moved = lax.rem(moved + size + step, size)
            place.append(moved)
        return tuple(place)

    loads = [
        pltpu.make_async_copy(source, target, load_sem.at[index])
        for index, (source, target) in enumerate(
            (
                (frac_hbm, frac_ref),
                (offset_hbm, offset_ref),
                (velocity_hbm, velocity_ref),
                (affine_hbm, affine_ref),
                (stress_hbm, stress_ref),
                (mass_hbm, mass_ref),
                (count_hbm, count_ref),
                (tile_hbm, tile_ref),
            )
        )
    ]
    for load in loads:
        load.start()
    z_sides = [device(0, 0, -1), device(0, 0, 1)]
    x_sides = [device(-1, 0, 0), device(1, 0, 0)]
    y_sides = [device(0, -1, 0), device(0, 1, 0)]
    xz_sides = [device(dx, 0, dz) for dx in (-1, 1) for dz in (-1, 1)]
    xy_sides = [device(dx, dy, 0) for dx in (-1, 1) for dy in (-1, 1)]
    barrier = pltpu.get_barrier_semaphore()
    for target in z_sides + x_sides + xz_sides + y_sides + xy_sides:
        pl.semaphore_signal(barrier, inc=1, device_id=target, device_id_type=MESH)

    blocks = mass_ref.shape[0]
    lane_row = lax.broadcasted_iota(jnp.int32, (1, LANES), 1)
    stride = 48
    for load in loads:
        load.wait()
    for block in range(blocks):
        cols = slice(block * BLOCK, (block + 1) * BLOCK)
        at = block * stride
        gathered[at : at + 3, :] = frac_ref[:, cols]
        gathered[at + 8 : at + 11, :] = offset_ref[:, cols].astype(jnp.float32)
        gathered[at + 16 : at + 19, :] = velocity_ref[:, cols]
        gathered[at + 24 : at + 33, :] = affine_ref[:, cols]
        gathered[at + 40 : at + 46, :] = stress_ref[:, cols]
        row = (T_MASS - T_SHARED) * blocks + block
        table[row : row + 1, :] = jnp.where(
            lane_row < count_ref[block], mass_ref[block : block + 1, :], 0.0
        )

    def dense(component):
        return gathered[pl.ds(component, blocks, stride=stride), :]

    def put(index, value):
        if index < T_SHARED:
            shared_ref[index * blocks : (index + 1) * blocks, :] = value
        else:
            start = (index - T_SHARED) * blocks
            table[start : start + blocks, :] = value

    affine = [dense(24 + component) for component in range(9)]
    stress = stress_update([dense(40 + component) for component in range(6)], affine)
    for component in range(6):
        stress_out[component * blocks : (component + 1) * blocks, :] = stress[component]
    live_mass = table[(T_MASS - T_SHARED) * blocks : (T_MASS - T_SHARED + 1) * blocks, :]
    for row_dim in range(3):
        put(T_MV + row_dim, live_mass * dense(16 + row_dim))
        for col_dim in range(3):
            put(
                T_A + 3 * row_dim + col_dim,
                live_mass
                * (
                    affine[3 * row_dim + col_dim]
                    - stress_scale * stress[pair_index[row_dim][col_dim]]
                ),
            )
    spline = []
    for dim in range(3):
        fraction = dense(dim)
        spline.append(
            (
                0.5 * (1.5 - fraction) ** 2,
                0.75 - (fraction - 1.0) ** 2,
                0.5 * (fraction - 0.5) ** 2,
                dense(8 + dim),
                dense(8 + dim) + fraction,
            )
        )
    left, middle, right, offset, position = spline[0]
    for node in range(6):
        shifted = float(node) - offset
        weight = jnp.where(
            shifted == 0.0,
            left,
            jnp.where(shifted == 1.0, middle, jnp.where(shifted == 2.0, right, 0.0)),
        )
        put(T_WX + node, weight)
        put(T_WXD + node, weight * (float(node) - position))
    for index in range(5):
        put(T_LY + index, spline[1][index])
        put(T_LZ + index, spline[2][index])
        y_table[index * blocks : (index + 1) * blocks, :] = spline[1][index]

    lanes = lax.broadcasted_iota(jnp.int32, (8, 32), 1)
    channel = [(lanes >= 8 * index) & (lanes < 8 * index + 8) for index in range(4)]
    rest = jnp.zeros((8, LANES - 32), jnp.float32)
    blank = jnp.zeros((8, LANES), jnp.float32)

    def row_of(block):
        def row(index):
            if index < T_SHARED:
                value = shared_ref[pl.ds(index * blocks + block, 1), :]
            else:
                value = table[pl.ds((index - T_SHARED) * blocks + block, 1), :]
            return jnp.broadcast_to(value, (8, LANES))

        return row

    def block_sums(block):
        row = row_of(block)
        wy, wyd = axis_weights(row, T_LY, T_MY, T_RY, T_OY, T_Y)
        wz, wzd = axis_weights(row, T_LZ, T_MZ, T_RZ, T_OZ, T_Z)
        wx = [row(T_WX + node) for node in range(6)]
        wxd = [row(T_WXD + node) for node in range(6)]
        left_side = jnp.concatenate(
            [
                jnp.concatenate([w * wy for w in wx], axis=0),
                jnp.concatenate([w * wy for w in wxd], axis=0),
                jnp.concatenate([w * wyd for w in wx], axis=0),
            ],
            axis=1,
        )
        value_rows = [
            wz * row(T_MV + dim) + wzd * row(T_A + 3 * dim + 2) for dim in range(3)
        ] + [wz * row(T_MASS)]
        x_rows = [wz * row(T_A + 3 * dim) for dim in range(3)] + [blank]
        y_rows = [wz * row(T_A + 3 * dim + 1) for dim in range(3)] + [blank]
        right_side = jnp.concatenate(
            [jnp.concatenate(r, axis=0) for r in (value_rows, x_rows, y_rows)], axis=1
        )
        left_high, left_low = split(left_side)
        right_high, right_low = split(right_side)

        return lax.dot_general(
            jnp.concatenate([left_high, left_high, left_low], axis=1),
            jnp.concatenate([right_high, right_low, right_high], axis=1),
            (((1,), (1,)), ((), ())),
            preferred_element_type=jnp.float32,
        )

    starts = (0, PITCH - 8, 2 * PITCH - 16, LANES - 24)

    def group_place(step, sums):
        rows = pl.ds(pl.multiple_of(step * 8 * GROUP, 8 * GROUP), 8 * GROUP)
        heights = [4 * (tile_ref[step * GROUP + member] & 7) for member in range(GROUP)]
        for node in range(6):
            mom_rows, mass_rows = [], []
            for member in range(GROUP):
                part = sums[member][8 * node : 8 * node + 8]
                moved = [
                    pltpu.roll(
                        jnp.concatenate([jnp.where(channel[index], part, 0.0), rest], axis=1),
                        starts[index] + heights[member],
                        axis=1,
                    )
                    for index in range(4)
                ]
                mom_rows.append(moved[0] + moved[1] + moved[2])
                mass_rows.append(moved[3])
            for column, values in enumerate((mom_rows, mass_rows)):
                high, low = split(jnp.concatenate(values, axis=0))
                cols = slice(column * LANES, (column + 1) * LANES)
                placed_high[node, rows, cols] = high
                placed_low[node, rows, cols] = low

    def group_sums(step):
        return tuple(block_sums(step * GROUP + member) for member in range(GROUP))

    def group(step, sums):
        following = group_sums(step)
        group_place(step - 1, sums)
        return following

    steps = blocks // GROUP
    group_place(steps - 1, lax.fori_loop(1, steps, group, group_sums(0)))

    spots = 8 * blocks
    spot = lax.broadcasted_iota(jnp.int32, (8, spots), 1)
    owner = spot >> 3
    tiles = jnp.zeros((8, spots), jnp.int32)
    for block in range(blocks):
        tiles = jnp.where(owner == block, tile_ref[block], tiles)
    target = ((tiles >> 7) << 10) + (((tiles >> 3) & 15) << 2) + (spot & 7)
    y_row = lax.broadcasted_iota(jnp.int32, (8, spots), 0)
    chooser = jnp.concatenate(
        [
            jnp.where(target == y_row + (1024 * tile_x + start), 1.0, 0.0)
            for tile_x in range(CX // 4)
            for start in range(0, PY, 8)
        ],
        axis=0,
    ).astype(jnp.bfloat16)
    for node in range(6):
        layers = jnp.dot(
            chooser, placed_high[node], preferred_element_type=jnp.float32
        ) + jnp.dot(chooser, placed_low[node], preferred_element_type=jnp.float32)
        for tile_x in range(CX // 4):
            part = layers[tile_x * PY : (tile_x + 1) * PY]
            x = 4 * tile_x + node
            at = slice(x * PY, (x + 1) * PY)
            if node < 4 or x >= CX:
                mom[at, :] = part[:, :LANES]
                mass[at, :] = part[:, LANES:]
            else:
                mom[at, :] += part[:, :LANES]
                mass[at, :] += part[:, LANES:]

    def copy(src, dst, slot, target):
        return pltpu.make_async_remote_copy(
            src_ref=src,
            dst_ref=dst,
            send_sem=send_sem.at[slot],
            recv_sem=recv_sem.at[slot],
            device_id=target,
            device_id_type=MESH,
        )

    lane = lax.broadcasted_iota(jnp.int32, (PY, LANES), 1)
    in_mom = lane < 3 * PITCH
    in_pitch = lax.rem(lane, PITCH)
    third = PY // 3
    lane3 = lane[:third]
    pl.semaphore_wait(barrier, 14)

    pair = jnp.where(in_mom, in_pitch >> 1, -1)
    far = lax.rem(lane + (LANES - CZ), LANES)
    far_pair = jnp.where(far < 3 * PITCH, lax.rem(far, PITCH) >> 1, -1)
    pair3 = lane3 >> 1
    far_pair3 = far[:third] >> 1
    outer = (0, CY)
    groups = (8, 8 + third, PY - third)

    def pick(values, start, x, whole):
        shift = start + 2 * x
        moved = pltpu.roll(values, shift, axis=1) if shift else values
        count = values.shape[0]
        sides = (pair, far_pair) if whole else (pair3, far_pair3)
        return [(side[:count] == shift // 2 if not whole else side[:count] == x, moved)
                for side in sides]

    def gather_pairs(pieces, whole):
        result = [None, None]
        for values, start, x in pieces:
            for side, (mask, moved) in enumerate(pick(values, start, x, whole)):
                before = 0.0 if result[side] is None else result[side]
                result[side] = jnp.where(mask, moved, before)
        return result

    def layer_rows(grid, x, first, count):
        return grid[x * PY + first : x * PY + first + count, :]

    def z_start(send, recv, slot):
        copies = [
            copy(send.at[side], recv.at[1 - side], slot + side, z_sides[side])
            for side in range(2)
        ]
        for c in copies:
            c.start()
        return copies

    for index, first in enumerate(outer):
        packed = gather_pairs([(layer_rows(mom, x, first, 8), 0, x) for x in range(PX)], True)
        for side in range(2):
            za_send[side, 8 * index : 8 * index + 8, :] = packed[side]
    packed = gather_pairs(
        [
            (layer_rows(mass, x, first, 8), PITCH * index, x)
            for index, first in enumerate(outer)
            for x in range(PX)
        ],
        False,
    )
    for side in range(2):
        za_send[side, 16:, :] = packed[side]
    za_copies = z_start(za_send, za_recv, 0)

    firsts = (0, CX * PY)
    for side in range(2):
        first = firsts[side]
        x_send[side, : 2 * PY, :] = mom[first : first + 2 * PY, :]
        for layer in range(2):
            start = first + layer * PY
            at = 2 * PY + layer * third
            x_send[side, at : at + third, :] = (
                mass[start : start + third, :]
                + pltpu.roll(mass[start + third : start + 2 * third, :], PITCH, axis=1)
                + pltpu.roll(mass[start + 2 * third : start + 3 * third, :], 2 * PITCH, axis=1)
            )
    x_copies = [
        copy(x_send.at[side], x_recv.at[1 - side], 2 + side, x_sides[side]) for side in range(2)
    ]
    for c in x_copies:
        c.start()

    packed = gather_pairs([(layer_rows(mom, x, 8, CY - 8), 0, x) for x in range(PX)], True)
    packed_mass = gather_pairs(
        [
            (layer_rows(mass, x, first, third), PITCH * index, x)
            for index, first in enumerate(groups)
            for x in range(PX)
        ],
        False,
    )
    for side in range(2):
        zb_send[side, : CY - 8, :] = packed[side]
        zb_send[side, CY - 8 :, :] = packed_mass[side]
    zb_copies = z_start(zb_send, zb_recv, 14)

    quad = lax.broadcasted_iota(jnp.int32, (8, LANES), 1) >> 2
    for edge in range(4):
        x0, z_side = CX * (edge // 2), edge % 2
        result = [None, None]
        for tile in range(PY // 8):
            half, start = tile // 8, 16 * (tile % 8)
            if 8 * tile in outer:
                z_buffer, mom_at, mass_at = za_send, tile, 16
                mass_group = outer.index(8 * tile)
            else:
                mass_group = min((tile - 1) // 3, 2)
                z_buffer, mom_at = zb_send, 8 * (tile - 1)
                mass_at = CY - 8 + 8 * tile - groups[mass_group]
            rows = z_buffer[z_side, mom_at : mom_at + 8, :]
            mass_rows = z_buffer[z_side, mass_at : mass_at + 8, :]
            for index in range(4):
                if index < 3:
                    source, at = rows, PITCH * index + 2 * x0 + CZ * z_side
                else:
                    source, at = mass_rows, PITCH * mass_group + 2 * x0 + CZ * z_side
                to = start + 4 * index
                moved = pltpu.roll(source, (2 * LANES + to - at) % LANES, axis=1)
                if result[half] is None:
                    result[half] = moved
                else:
                    result[half] = jnp.where(quad == to // 4, moved, result[half])
        xz_send[edge, :8, :] = result[0]
        xz_send[edge, 8:, :] = result[1]
    xz_copies = [
        copy(xz_send.at[edge], xz_recv.at[3 - edge], 6 + edge, xz_sides[edge])
        for edge in range(4)
    ]
    for c in xz_copies:
        c.start()

    rim = in_mom & ((in_pitch < 2) | ((in_pitch >= CZ) & (in_pitch < CZ + 2)))
    rim3 = (lane3 < 2) | ((lane3 >= CZ) & (lane3 < CZ + 2))

    def spread(grid, x, first, count, received, start, whole):
        low, high = received
        mask = pair[:count] == x if whole else pair3[:count] == start // 2 + x
        moved = pltpu.roll(
            jnp.where(mask, high, low), (2 * LANES + CZ - start - 2 * x) % LANES, axis=1
        )
        at = slice(x * PY + first, x * PY + first + count)
        grid[at, :] += jnp.where((rim if whole else rim3)[:count], moved, 0.0)

    for c in za_copies:
        c.wait()
    received = pltpu.roll(za_recv[0], 64, axis=1), za_recv[1]
    for x in range(PX):
        for index, first in enumerate(outer):
            rows = slice(8 * index, 8 * index + 8)
            spread(mom, x, first, 8, [side[rows] for side in received], 0, True)
            spread(mass, x, first, 8, [side[16:] for side in received], PITCH * index, False)

    y_firsts = (0, CY)
    for side in range(2):
        y0 = y_firsts[side]
        y_send[side, 0:PX, :] = mom[pl.ds(y0, PX, stride=PY), :]
        y_send[side, PX : 2 * PX, :] = mom[pl.ds(y0 + 1, PX, stride=PY), :]
        y_send[side, 2 * PX : 3 * PX, :] = mass[pl.ds(y0, PX, stride=PY), :] + pltpu.roll(
            mass[pl.ds(y0 + 1, PX, stride=PY), :], 64, axis=1
        )
        y_send[side, 3 * PX :, :] = jnp.zeros((2, LANES), jnp.float32)
    y_copies = [
        copy(y_send.at[side], y_recv.at[1 - side], 4 + side, y_sides[side]) for side in range(2)
    ]
    for edge in range(4):
        x0, y0 = CX * (edge // 2), y_firsts[edge % 2]
        for layer in range(2):
            at = (x0 + layer) * PY + y0
            xy_send[edge, 2 * layer : 2 * layer + 2, :] = mom[at : at + 2, :]
            xy_send[edge, 4 + 2 * layer : 6 + 2 * layer, :] = mass[at : at + 2, :]
        y_copies.append(copy(xy_send.at[edge], xy_recv.at[3 - edge], 10 + edge, xy_sides[edge]))
    for c in y_copies:
        c.start()

    for c in zb_copies:
        c.wait()
    received = pltpu.roll(zb_recv[0], 64, axis=1), zb_recv[1]
    for x in range(PX):
        spread(mom, x, 8, CY - 8, [side[: CY - 8] for side in received], 0, True)
        for index, first in enumerate(groups):
            skip = 0 if index < 2 else 8
            count = third if index < 2 else 8
            rows = slice(CY - 8 + skip, CY - 8 + skip + count)
            spread(
                mass, x, first + skip, count, [side[rows] for side in received],
                PITCH * index, False,
            )

    width_x = lax.axis_size("gx") * CX
    height_y = lax.axis_size("gy") * CY
    depth_z = lax.axis_size("gz") * CZ
    first_z = lax.axis_index("gz") * CZ
    first_y = lax.axis_index("gy") * CY
    first_x = lax.axis_index("gx") * CX
    z_index = lax.rem(lane - 2 * PITCH - 1 + first_z + depth_z, depth_z)
    is_y = (lane >= PITCH) & (lane < 2 * PITCH)
    is_z = (lane >= 2 * PITCH) & (lane < 3 * PITCH)
    z_floor = is_z & (z_index < 2)
    z_top = is_z & (z_index >= depth_z - 2)
    fall = jnp.where(is_y, time_step * gravity, 0.0)
    row_index = lax.broadcasted_iota(jnp.int32, (PY, LANES), 0)
    y_floor = is_y & (lax.rem(row_index - 1 + first_y + height_y, height_y) < 2)

    def update(mom_values, mass_values, floor, count):
        inverse = 1.0 / (mass_values + mass_floor)
        inverse = jnp.where(
            lane[:count] < PITCH,
            inverse,
            jnp.where(
                is_y[:count],
                pltpu.roll(inverse, PITCH, axis=1),
                pltpu.roll(inverse, 2 * PITCH, axis=1),
            ),
        )
        values = mom_values * inverse - fall[:count]
        values = jnp.where(z_floor[:count] | floor, jnp.maximum(values, 0.0), values)
        return jnp.where(z_top[:count], jnp.minimum(values, 0.0), values)

    def off_outlet(x):
        x_index = lax.rem(first_x + x - 1 + width_x, width_x)
        return (x_index < width_x // 4) | (x_index >= width_x - width_x // 4)

    def update_layer(x):
        at = pl.ds(pl.multiple_of(x * PY, 8), PY)
        velocity_out[at, :] = update(mom[at, :], mass[at, :], y_floor & off_outlet(x), PY)

    def layers(step, carry):
        for member in range(7):
            update_layer(2 + 7 * step + member)
        return carry

    lax.fori_loop(0, 2, layers, 0)

    def right_sides(step, carry):
        for member in range(2):
            block = 2 * step + member
            row = row_of(block)
            wz, wzd = axis_weights(row, T_LZ, T_MZ, T_RZ, T_OZ, T_Z)
            wx = [row(T_WX + node) for node in range(6)]
            wxd = [row(T_WXD + node) for node in range(6)]
            at = pl.ds(pl.multiple_of(48 * block, 16), 48)
            for index, (along_x, along_z) in enumerate(((wx, wz), (wxd, wz), (wx, wzd))):
                high, low = split(jnp.concatenate([w * along_z for w in along_x], axis=0))
                cols = slice(index * LANES, (index + 1) * LANES)
                collect_high[at, cols] = high
                collect_low[at, cols] = low
        return carry

    lax.fori_loop(0, blocks // 2, right_sides, 0)

    for c in xz_copies:
        c.wait()
    lane8 = lane[:8]
    for side in range(2):
        for layer in range(2):
            for tile in range(PY // 8):
                half, start = tile // 8, 16 * (tile % 8)
                mom_value, mass_value = 0.0, 0.0
                for z_side in range(2):
                    source = xz_recv[2 * side + z_side, 8 * half : 8 * half + 8, :]
                    for index in range(4):
                        to = (PITCH * index if index < 3 else 0) + CZ * z_side
                        at = start + 4 * index + 2 * layer
                        moved = pltpu.roll(source, (LANES + to - at) % LANES, axis=1)
                        here = (lane8 >= to) & (lane8 < to + 2)
                        if index < 3:
                            mom_value = jnp.where(here, moved, mom_value)
                        else:
                            mass_value = jnp.where(here, moved, mass_value)
                at = firsts[side] + layer * PY + 8 * tile
                mom[at : at + 8, :] += mom_value
                mass[at : at + 8, :] += mass_value

    for c in x_copies:
        c.wait()
    near3 = lane3 < PITCH
    for side in range(2):
        first = firsts[side]
        mom[first : first + 2 * PY, :] += x_recv[side, : 2 * PY, :]
        for layer in range(2):
            at = 2 * PY + layer * third
            got = x_recv[side, at : at + third, :]
            for part in range(3):
                start = first + layer * PY + part * third
                moved = pltpu.roll(got, (LANES - PITCH * part) % LANES, axis=1)
                mass[start : start + third, :] += jnp.where(near3, moved, 0.0)
    for x in (0, 1, CX, CX + 1):
        update_layer(x)
    front = lane < 64
    for c in y_copies:
        c.wait()
    for side in range(2):
        y0 = y_firsts[side]
        got = y_recv[side, 2 * PX : 3 * PX, :]
        at0 = pl.ds(y0, PX, stride=PY)
        at1 = pl.ds(y0 + 1, PX, stride=PY)
        mom[at0, :] = mom[at0, :] + y_recv[side, 0:PX, :]
        mom[at1, :] = mom[at1, :] + y_recv[side, PX : 2 * PX, :]
        mass[at0, :] = mass[at0, :] + jnp.where(front[:PX], got, 0.0)
        mass[at1, :] = mass[at1, :] + jnp.where(front[:PX], pltpu.roll(got, 64, axis=1), 0.0)
    for edge in range(4):
        x0, y0 = CX * (edge // 2), y_firsts[edge % 2]
        for layer in range(2):
            at = (x0 + layer) * PY + y0
            mom[at : at + 2, :] += xy_recv[edge, 2 * layer : 2 * layer + 2, :]
            mass[at : at + 2, :] += xy_recv[edge, 4 + 2 * layer : 6 + 2 * layer, :]
    x_rows = lax.broadcasted_iota(jnp.int32, (PX, LANES), 0)
    outside = off_outlet(x_rows)
    for y in (0, 1, CY, CY + 1):
        at = pl.ds(y, PX, stride=PY)
        on_floor = lax.rem(first_y + (y - 1 + height_y), height_y) < 2
        velocity_out[at, :] = update(
            mom[at, :], mass[at, :], is_y[:PX] & outside & on_floor, PX
        )


def collect_kernel(
    tile_hbm,
    velocity,
    right_high,
    right_low,
    y_table,
    stress_in,
    new_velocity_ref,
    new_affine_ref,
    new_stress_hbm,
    grid_velocity_hbm,
    tile_ref,
    new_stress_ref,
    grid_velocity_ref,
    partial,
    final,
    copy_sem,
):
    blocks = tile_hbm.shape[0]
    tile_copy = pltpu.make_async_copy(tile_hbm, tile_ref, copy_sem.at[0])
    tile_copy.start()
    for block in range(blocks):
        new_stress_ref[:, block * BLOCK : (block + 1) * BLOCK] = stress_in[
            pl.ds(block, 6, stride=blocks), :
        ]
    stress_copy = pltpu.make_async_copy(new_stress_ref, new_stress_hbm, copy_sem.at[1])
    stress_copy.start()
    def output(step, carry):
        for member in range(4):
            x = 4 * step + member
            turned = jnp.transpose(velocity[pl.ds((x + 1) * PY + 1, CY), :])
            for dim in range(3):
                grid_velocity_ref[dim, x] = turned[PITCH * dim + 1 : PITCH * dim + 1 + CZ]
        return carry

    lax.fori_loop(0, CX // 4, output, 0)
    grid_copy = pltpu.make_async_copy(grid_velocity_ref, grid_velocity_hbm, copy_sem.at[2])
    grid_copy.start()
    tile_copy.wait()

    lanes = lax.broadcasted_iota(jnp.int32, (8, LANES), 1)

    def gather(block):
        tile_x, tile_y, tile_z = tile_coords(tile_ref, block)
        planes = []
        for node in range(6):
            at = pl.ds(pl.multiple_of((4 * tile_x + node) * PY + 4 * tile_y, 4), 8)
            planes.append(velocity[at, :])
        rows = []
        for dim in range(3):
            merged = None
            for node in range(6):
                moved = pltpu.roll(
                    planes[node],
                    LANES + 8 * node - PITCH * dim - 4 * tile_z,
                    axis=1,
                )
                merged = moved if merged is None else jnp.where(lanes < 8 * node, merged, moved)
            rows.append(merged)
        return jnp.concatenate(rows, axis=0)

    def contract(block, left_side):
        left_high, left_low = split(left_side[:, :48])
        at = pl.ds(pl.multiple_of(48 * block, 16), 48)
        both = jnp.dot(
            jnp.concatenate([left_high, left_low], axis=0),
            right_high[at, :],
            preferred_element_type=jnp.float32,
        )
        return (
            both[:24]
            + both[24:]
            + jnp.dot(left_high, right_low[at, :], preferred_element_type=jnp.float32)
        )

    def weigh(block, sums):
        def row(index):
            return jnp.broadcast_to(y_table[pl.ds(index * blocks + block, 1), :], (8, LANES))

        wy, wyd = axis_weights(row, 0, 1, 2, 3, 4)
        for dim in range(3):
            part = sums[8 * dim : 8 * dim + 8]
            terms = (
                (dim, wy * part[:, :128]),
                (3 + 3 * dim, wy * part[:, 128:256]),
                (4 + 3 * dim, wyd * part[:, :128]),
                (5 + 3 * dim, wy * part[:, 256:]),
            )
            for component, value in terms:
                at = pl.ds(pl.multiple_of(component * 8 * blocks + 8 * block, 8), 8)
                partial[at, :] = value

    def of_group(function, step, *values):
        return tuple(
            function(step * GROUP + member, *(value[member] for value in values))
            for member in range(GROUP)
        )

    def group(step, carry):
        left_sides, sums = carry
        following = of_group(gather, step + 2)
        products = of_group(contract, step + 1, left_sides)
        of_group(weigh, step, sums)
        return following, products

    steps = blocks // GROUP
    carry = of_group(gather, 1), of_group(contract, 0, of_group(gather, 0))
    left_sides, sums = lax.fori_loop(0, steps - 2, group, carry)
    of_group(weigh, steps - 2, sums)
    of_group(weigh, steps - 1, of_group(contract, steps - 1, left_sides))
    for component in range(12):
        total = partial[pl.ds(component * 8 * blocks, blocks, stride=8), :]
        for node in range(1, 6):
            total = total + partial[pl.ds(component * 8 * blocks + node, blocks, stride=8), :]
        if component >= 3:
            total = 4.0 * total
        final[component * blocks : (component + 1) * blocks, :] = total
    for block in range(blocks):
        cols = slice(block * BLOCK, (block + 1) * BLOCK)
        new_velocity_ref[:, cols] = final[pl.ds(block, 3, stride=blocks), :]
        new_affine_ref[:, cols] = final[pl.ds(3 * blocks + block, 9, stride=blocks), :]
    stress_copy.wait()
    grid_copy.wait()


def shards(
    point_frac,
    cell_offset,
    point_velocity,
    point_affine,
    point_stress,
    point_mass,
    block_tile,
    block_count,
):
    blocks = block_tile.shape[0]
    points = blocks * BLOCK
    vmem = pl.BlockSpec(memory_space=pltpu.VMEM)
    hbm = pl.BlockSpec(memory_space=pltpu.HBM)
    f32 = jnp.float32
    grid_shape = jax.ShapeDtypeStruct((ROWS, LANES), f32)
    face = PY + PY // 3
    arguments = [
        pltpu.with_memory_space_constraint(value, pltpu.HBM)
        for value in (
            block_tile,
            block_count,
            point_frac,
            cell_offset,
            point_velocity,
            point_affine,
            point_stress,
            point_mass.reshape(blocks, BLOCK),
        )
    ]
    right_shape = jax.ShapeDtypeStruct((48 * blocks, 3 * LANES), jnp.bfloat16)
    velocity, right_high, right_low, y_table, stress = pl.pallas_call(
        deposit_kernel,
        name="deposit",
        out_shape=(
            grid_shape,
            right_shape,
            right_shape,
            jax.ShapeDtypeStruct((5 * blocks, LANES), f32),
            jax.ShapeDtypeStruct((6 * blocks, LANES), f32),
        ),
        in_specs=[hbm] * 8,
        out_specs=(vmem,) * 5,
        scratch_shapes=[
            pltpu.VMEM((ROWS, LANES), f32),
            pltpu.VMEM((ROWS, LANES), f32),
            pltpu.VMEM((T_SHARED * blocks, LANES), f32),
            pltpu.SMEM((blocks,), jnp.int32),
            pltpu.SMEM((blocks,), jnp.int32),
            pltpu.VMEM((3, points), f32),
            pltpu.VMEM((3, points), jnp.int32),
            pltpu.VMEM((3, points), f32),
            pltpu.VMEM((9, points), f32),
            pltpu.VMEM((6, points), f32),
            pltpu.VMEM((blocks, BLOCK), f32),
            pltpu.VMEM((48 * blocks, LANES), f32),
            pltpu.VMEM(((T_ALL - T_SHARED) * blocks, LANES), f32),
            pltpu.VMEM((6, 8 * blocks, 2 * LANES), jnp.bfloat16),
            pltpu.VMEM((6, 8 * blocks, 2 * LANES), jnp.bfloat16),
            pltpu.VMEM((2, 24, LANES), f32),
            pltpu.VMEM((2, 24, LANES), f32),
            pltpu.VMEM((2, CY - 8 + PY // 3, LANES), f32),
            pltpu.VMEM((2, CY - 8 + PY // 3, LANES), f32),
            pltpu.VMEM((2, 2 * face, LANES), f32),
            pltpu.VMEM((2, 2 * face, LANES), f32),
            pltpu.VMEM((4, 16, LANES), f32),
            pltpu.VMEM((4, 16, LANES), f32),
            pltpu.VMEM((2, 3 * PX + 2, LANES), f32),
            pltpu.VMEM((2, 3 * PX + 2, LANES), f32),
            pltpu.VMEM((4, 8, LANES), f32),
            pltpu.VMEM((4, 8, LANES), f32),
            pltpu.SemaphoreType.DMA((8,)),
            pltpu.SemaphoreType.DMA((16,)),
            pltpu.SemaphoreType.DMA((16,)),
        ],
        compiler_params=pltpu.CompilerParams(
            collective_id=0, has_side_effects=True, vmem_limit_bytes=VMEM_LIMIT
        ),
    )(*arguments)
    new_velocity, new_affine, new_stress, grid_velocity = pl.pallas_call(
        collect_kernel,
        name="collect",
        out_shape=(
            jax.ShapeDtypeStruct((3, points), f32),
            jax.ShapeDtypeStruct((9, points), f32),
            jax.ShapeDtypeStruct((6, points), f32),
            jax.ShapeDtypeStruct((3, CX, CZ, CY), f32),
        ),
        in_specs=[hbm] + [vmem] * 5,
        out_specs=(vmem, vmem, hbm, hbm),
        scratch_shapes=[
            pltpu.SMEM((blocks,), jnp.int32),
            pltpu.VMEM((6, points), f32),
            pltpu.VMEM((3, CX, CZ, CY), f32),
            pltpu.VMEM((12 * 8 * blocks, LANES), f32),
            pltpu.VMEM((12 * blocks, LANES), f32),
            pltpu.SemaphoreType.DMA((3,)),
        ],
        compiler_params=pltpu.CompilerParams(vmem_limit_bytes=VMEM_LIMIT),
    )(arguments[0], velocity, right_high, right_low, y_table, stress)
    return (new_velocity, new_affine, new_stress, jnp.swapaxes(grid_velocity, 2, 3))


def solution(mesh):
    points = P(None, ("gx", "gy", "gz"))
    flat = P(("gx", "gy", "gz"))
    return jax.shard_map(
        shards,
        mesh=mesh,
        in_specs=(points,) * 5 + (flat,) * 3,
        out_specs=(points, points, points, P(None, "gx", "gy", "gz")),
        check_vma=False,
    )
```

```python
import jax
import jax.numpy as jnp
from jax import lax
from jax.experimental import pallas as pl
from jax.experimental.pallas import tpu as pltpu
from jax.sharding import PartitionSpec as P

CX = 16
CY = 64
CZ = 32
BLOCK = 128

time_step = 0.1
gravity = 1.0
shear_modulus = 2.0
bulk_modulus = 4.0
friction_static = 0.38
friction_limit = 0.64
inertial_ref = 0.28
grain_size = 0.5
grain_density = 1.0
pressure_floor = 0.5
shear_floor = 0.5
mass_floor = 0.05
stress_scale = 0.4
pair_index = ((0, 5, 4), (5, 1, 3), (4, 3, 2))
component_pairs = ((0, 0), (1, 1), (2, 2), (1, 2), (0, 2), (0, 1))

PX = CX + 2
PY = 72
PITCH = 40
LANES = 128
ROWS = PX * PY
GROUP = 16
VMEM_LIMIT = 16 * 1024 * 1024
MESH = pl.DeviceIdType.MESH

T_WX, T_WXD = 0, 6
T_LY, T_MY, T_RY, T_OY, T_Y = 12, 13, 14, 15, 16
T_LZ, T_MZ, T_RZ, T_OZ, T_Z = 17, 18, 19, 20, 21
T_SHARED = 22
T_MASS, T_MV, T_A = 22, 23, 26
T_ALL = 35


def stress_update(stress, affine):
    strain_rate = [
        [
            0.5 * (affine[3 * row_dim + col_dim] + affine[3 * col_dim + row_dim])
            for col_dim in range(3)
        ]
        for row_dim in range(3)
    ]
    volume_rate = strain_rate[0][0] + strain_rate[1][1] + strain_rate[2][2]
    deviator = [
        [
            strain_rate[row_dim][col_dim] - (volume_rate / 3.0 if row_dim == col_dim else 0.0)
            for col_dim in range(3)
        ]
        for row_dim in range(3)
    ]
    trial_stress = []
    for component in range(6):
        row_dim, col_dim = component_pairs[component]
        value = stress[component] + time_step * 2.0 * shear_modulus * deviator[row_dim][col_dim]
        if component < 3:
            value = value + time_step * bulk_modulus * volume_rate
        trial_stress.append(value)
    pressure = -(trial_stress[0] + trial_stress[1] + trial_stress[2]) / 3.0
    shear_part = [trial_stress[component] + pressure for component in range(3)] + trial_stress[3:]
    shear_stress = jnp.sqrt(
        0.5 * (shear_part[0] ** 2 + shear_part[1] ** 2 + shear_part[2] ** 2)
        + shear_part[3] ** 2
        + shear_part[4] ** 2
        + shear_part[5] ** 2
    )
    shear_rate = jnp.sqrt(
        2.0
        * (
            deviator[0][0] ** 2
            + deviator[1][1] ** 2
            + deviator[2][2] ** 2
            + 2.0 * (deviator[1][2] ** 2 + deviator[0][2] ** 2 + deviator[0][1] ** 2)
        )
    )
    inertial = (
        shear_rate * grain_size / jnp.sqrt(jnp.maximum(pressure, pressure_floor) / grain_density)
    )
    friction = friction_static + (friction_limit - friction_static) * inertial / (
        inertial_ref + inertial
    )
    support = jnp.maximum(pressure, 0.0)
    factor = jnp.minimum(1.0, friction * support / jnp.maximum(shear_stress, shear_floor))
    return [shear_part[component] * factor - support for component in range(3)] + [
        shear_part[component] * factor for component in range(3, 6)
    ]


def split(values):
    high = values.astype(jnp.bfloat16)
    low = (values - high.astype(jnp.float32)).astype(jnp.bfloat16)
    return high, low


def tile_coords(tile_ref, block):
    tile = tile_ref[block]
    return tile >> 7, (tile >> 3) & 15, tile & 7


def axis_weights(row, left, middle, right, offset, position):
    index = lax.broadcasted_iota(jnp.int32, (8, LANES), 0).astype(jnp.float32)
    shifted = index - row(offset)
    weight = jnp.where(
        shifted == 0.0,
        row(left),
        jnp.where(shifted == 1.0, row(middle), jnp.where(shifted == 2.0, row(right), 0.0)),
    )
    return weight, weight * (index - row(position))


def deposit_kernel(
    tile_hbm,
    count_hbm,
    frac_hbm,
    offset_hbm,
    velocity_hbm,
    affine_hbm,
    stress_hbm,
    mass_hbm,
    velocity_out,
    collect_high,
    collect_low,
    y_table,
    stress_out,
    mom,
    mass,
    shared_ref,
    tile_ref,
    count_ref,
    frac_ref,
    offset_ref,
    velocity_ref,
    affine_ref,
    stress_ref,
    mass_ref,
    gathered,
    table,
    placed_high,
    placed_low,
    za_send,
    za_recv,
    zb_send,
    zb_recv,
    x_send,
    x_recv,
    xz_send,
    xz_recv,
    y_send,
    y_recv,
    xy_send,
    xy_recv,
    load_sem,
    send_sem,
    recv_sem,
):
    axes = ("gx", "gy", "gz")

    def device(dx, dy, dz):
        place = []
        for axis, step in zip(axes, (dx, dy, dz)):
            size = lax.axis_size(axis)
            moved = lax.axis_index(axis)
            if step and size & (size - 1) == 0:
                moved = (moved + size + step) & (size - 1)
            elif step:
                moved = lax.rem(moved + size + step, size)
            place.append(moved)
        return tuple(place)

    loads = [
        pltpu.make_async_copy(source, target, load_sem.at[index])
        for index, (source, target) in enumerate(
            (
                (frac_hbm, frac_ref),
                (offset_hbm, offset_ref),
                (velocity_hbm, velocity_ref),
                (affine_hbm, affine_ref),
                (stress_hbm, stress_ref),
                (mass_hbm, mass_ref),
                (count_hbm, count_ref),
                (tile_hbm, tile_ref),
            )
        )
    ]
    for load in loads:
        load.start()
    z_sides = [device(0, 0, -1), device(0, 0, 1)]
    x_sides = [device(-1, 0, 0), device(1, 0, 0)]
    y_sides = [device(0, -1, 0), device(0, 1, 0)]
    xz_sides = [device(dx, 0, dz) for dx in (-1, 1) for dz in (-1, 1)]
    xy_sides = [device(dx, dy, 0) for dx in (-1, 1) for dy in (-1, 1)]
    barrier = pltpu.get_barrier_semaphore()
    for target in z_sides + x_sides + xz_sides + y_sides + xy_sides:
        pl.semaphore_signal(barrier, inc=1, device_id=target, device_id_type=MESH)

    blocks = mass_ref.shape[0]
    lane_row = lax.broadcasted_iota(jnp.int32, (1, LANES), 1)
    stride = 48
    for load in loads:
        load.wait()
    for block in range(blocks):
        cols = slice(block * BLOCK, (block + 1) * BLOCK)
        at = block * stride
        gathered[at : at + 3, :] = frac_ref[:, cols]
        gathered[at + 8 : at + 11, :] = offset_ref[:, cols].astype(jnp.float32)
        gathered[at + 16 : at + 19, :] = velocity_ref[:, cols]
        gathered[at + 24 : at + 33, :] = affine_ref[:, cols]
        gathered[at + 40 : at + 46, :] = stress_ref[:, cols]
        row = (T_MASS - T_SHARED) * blocks + block
        table[row : row + 1, :] = jnp.where(
            lane_row < count_ref[block], mass_ref[block : block + 1, :], 0.0
        )

    def dense(component):
        return gathered[pl.ds(component, blocks, stride=stride), :]

    def put(index, value):
        if index < T_SHARED:
            shared_ref[index * blocks : (index + 1) * blocks, :] = value
        else:
            start = (index - T_SHARED) * blocks
            table[start : start + blocks, :] = value

    affine = [dense(24 + component) for component in range(9)]
    stress = stress_update([dense(40 + component) for component in range(6)], affine)
    for component in range(6):
        stress_out[component * blocks : (component + 1) * blocks, :] = stress[component]
    live_mass = table[(T_MASS - T_SHARED) * blocks : (T_MASS - T_SHARED + 1) * blocks, :]
    for row_dim in range(3):
        put(T_MV + row_dim, live_mass * dense(16 + row_dim))
        for col_dim in range(3):
            put(
                T_A + 3 * row_dim + col_dim,
                live_mass
                * (
                    affine[3 * row_dim + col_dim]
                    - stress_scale * stress[pair_index[row_dim][col_dim]]
                ),
            )
    spline = []
    for dim in range(3):
        fraction = dense(dim)
        spline.append(
            (
                0.5 * (1.5 - fraction) ** 2,
                0.75 - (fraction - 1.0) ** 2,
                0.5 * (fraction - 0.5) ** 2,
                dense(8 + dim),
                dense(8 + dim) + fraction,
            )
        )
    left, middle, right, offset, position = spline[0]
    for node in range(6):
        shifted = float(node) - offset
        weight = jnp.where(
            shifted == 0.0,
            left,
            jnp.where(shifted == 1.0, middle, jnp.where(shifted == 2.0, right, 0.0)),
        )
        put(T_WX + node, weight)
        put(T_WXD + node, weight * (float(node) - position))
    for index in range(5):
        put(T_LY + index, spline[1][index])
        put(T_LZ + index, spline[2][index])
        y_table[index * blocks : (index + 1) * blocks, :] = spline[1][index]

    lanes = lax.broadcasted_iota(jnp.int32, (8, 32), 1)
    channel = [(lanes >= 8 * index) & (lanes < 8 * index + 8) for index in range(4)]
    rest = jnp.zeros((8, LANES - 32), jnp.float32)
    blank = jnp.zeros((8, LANES), jnp.float32)

    def row_of(block):
        def row(index):
            if index < T_SHARED:
                value = shared_ref[pl.ds(index * blocks + block, 1), :]
            else:
                value = table[pl.ds((index - T_SHARED) * blocks + block, 1), :]
            return jnp.broadcast_to(value, (8, LANES))

        return row

    def block_sums(block):
        row = row_of(block)
        wy, wyd = axis_weights(row, T_LY, T_MY, T_RY, T_OY, T_Y)
        wz, wzd = axis_weights(row, T_LZ, T_MZ, T_RZ, T_OZ, T_Z)
        wx = [row(T_WX + node) for node in range(6)]
        wxd = [row(T_WXD + node) for node in range(6)]
        left_side = jnp.concatenate(
            [
                jnp.concatenate([w * wy for w in wx], axis=0),
                jnp.concatenate([w * wy for w in wxd], axis=0),
                jnp.concatenate([w * wyd for w in wx], axis=0),
            ],
            axis=1,
        )
        value_rows = [
            wz * row(T_MV + dim) + wzd * row(T_A + 3 * dim + 2) for dim in range(3)
        ] + [wz * row(T_MASS)]
        x_rows = [wz * row(T_A + 3 * dim) for dim in range(3)] + [blank]
        y_rows = [wz * row(T_A + 3 * dim + 1) for dim in range(3)] + [blank]
        right_side = jnp.concatenate(
            [jnp.concatenate(r, axis=0) for r in (value_rows, x_rows, y_rows)], axis=1
        )
        left_high, left_low = split(left_side)
        right_high, right_low = split(right_side)

        return lax.dot_general(
            jnp.concatenate([left_high, left_high, left_low], axis=1),
            jnp.concatenate([right_high, right_low, right_high], axis=1),
            (((1,), (1,)), ((), ())),
            preferred_element_type=jnp.float32,
        )

    starts = (0, PITCH - 8, 2 * PITCH - 16, LANES - 24)

    def group_place(step, sums):
        rows = pl.ds(pl.multiple_of(step * 8 * GROUP, 8 * GROUP), 8 * GROUP)
        heights = [4 * (tile_ref[step * GROUP + member] & 7) for member in range(GROUP)]
        for node in range(6):
            mom_rows, mass_rows = [], []
            for member in range(GROUP):
                part = sums[member][8 * node : 8 * node + 8]
                moved = [
                    pltpu.roll(
                        jnp.concatenate([jnp.where(channel[index], part, 0.0), rest], axis=1),
                        starts[index] + heights[member],
                        axis=1,
                    )
                    for index in range(4)
                ]
                mom_rows.append(moved[0] + moved[1] + moved[2])
                mass_rows.append(moved[3])
            for column, values in enumerate((mom_rows, mass_rows)):
                high, low = split(jnp.concatenate(values, axis=0))
                cols = slice(column * LANES, (column + 1) * LANES)
                placed_high[node, rows, cols] = high
                placed_low[node, rows, cols] = low

    def group_sums(step):
        return tuple(block_sums(step * GROUP + member) for member in range(GROUP))

    def group(step, sums):
        following = group_sums(step)
        group_place(step - 1, sums)
        return following

    steps = blocks // GROUP
    group_place(steps - 1, lax.fori_loop(1, steps, group, group_sums(0)))

    spots = 8 * blocks
    spot = lax.broadcasted_iota(jnp.int32, (8, spots), 1)
    owner = spot >> 3
    tiles = jnp.zeros((8, spots), jnp.int32)
    for block in range(blocks):
        tiles = jnp.where(owner == block, tile_ref[block], tiles)
    target = ((tiles >> 7) << 10) + (((tiles >> 3) & 15) << 2) + (spot & 7)
    y_row = lax.broadcasted_iota(jnp.int32, (8, spots), 0)
    chooser = jnp.concatenate(
        [
            jnp.where(target == y_row + (1024 * tile_x + start), 1.0, 0.0)
            for tile_x in range(CX // 4)
            for start in range(0, PY, 8)
        ],
        axis=0,
    ).astype(jnp.bfloat16)
    for node in range(6):
        layers = jnp.dot(
            chooser, placed_high[node], preferred_element_type=jnp.float32
        ) + jnp.dot(chooser, placed_low[node], preferred_element_type=jnp.float32)
        for tile_x in range(CX // 4):
            part = layers[tile_x * PY : (tile_x + 1) * PY]
            x = 4 * tile_x + node
            at = slice(x * PY, (x + 1) * PY)
            if node < 4 or x >= CX:
                mom[at, :] = part[:, :LANES]
                mass[at, :] = part[:, LANES:]
            else:
                mom[at, :] += part[:, :LANES]
                mass[at, :] += part[:, LANES:]

    def copy(src, dst, slot, target):
        return pltpu.make_async_remote_copy(
            src_ref=src,
            dst_ref=dst,
            send_sem=send_sem.at[slot],
            recv_sem=recv_sem.at[slot],
            device_id=target,
            device_id_type=MESH,
        )

    lane = lax.broadcasted_iota(jnp.int32, (PY, LANES), 1)
    in_mom = lane < 3 * PITCH
    in_pitch = lax.rem(lane, PITCH)
    third = PY // 3
    lane3 = lane[:third]
    pl.semaphore_wait(barrier, 14)

    firsts = (0, CX * PY)
    used = CY + 2
    short = used // 3
    for side in range(2):
        for layer in range(2):
            start = firsts[side] + layer * PY
            x_send[side, layer * used : (layer + 1) * used, :] = mom[start : start + used, :]
            at = 2 * used + layer * short
            x_send[side, at : at + short, :] = (
                mass[start : start + short, :]
                + pltpu.roll(mass[start + short : start + 2 * short, :], PITCH, axis=1)
                + pltpu.roll(mass[start + 2 * short : start + 3 * short, :], 2 * PITCH, axis=1)
            )
    x_copies = [
        copy(x_send.at[side], x_recv.at[1 - side], 2 + side, x_sides[side]) for side in range(2)
    ]
    for c in x_copies:
        c.start()

    pair = jnp.where(in_mom, in_pitch >> 1, -1)
    far = lax.rem(lane + (LANES - CZ), LANES)
    far_pair = jnp.where(far < 3 * PITCH, lax.rem(far, PITCH) >> 1, -1)
    pair3 = lane3 >> 1
    far_pair3 = far[:third] >> 1
    outer = (0, CY)
    groups = (8, 8 + third, PY - third)

    def pick(values, start, x, whole):
        shift = start + 2 * x
        moved = pltpu.roll(values, shift, axis=1) if shift else values
        count = values.shape[0]
        sides = (pair, far_pair) if whole else (pair3, far_pair3)
        return [(side[:count] == shift // 2 if not whole else side[:count] == x, moved)
                for side in sides]

    def gather_pairs(pieces, whole):
        result = [None, None]
        for values, start, x in pieces:
            for side, (mask, moved) in enumerate(pick(values, start, x, whole)):
                before = 0.0 if result[side] is None else result[side]
                result[side] = jnp.where(mask, moved, before)
        return result

    def layer_rows(grid, x, first, count):
        return grid[x * PY + first : x * PY + first + count, :]

    def z_start(send, recv, slot):
        copies = [
            copy(send.at[side], recv.at[1 - side], slot + side, z_sides[side])
            for side in range(2)
        ]
        for c in copies:
            c.start()
        return copies

    for index, first in enumerate(outer):
        packed = gather_pairs([(layer_rows(mom, x, first, 8), 0, x) for x in range(PX)], True)
        for side in range(2):
            za_send[side, 8 * index : 8 * index + 8, :] = packed[side]
    packed = gather_pairs(
        [
            (layer_rows(mass, x, first, 8), PITCH * index, x)
            for index, first in enumerate(outer)
            for x in range(PX)
        ],
        False,
    )
    for side in range(2):
        za_send[side, 16:, :] = packed[side]
    za_copies = z_start(za_send, za_recv, 0)

    packed = gather_pairs([(layer_rows(mom, x, 8, CY - 8), 0, x) for x in range(PX)], True)
    packed_mass = gather_pairs(
        [
            (layer_rows(mass, x, first, third), PITCH * index, x)
            for index, first in enumerate(groups)
            for x in range(PX)
        ],
        False,
    )
    for side in range(2):
        zb_send[side, : CY - 8, :] = packed[side]
        zb_send[side, CY - 8 :, :] = packed_mass[side]
    zb_copies = z_start(zb_send, zb_recv, 14)

    quad = lax.broadcasted_iota(jnp.int32, (8, LANES), 1) >> 2
    for edge in range(4):
        x0, z_side = CX * (edge // 2), edge % 2
        result = [None, None]
        for tile in range(PY // 8):
            half, start = tile // 8, 16 * (tile % 8)
            if 8 * tile in outer:
                z_buffer, mom_at, mass_at = za_send, tile, 16
                mass_group = outer.index(8 * tile)
            else:
                mass_group = min((tile - 1) // 3, 2)
                z_buffer, mom_at = zb_send, 8 * (tile - 1)
                mass_at = CY - 8 + 8 * tile - groups[mass_group]
            rows = z_buffer[z_side, mom_at : mom_at + 8, :]
            mass_rows = z_buffer[z_side, mass_at : mass_at + 8, :]
            for index in range(4):
                if index < 3:
                    source, at = rows, PITCH * index + 2 * x0 + CZ * z_side
                else:
                    source, at = mass_rows, PITCH * mass_group + 2 * x0 + CZ * z_side
                to = start + 4 * index
                moved = pltpu.roll(source, (2 * LANES + to - at) % LANES, axis=1)
                if result[half] is None:
                    result[half] = moved
                else:
                    result[half] = jnp.where(quad == to // 4, moved, result[half])
        xz_send[edge, :8, :] = result[0]
        xz_send[edge, 8:, :] = result[1]
    xz_copies = [
        copy(xz_send.at[edge], xz_recv.at[3 - edge], 6 + edge, xz_sides[edge])
        for edge in range(4)
    ]
    for c in xz_copies:
        c.start()

    rim = in_mom & ((in_pitch < 2) | ((in_pitch >= CZ) & (in_pitch < CZ + 2)))
    rim3 = (lane3 < 2) | ((lane3 >= CZ) & (lane3 < CZ + 2))

    def spread(grid, x, first, count, received, start, whole):
        low, high = received
        mask = pair[:count] == x if whole else pair3[:count] == start // 2 + x
        moved = pltpu.roll(
            jnp.where(mask, high, low), (2 * LANES + CZ - start - 2 * x) % LANES, axis=1
        )
        at = slice(x * PY + first, x * PY + first + count)
        grid[at, :] += jnp.where((rim if whole else rim3)[:count], moved, 0.0)

    for c in za_copies:
        c.wait()
    received = pltpu.roll(za_recv[0], 64, axis=1), za_recv[1]
    for x in range(PX):
        for index, first in enumerate(outer):
            rows = slice(8 * index, 8 * index + 8)
            spread(mom, x, first, 8, [side[rows] for side in received], 0, True)
            spread(mass, x, first, 8, [side[16:] for side in received], PITCH * index, False)

    y_firsts = (0, CY)
    for side in range(2):
        y0 = y_firsts[side]
        y_send[side, 0:PX, :] = mom[pl.ds(y0, PX, stride=PY), :]
        y_send[side, PX : 2 * PX, :] = mom[pl.ds(y0 + 1, PX, stride=PY), :]
        y_send[side, 2 * PX : 3 * PX, :] = mass[pl.ds(y0, PX, stride=PY), :] + pltpu.roll(
            mass[pl.ds(y0 + 1, PX, stride=PY), :], 64, axis=1
        )
        y_send[side, 3 * PX :, :] = jnp.zeros((2, LANES), jnp.float32)
    y_copies = [
        copy(y_send.at[side], y_recv.at[1 - side], 4 + side, y_sides[side]) for side in range(2)
    ]
    for edge in range(4):
        x0, y0 = CX * (edge // 2), y_firsts[edge % 2]
        for layer in range(2):
            at = (x0 + layer) * PY + y0
            xy_send[edge, 2 * layer : 2 * layer + 2, :] = mom[at : at + 2, :]
            xy_send[edge, 4 + 2 * layer : 6 + 2 * layer, :] = mass[at : at + 2, :]
        y_copies.append(copy(xy_send.at[edge], xy_recv.at[3 - edge], 10 + edge, xy_sides[edge]))
    for c in y_copies:
        c.start()

    for c in zb_copies:
        c.wait()
    received = pltpu.roll(zb_recv[0], 64, axis=1), zb_recv[1]
    for x in range(PX):
        spread(mom, x, 8, CY - 8, [side[: CY - 8] for side in received], 0, True)
        for index, first in enumerate(groups):
            skip = 0 if index < 2 else 8
            count = third if index < 2 else 8
            rows = slice(CY - 8 + skip, CY - 8 + skip + count)
            spread(
                mass, x, first + skip, count, [side[rows] for side in received],
                PITCH * index, False,
            )

    width_x = lax.axis_size("gx") * CX
    height_y = lax.axis_size("gy") * CY
    depth_z = lax.axis_size("gz") * CZ
    first_z = lax.axis_index("gz") * CZ
    first_y = lax.axis_index("gy") * CY
    first_x = lax.axis_index("gx") * CX
    z_index = lax.rem(lane - 2 * PITCH - 1 + first_z + depth_z, depth_z)
    is_y = (lane >= PITCH) & (lane < 2 * PITCH)
    is_z = (lane >= 2 * PITCH) & (lane < 3 * PITCH)
    z_floor = is_z & (z_index < 2)
    z_top = is_z & (z_index >= depth_z - 2)
    fall = jnp.where(is_y, time_step * gravity, 0.0)
    row_index = lax.broadcasted_iota(jnp.int32, (PY, LANES), 0)
    y_floor = is_y & (lax.rem(row_index - 1 + first_y + height_y, height_y) < 2)

    def update(mom_values, mass_values, floor, count):
        inverse = 1.0 / (mass_values + mass_floor)
        inverse = jnp.where(
            lane[:count] < PITCH,
            inverse,
            jnp.where(
                is_y[:count],
                pltpu.roll(inverse, PITCH, axis=1),
                pltpu.roll(inverse, 2 * PITCH, axis=1),
            ),
        )
        values = mom_values * inverse - fall[:count]
        values = jnp.where(z_floor[:count] | floor, jnp.maximum(values, 0.0), values)
        return jnp.where(z_top[:count], jnp.minimum(values, 0.0), values)

    def off_outlet(x):
        x_index = lax.rem(first_x + x - 1 + width_x, width_x)
        return (x_index < width_x // 4) | (x_index >= width_x - width_x // 4)

    def update_layer(x):
        at = pl.ds(pl.multiple_of(x * PY, 8), PY)
        velocity_out[at, :] = update(mom[at, :], mass[at, :], y_floor & off_outlet(x), PY)

    def layers(step, carry):
        for member in range(7):
            update_layer(2 + 7 * step + member)
        return carry

    lax.fori_loop(0, 2, layers, 0)

    def right_sides(step, carry):
        for member in range(2):
            block = 2 * step + member
            row = row_of(block)
            wz, wzd = axis_weights(row, T_LZ, T_MZ, T_RZ, T_OZ, T_Z)
            wx = [row(T_WX + node) for node in range(6)]
            wxd = [row(T_WXD + node) for node in range(6)]
            at = pl.ds(pl.multiple_of(48 * block, 16), 48)
            for index, (along_x, along_z) in enumerate(((wx, wz), (wxd, wz), (wx, wzd))):
                high, low = split(jnp.concatenate([w * along_z for w in along_x], axis=0))
                cols = slice(index * LANES, (index + 1) * LANES)
                collect_high[at, cols] = high
                collect_low[at, cols] = low
        return carry

    lax.fori_loop(0, blocks // 2, right_sides, 0)

    for c in xz_copies:
        c.wait()
    lane8 = lane[:8]
    for side in range(2):
        for layer in range(2):
            for tile in range(PY // 8):
                half, start = tile // 8, 16 * (tile % 8)
                mom_value, mass_value = 0.0, 0.0
                for z_side in range(2):
                    source = xz_recv[2 * side + z_side, 8 * half : 8 * half + 8, :]
                    for index in range(4):
                        to = (PITCH * index if index < 3 else 0) + CZ * z_side
                        at = start + 4 * index + 2 * layer
                        moved = pltpu.roll(source, (LANES + to - at) % LANES, axis=1)
                        here = (lane8 >= to) & (lane8 < to + 2)
                        if index < 3:
                            mom_value = jnp.where(here, moved, mom_value)
                        else:
                            mass_value = jnp.where(here, moved, mass_value)
                at = firsts[side] + layer * PY + 8 * tile
                mom[at : at + 8, :] += mom_value
                mass[at : at + 8, :] += mass_value

    for c in x_copies:
        c.wait()
    near = lane[:short] < PITCH
    for side in range(2):
        for layer in range(2):
            start = firsts[side] + layer * PY
            mom[start : start + used, :] += x_recv[side, layer * used : (layer + 1) * used, :]
            at = 2 * used + layer * short
            got = x_recv[side, at : at + short, :]
            for part in range(3):
                first = start + part * short
                moved = pltpu.roll(got, LANES - PITCH * part, axis=1) if part else got
                mass[first : first + short, :] += jnp.where(near, moved, 0.0)
    for x in (0, 1, CX, CX + 1):
        update_layer(x)
    front = lane < 64
    for c in y_copies:
        c.wait()
    for side in range(2):
        y0 = y_firsts[side]
        got = y_recv[side, 2 * PX : 3 * PX, :]
        at0 = pl.ds(y0, PX, stride=PY)
        at1 = pl.ds(y0 + 1, PX, stride=PY)
        mom[at0, :] = mom[at0, :] + y_recv[side, 0:PX, :]
        mom[at1, :] = mom[at1, :] + y_recv[side, PX : 2 * PX, :]
        mass[at0, :] = mass[at0, :] + jnp.where(front[:PX], got, 0.0)
        mass[at1, :] = mass[at1, :] + jnp.where(front[:PX], pltpu.roll(got, 64, axis=1), 0.0)
    for edge in range(4):
        x0, y0 = CX * (edge // 2), y_firsts[edge % 2]
        for layer in range(2):
            at = (x0 + layer) * PY + y0
            mom[at : at + 2, :] += xy_recv[edge, 2 * layer : 2 * layer + 2, :]
            mass[at : at + 2, :] += xy_recv[edge, 4 + 2 * layer : 6 + 2 * layer, :]
    x_rows = lax.broadcasted_iota(jnp.int32, (PX, LANES), 0)
    outside = off_outlet(x_rows)
    for y in (0, 1, CY, CY + 1):
        at = pl.ds(y, PX, stride=PY)
        on_floor = lax.rem(first_y + (y - 1 + height_y), height_y) < 2
        velocity_out[at, :] = update(
            mom[at, :], mass[at, :], is_y[:PX] & outside & on_floor, PX
        )


def collect_kernel(
    tile_hbm,
    velocity,
    right_high,
    right_low,
    y_table,
    stress_in,
    new_velocity_ref,
    new_affine_ref,
    new_stress_hbm,
    grid_velocity_hbm,
    tile_ref,
    new_stress_ref,
    grid_velocity_ref,
    partial,
    final,
    copy_sem,
):
    blocks = tile_hbm.shape[0]
    tile_copy = pltpu.make_async_copy(tile_hbm, tile_ref, copy_sem.at[0])
    tile_copy.start()
    for block in range(blocks):
        new_stress_ref[:, block * BLOCK : (block + 1) * BLOCK] = stress_in[
            pl.ds(block, 6, stride=blocks), :
        ]
    stress_copy = pltpu.make_async_copy(new_stress_ref, new_stress_hbm, copy_sem.at[1])
    stress_copy.start()
    def output(step, carry):
        for member in range(4):
            x = 4 * step + member
            turned = jnp.transpose(velocity[pl.ds((x + 1) * PY + 1, CY), :])
            for dim in range(3):
                grid_velocity_ref[dim, x] = turned[PITCH * dim + 1 : PITCH * dim + 1 + CZ]
        return carry

    lax.fori_loop(0, CX // 4, output, 0)
    grid_copy = pltpu.make_async_copy(grid_velocity_ref, grid_velocity_hbm, copy_sem.at[2])
    grid_copy.start()
    tile_copy.wait()

    lanes = lax.broadcasted_iota(jnp.int32, (8, LANES), 1)

    def gather(block):
        tile_x, tile_y, tile_z = tile_coords(tile_ref, block)
        planes = []
        for node in range(6):
            at = pl.ds(pl.multiple_of((4 * tile_x + node) * PY + 4 * tile_y, 4), 8)
            planes.append(velocity[at, :])
        rows = []
        for dim in range(3):
            merged = None
            for node in range(6):
                moved = pltpu.roll(
                    planes[node],
                    LANES + 8 * node - PITCH * dim - 4 * tile_z,
                    axis=1,
                )
                merged = moved if merged is None else jnp.where(lanes < 8 * node, merged, moved)
            rows.append(merged)
        return jnp.concatenate(rows, axis=0)

    def contract(block, left_side):
        left_high, left_low = split(left_side[:, :48])
        at = pl.ds(pl.multiple_of(48 * block, 16), 48)
        both = jnp.dot(
            jnp.concatenate([left_high, left_low], axis=0),
            right_high[at, :],
            preferred_element_type=jnp.float32,
        )
        return (
            both[:24]
            + both[24:]
            + jnp.dot(left_high, right_low[at, :], preferred_element_type=jnp.float32)
        )

    def weigh(block, sums):
        def row(index):
            return jnp.broadcast_to(y_table[pl.ds(index * blocks + block, 1), :], (8, LANES))

        wy, wyd = axis_weights(row, 0, 1, 2, 3, 4)
        for dim in range(3):
            part = sums[8 * dim : 8 * dim + 8]
            terms = (
                (dim, wy * part[:, :128]),
                (3 + 3 * dim, wy * part[:, 128:256]),
                (4 + 3 * dim, wyd * part[:, :128]),
                (5 + 3 * dim, wy * part[:, 256:]),
            )
            for component, value in terms:
                at = pl.ds(pl.multiple_of(component * 8 * blocks + 8 * block, 8), 8)
                partial[at, :] = value

    def of_group(function, step, *values):
        return tuple(
            function(step * GROUP + member, *(value[member] for value in values))
            for member in range(GROUP)
        )

    def group(step, carry):
        left_sides, sums = carry
        following = of_group(gather, step + 2)
        products = of_group(contract, step + 1, left_sides)
        of_group(weigh, step, sums)
        return following, products

    steps = blocks // GROUP
    carry = of_group(gather, 1), of_group(contract, 0, of_group(gather, 0))
    left_sides, sums = lax.fori_loop(0, steps - 2, group, carry)
    of_group(weigh, steps - 2, sums)
    of_group(weigh, steps - 1, of_group(contract, steps - 1, left_sides))
    for component in range(12):
        total = partial[pl.ds(component * 8 * blocks, blocks, stride=8), :]
        for node in range(1, 6):
            total = total + partial[pl.ds(component * 8 * blocks + node, blocks, stride=8), :]
        if component >= 3:
            total = 4.0 * total
        final[component * blocks : (component + 1) * blocks, :] = total
    for block in range(blocks):
        cols = slice(block * BLOCK, (block + 1) * BLOCK)
        new_velocity_ref[:, cols] = final[pl.ds(block, 3, stride=blocks), :]
        new_affine_ref[:, cols] = final[pl.ds(3 * blocks + block, 9, stride=blocks), :]
    stress_copy.wait()
    grid_copy.wait()


def shards(
    point_frac,
    cell_offset,
    point_velocity,
    point_affine,
    point_stress,
    point_mass,
    block_tile,
    block_count,
):
    blocks = block_tile.shape[0]
    points = blocks * BLOCK
    vmem = pl.BlockSpec(memory_space=pltpu.VMEM)
    hbm = pl.BlockSpec(memory_space=pltpu.HBM)
    f32 = jnp.float32
    grid_shape = jax.ShapeDtypeStruct((ROWS, LANES), f32)
    face = PY + PY // 3
    arguments = [
        pltpu.with_memory_space_constraint(value, pltpu.HBM)
        for value in (
            block_tile,
            block_count,
            point_frac,
            cell_offset,
            point_velocity,
            point_affine,
            point_stress,
            point_mass.reshape(blocks, BLOCK),
        )
    ]
    right_shape = jax.ShapeDtypeStruct((48 * blocks, 3 * LANES), jnp.bfloat16)
    velocity, right_high, right_low, y_table, stress = pl.pallas_call(
        deposit_kernel,
        name="deposit",
        out_shape=(
            grid_shape,
            right_shape,
            right_shape,
            jax.ShapeDtypeStruct((5 * blocks, LANES), f32),
            jax.ShapeDtypeStruct((6 * blocks, LANES), f32),
        ),
        in_specs=[hbm] * 8,
        out_specs=(vmem,) * 5,
        scratch_shapes=[
            pltpu.VMEM((ROWS, LANES), f32),
            pltpu.VMEM((ROWS, LANES), f32),
            pltpu.VMEM((T_SHARED * blocks, LANES), f32),
            pltpu.SMEM((blocks,), jnp.int32),
            pltpu.SMEM((blocks,), jnp.int32),
            pltpu.VMEM((3, points), f32),
            pltpu.VMEM((3, points), jnp.int32),
            pltpu.VMEM((3, points), f32),
            pltpu.VMEM((9, points), f32),
            pltpu.VMEM((6, points), f32),
            pltpu.VMEM((blocks, BLOCK), f32),
            pltpu.VMEM((48 * blocks, LANES), f32),
            pltpu.VMEM(((T_ALL - T_SHARED) * blocks, LANES), f32),
            pltpu.VMEM((6, 8 * blocks, 2 * LANES), jnp.bfloat16),
            pltpu.VMEM((6, 8 * blocks, 2 * LANES), jnp.bfloat16),
            pltpu.VMEM((2, 24, LANES), f32),
            pltpu.VMEM((2, 24, LANES), f32),
            pltpu.VMEM((2, CY - 8 + PY // 3, LANES), f32),
            pltpu.VMEM((2, CY - 8 + PY // 3, LANES), f32),
            pltpu.VMEM((2, 8 * (CY + 2) // 3, LANES), f32),
            pltpu.VMEM((2, 8 * (CY + 2) // 3, LANES), f32),
            pltpu.VMEM((4, 16, LANES), f32),
            pltpu.VMEM((4, 16, LANES), f32),
            pltpu.VMEM((2, 3 * PX + 2, LANES), f32),
            pltpu.VMEM((2, 3 * PX + 2, LANES), f32),
            pltpu.VMEM((4, 8, LANES), f32),
            pltpu.VMEM((4, 8, LANES), f32),
            pltpu.SemaphoreType.DMA((8,)),
            pltpu.SemaphoreType.DMA((16,)),
            pltpu.SemaphoreType.DMA((16,)),
        ],
        compiler_params=pltpu.CompilerParams(
            collective_id=0, has_side_effects=True, vmem_limit_bytes=VMEM_LIMIT
        ),
    )(*arguments)
    new_velocity, new_affine, new_stress, grid_velocity = pl.pallas_call(
        collect_kernel,
        name="collect",
        out_shape=(
            jax.ShapeDtypeStruct((3, points), f32),
            jax.ShapeDtypeStruct((9, points), f32),
            jax.ShapeDtypeStruct((6, points), f32),
            jax.ShapeDtypeStruct((3, CX, CZ, CY), f32),
        ),
        in_specs=[hbm] + [vmem] * 5,
        out_specs=(vmem, vmem, hbm, hbm),
        scratch_shapes=[
            pltpu.SMEM((blocks,), jnp.int32),
            pltpu.VMEM((6, points), f32),
            pltpu.VMEM((3, CX, CZ, CY), f32),
            pltpu.VMEM((12 * 8 * blocks, LANES), f32),
            pltpu.VMEM((12 * blocks, LANES), f32),
            pltpu.SemaphoreType.DMA((3,)),
        ],
        compiler_params=pltpu.CompilerParams(vmem_limit_bytes=VMEM_LIMIT),
    )(arguments[0], velocity, right_high, right_low, y_table, stress)
    return (new_velocity, new_affine, new_stress, jnp.swapaxes(grid_velocity, 2, 3))


def solution(mesh):
    points = P(None, ("gx", "gy", "gz"))
    flat = P(("gx", "gy", "gz"))
    return jax.shard_map(
        shards,
        mesh=mesh,
        in_specs=(points,) * 5 + (flat,) * 3,
        out_specs=(points, points, points, P(None, "gx", "gy", "gz")),
        check_vma=False,
    )
```

```python
import jax
import jax.numpy as jnp
from jax import lax
from jax.experimental import pallas as pl
from jax.experimental.pallas import tpu as pltpu
from jax.sharding import PartitionSpec as P

CX = 16
CY = 64
CZ = 32
BLOCK = 128

time_step = 0.1
gravity = 1.0
shear_modulus = 2.0
bulk_modulus = 4.0
friction_static = 0.38
friction_limit = 0.64
inertial_ref = 0.28
grain_size = 0.5
grain_density = 1.0
pressure_floor = 0.5
shear_floor = 0.5
mass_floor = 0.05
stress_scale = 0.4
pair_index = ((0, 5, 4), (5, 1, 3), (4, 3, 2))
component_pairs = ((0, 0), (1, 1), (2, 2), (1, 2), (0, 2), (0, 1))

PX = CX + 2
PY = 72
PITCH = 40
LANES = 128
ROWS = PX * PY
GROUP = 16
VMEM_LIMIT = 16 * 1024 * 1024
MESH = pl.DeviceIdType.MESH

T_WX, T_WXD = 0, 6
T_LY, T_MY, T_RY, T_OY, T_Y = 12, 13, 14, 15, 16
T_LZ, T_MZ, T_RZ, T_OZ, T_Z = 17, 18, 19, 20, 21
T_SHARED = 22
T_MASS, T_MV, T_A = 22, 23, 26
T_ALL = 35


def stress_update(stress, affine):
    strain_rate = [
        [
            0.5 * (affine[3 * row_dim + col_dim] + affine[3 * col_dim + row_dim])
            for col_dim in range(3)
        ]
        for row_dim in range(3)
    ]
    volume_rate = strain_rate[0][0] + strain_rate[1][1] + strain_rate[2][2]
    deviator = [
        [
            strain_rate[row_dim][col_dim] - (volume_rate / 3.0 if row_dim == col_dim else 0.0)
            for col_dim in range(3)
        ]
        for row_dim in range(3)
    ]
    trial_stress = []
    for component in range(6):
        row_dim, col_dim = component_pairs[component]
        value = stress[component] + time_step * 2.0 * shear_modulus * deviator[row_dim][col_dim]
        if component < 3:
            value = value + time_step * bulk_modulus * volume_rate
        trial_stress.append(value)
    pressure = -(trial_stress[0] + trial_stress[1] + trial_stress[2]) / 3.0
    shear_part = [trial_stress[component] + pressure for component in range(3)] + trial_stress[3:]
    shear_stress = jnp.sqrt(
        0.5 * (shear_part[0] ** 2 + shear_part[1] ** 2 + shear_part[2] ** 2)
        + shear_part[3] ** 2
        + shear_part[4] ** 2
        + shear_part[5] ** 2
    )
    shear_rate = jnp.sqrt(
        2.0
        * (
            deviator[0][0] ** 2
            + deviator[1][1] ** 2
            + deviator[2][2] ** 2
            + 2.0 * (deviator[1][2] ** 2 + deviator[0][2] ** 2 + deviator[0][1] ** 2)
        )
    )
    inertial = (
        shear_rate * grain_size / jnp.sqrt(jnp.maximum(pressure, pressure_floor) / grain_density)
    )
    friction = friction_static + (friction_limit - friction_static) * inertial / (
        inertial_ref + inertial
    )
    support = jnp.maximum(pressure, 0.0)
    factor = jnp.minimum(1.0, friction * support / jnp.maximum(shear_stress, shear_floor))
    return [shear_part[component] * factor - support for component in range(3)] + [
        shear_part[component] * factor for component in range(3, 6)
    ]


def split(values):
    high = values.astype(jnp.bfloat16)
    low = (values - high.astype(jnp.float32)).astype(jnp.bfloat16)
    return high, low


def tile_coords(tile_ref, block):
    tile = tile_ref[block]
    return tile >> 7, (tile >> 3) & 15, tile & 7


def axis_weights(row, left, middle, right, offset, position):
    index = lax.broadcasted_iota(jnp.int32, (8, LANES), 0).astype(jnp.float32)
    shifted = index - row(offset)
    weight = jnp.where(
        shifted == 0.0,
        row(left),
        jnp.where(shifted == 1.0, row(middle), jnp.where(shifted == 2.0, row(right), 0.0)),
    )
    return weight, weight * (index - row(position))


def deposit_kernel(
    tile_hbm,
    count_hbm,
    frac_hbm,
    offset_hbm,
    velocity_hbm,
    affine_hbm,
    stress_hbm,
    mass_hbm,
    velocity_out,
    collect_high,
    collect_low,
    y_table,
    new_stress,
    mom,
    mass,
    shared_ref,
    stress_out,
    tile_ref,
    count_ref,
    frac_ref,
    offset_ref,
    velocity_ref,
    affine_ref,
    stress_ref,
    mass_ref,
    gathered,
    table,
    placed_high,
    placed_low,
    za_send,
    za_recv,
    zb_send,
    zb_recv,
    x_send,
    x_recv,
    xz_send,
    xz_recv,
    y_send,
    y_recv,
    xy_send,
    xy_recv,
    load_sem,
    send_sem,
    recv_sem,
):
    axes = ("gx", "gy", "gz")

    def device(dx, dy, dz):
        place = []
        for axis, step in zip(axes, (dx, dy, dz)):
            size = lax.axis_size(axis)
            moved = lax.axis_index(axis)
            if step and size & (size - 1) == 0:
                moved = (moved + size + step) & (size - 1)
            elif step:
                moved = lax.rem(moved + size + step, size)
            place.append(moved)
        return tuple(place)

    loads = [
        pltpu.make_async_copy(source, target, load_sem.at[index])
        for index, (source, target) in enumerate(
            (
                (frac_hbm, frac_ref),
                (offset_hbm, offset_ref),
                (velocity_hbm, velocity_ref),
                (affine_hbm, affine_ref),
                (stress_hbm, stress_ref),
                (mass_hbm, mass_ref),
                (count_hbm, count_ref),
                (tile_hbm, tile_ref),
            )
        )
    ]
    for load in loads:
        load.start()
    z_sides = [device(0, 0, -1), device(0, 0, 1)]
    x_sides = [device(-1, 0, 0), device(1, 0, 0)]
    y_sides = [device(0, -1, 0), device(0, 1, 0)]
    xz_sides = [device(dx, 0, dz) for dx in (-1, 1) for dz in (-1, 1)]
    xy_sides = [device(dx, dy, 0) for dx in (-1, 1) for dy in (-1, 1)]
    barrier = pltpu.get_barrier_semaphore()
    for target in z_sides + x_sides + xz_sides + y_sides + xy_sides:
        pl.semaphore_signal(barrier, inc=1, device_id=target, device_id_type=MESH)

    blocks = mass_ref.shape[0]
    lane_row = lax.broadcasted_iota(jnp.int32, (1, LANES), 1)
    stride = 48
    for load in loads:
        load.wait()
    for block in range(blocks):
        cols = slice(block * BLOCK, (block + 1) * BLOCK)
        at = block * stride
        gathered[at : at + 3, :] = frac_ref[:, cols]
        gathered[at + 8 : at + 11, :] = offset_ref[:, cols].astype(jnp.float32)
        gathered[at + 16 : at + 19, :] = velocity_ref[:, cols]
        gathered[at + 24 : at + 33, :] = affine_ref[:, cols]
        gathered[at + 40 : at + 46, :] = stress_ref[:, cols]
        row = (T_MASS - T_SHARED) * blocks + block
        table[row : row + 1, :] = jnp.where(
            lane_row < count_ref[block], mass_ref[block : block + 1, :], 0.0
        )

    def dense(component):
        return gathered[pl.ds(component, blocks, stride=stride), :]

    def put(index, value):
        if index < T_SHARED:
            shared_ref[index * blocks : (index + 1) * blocks, :] = value
        else:
            start = (index - T_SHARED) * blocks
            table[start : start + blocks, :] = value

    affine = [dense(24 + component) for component in range(9)]
    stress = stress_update([dense(40 + component) for component in range(6)], affine)
    for component in range(6):
        stress_out[component * blocks : (component + 1) * blocks, :] = stress[component]
    live_mass = table[(T_MASS - T_SHARED) * blocks : (T_MASS - T_SHARED + 1) * blocks, :]
    for row_dim in range(3):
        put(T_MV + row_dim, live_mass * dense(16 + row_dim))
        for col_dim in range(3):
            put(
                T_A + 3 * row_dim + col_dim,
                live_mass
                * (
                    affine[3 * row_dim + col_dim]
                    - stress_scale * stress[pair_index[row_dim][col_dim]]
                ),
            )
    spline = []
    for dim in range(3):
        fraction = dense(dim)
        spline.append(
            (
                0.5 * (1.5 - fraction) ** 2,
                0.75 - (fraction - 1.0) ** 2,
                0.5 * (fraction - 0.5) ** 2,
                dense(8 + dim),
                dense(8 + dim) + fraction,
            )
        )
    left, middle, right, offset, position = spline[0]
    for node in range(6):
        shifted = float(node) - offset
        weight = jnp.where(
            shifted == 0.0,
            left,
            jnp.where(shifted == 1.0, middle, jnp.where(shifted == 2.0, right, 0.0)),
        )
        put(T_WX + node, weight)
        put(T_WXD + node, weight * (float(node) - position))
    for index in range(5):
        put(T_LY + index, spline[1][index])
        put(T_LZ + index, spline[2][index])
        y_table[index * blocks : (index + 1) * blocks, :] = spline[1][index]

    lanes = lax.broadcasted_iota(jnp.int32, (8, 32), 1)
    channel = [(lanes >= 8 * index) & (lanes < 8 * index + 8) for index in range(4)]
    rest = jnp.zeros((8, LANES - 32), jnp.float32)
    blank = jnp.zeros((8, LANES), jnp.float32)

    def row_of(block):
        def row(index):
            if index < T_SHARED:
                value = shared_ref[pl.ds(index * blocks + block, 1), :]
            else:
                value = table[pl.ds((index - T_SHARED) * blocks + block, 1), :]
            return jnp.broadcast_to(value, (8, LANES))

        return row

    def block_sums(block):
        row = row_of(block)
        wy, wyd = axis_weights(row, T_LY, T_MY, T_RY, T_OY, T_Y)
        wz, wzd = axis_weights(row, T_LZ, T_MZ, T_RZ, T_OZ, T_Z)
        wx = [row(T_WX + node) for node in range(6)]
        wxd = [row(T_WXD + node) for node in range(6)]
        left_side = jnp.concatenate(
            [
                jnp.concatenate([w * wy for w in wx], axis=0),
                jnp.concatenate([w * wy for w in wxd], axis=0),
                jnp.concatenate([w * wyd for w in wx], axis=0),
            ],
            axis=1,
        )
        value_rows = [
            wz * row(T_MV + dim) + wzd * row(T_A + 3 * dim + 2) for dim in range(3)
        ] + [wz * row(T_MASS)]
        x_rows = [wz * row(T_A + 3 * dim) for dim in range(3)] + [blank]
        y_rows = [wz * row(T_A + 3 * dim + 1) for dim in range(3)] + [blank]
        right_side = jnp.concatenate(
            [jnp.concatenate(r, axis=0) for r in (value_rows, x_rows, y_rows)], axis=1
        )
        left_high, left_low = split(left_side)
        right_high, right_low = split(right_side)

        return lax.dot_general(
            jnp.concatenate([left_high, left_high, left_low], axis=1),
            jnp.concatenate([right_high, right_low, right_high], axis=1),
            (((1,), (1,)), ((), ())),
            preferred_element_type=jnp.float32,
        )

    starts = (0, PITCH - 8, 2 * PITCH - 16, LANES - 24)

    def group_place(step, sums):
        rows = pl.ds(pl.multiple_of(step * 8 * GROUP, 8 * GROUP), 8 * GROUP)
        heights = [4 * (tile_ref[step * GROUP + member] & 7) for member in range(GROUP)]
        for node in range(6):
            mom_rows, mass_rows = [], []
            for member in range(GROUP):
                part = sums[member][8 * node : 8 * node + 8]
                moved = [
                    pltpu.roll(
                        jnp.concatenate([jnp.where(channel[index], part, 0.0), rest], axis=1),
                        starts[index] + heights[member],
                        axis=1,
                    )
                    for index in range(4)
                ]
                mom_rows.append(moved[0] + moved[1] + moved[2])
                mass_rows.append(moved[3])
            for column, values in enumerate((mom_rows, mass_rows)):
                high, low = split(jnp.concatenate(values, axis=0))
                cols = slice(column * LANES, (column + 1) * LANES)
                placed_high[node, rows, cols] = high
                placed_low[node, rows, cols] = low

    def group_sums(step):
        return tuple(block_sums(step * GROUP + member) for member in range(GROUP))

    def group(step, sums):
        following = group_sums(step)
        group_place(step - 1, sums)
        return following

    steps = blocks // GROUP
    group_place(steps - 1, lax.fori_loop(1, steps, group, group_sums(0)))

    spots = 8 * blocks
    spot = lax.broadcasted_iota(jnp.int32, (8, spots), 1)
    owner = spot >> 3
    tiles = jnp.zeros((8, spots), jnp.int32)
    for block in range(blocks):
        tiles = jnp.where(owner == block, tile_ref[block], tiles)
    target = ((tiles >> 7) << 10) + (((tiles >> 3) & 15) << 2) + (spot & 7)
    y_row = lax.broadcasted_iota(jnp.int32, (8, spots), 0)
    chooser = jnp.concatenate(
        [
            jnp.where(target == y_row + (1024 * tile_x + start), 1.0, 0.0)
            for tile_x in range(CX // 4)
            for start in range(0, PY, 8)
        ],
        axis=0,
    ).astype(jnp.bfloat16)
    for node in range(6):
        layers = jnp.dot(
            chooser, placed_high[node], preferred_element_type=jnp.float32
        ) + jnp.dot(chooser, placed_low[node], preferred_element_type=jnp.float32)
        for tile_x in range(CX // 4):
            part = layers[tile_x * PY : (tile_x + 1) * PY]
            x = 4 * tile_x + node
            at = slice(x * PY, (x + 1) * PY)
            if node < 4 or x >= CX:
                mom[at, :] = part[:, :LANES]
                mass[at, :] = part[:, LANES:]
            else:
                mom[at, :] += part[:, :LANES]
                mass[at, :] += part[:, LANES:]

    def copy(src, dst, slot, target):
        return pltpu.make_async_remote_copy(
            src_ref=src,
            dst_ref=dst,
            send_sem=send_sem.at[slot],
            recv_sem=recv_sem.at[slot],
            device_id=target,
            device_id_type=MESH,
        )

    lane = lax.broadcasted_iota(jnp.int32, (PY, LANES), 1)
    in_mom = lane < 3 * PITCH
    in_pitch = lax.rem(lane, PITCH)
    third = PY // 3
    lane3 = lane[:third]
    pl.semaphore_wait(barrier, 14)

    firsts = (0, CX * PY)
    used = CY + 2
    short = used // 3
    for side in range(2):
        for layer in range(2):
            start = firsts[side] + layer * PY
            x_send[side, layer * used : (layer + 1) * used, :] = mom[start : start + used, :]
            at = 2 * used + layer * short
            x_send[side, at : at + short, :] = (
                mass[start : start + short, :]
                + pltpu.roll(mass[start + short : start + 2 * short, :], PITCH, axis=1)
                + pltpu.roll(mass[start + 2 * short : start + 3 * short, :], 2 * PITCH, axis=1)
            )
    x_copies = [
        copy(x_send.at[side], x_recv.at[1 - side], 2 + side, x_sides[side]) for side in range(2)
    ]
    for c in x_copies:
        c.start()

    pair = jnp.where(in_mom, in_pitch >> 1, -1)
    far = lax.rem(lane + (LANES - CZ), LANES)
    far_pair = jnp.where(far < 3 * PITCH, lax.rem(far, PITCH) >> 1, -1)
    pair3 = lane3 >> 1
    far_pair3 = far[:third] >> 1
    outer = (0, CY)
    groups = (8, 8 + third, PY - third)

    def pick(values, start, x, whole):
        shift = start + 2 * x
        moved = pltpu.roll(values, shift, axis=1) if shift else values
        count = values.shape[0]
        sides = (pair, far_pair) if whole else (pair3, far_pair3)
        return [(side[:count] == shift // 2 if not whole else side[:count] == x, moved)
                for side in sides]

    def gather_pairs(pieces, whole):
        result = [None, None]
        for values, start, x in pieces:
            for side, (mask, moved) in enumerate(pick(values, start, x, whole)):
                before = 0.0 if result[side] is None else result[side]
                result[side] = jnp.where(mask, moved, before)
        return result

    def layer_rows(grid, x, first, count):
        return grid[x * PY + first : x * PY + first + count, :]

    def z_start(send, recv, slot):
        copies = [
            copy(send.at[side], recv.at[1 - side], slot + side, z_sides[side])
            for side in range(2)
        ]
        for c in copies:
            c.start()
        return copies

    for index, first in enumerate(outer):
        packed = gather_pairs([(layer_rows(mom, x, first, 8), 0, x) for x in range(PX)], True)
        for side in range(2):
            za_send[side, 8 * index : 8 * index + 8, :] = packed[side]
    packed = gather_pairs(
        [
            (layer_rows(mass, x, first, 8), PITCH * index, x)
            for index, first in enumerate(outer)
            for x in range(PX)
        ],
        False,
    )
    for side in range(2):
        za_send[side, 16:, :] = packed[side]
    za_copies = z_start(za_send, za_recv, 0)

    packed = gather_pairs([(layer_rows(mom, x, 8, CY - 8), 0, x) for x in range(PX)], True)
    packed_mass = gather_pairs(
        [
            (layer_rows(mass, x, first, third), PITCH * index, x)
            for index, first in enumerate(groups)
            for x in range(PX)
        ],
        False,
    )
    for side in range(2):
        zb_send[side, : CY - 8, :] = packed[side]
        zb_send[side, CY - 8 :, :] = packed_mass[side]
    zb_copies = z_start(zb_send, zb_recv, 14)

    quad = lax.broadcasted_iota(jnp.int32, (8, LANES), 1) >> 2
    for edge in range(4):
        x0, z_side = CX * (edge // 2), edge % 2
        result = [None, None]
        for tile in range(PY // 8):
            half, start = tile // 8, 16 * (tile % 8)
            if 8 * tile in outer:
                z_buffer, mom_at, mass_at = za_send, tile, 16
                mass_group = outer.index(8 * tile)
            else:
                mass_group = min((tile - 1) // 3, 2)
                z_buffer, mom_at = zb_send, 8 * (tile - 1)
                mass_at = CY - 8 + 8 * tile - groups[mass_group]
            rows = z_buffer[z_side, mom_at : mom_at + 8, :]
            mass_rows = z_buffer[z_side, mass_at : mass_at + 8, :]
            for index in range(4):
                if index < 3:
                    source, at = rows, PITCH * index + 2 * x0 + CZ * z_side
                else:
                    source, at = mass_rows, PITCH * mass_group + 2 * x0 + CZ * z_side
                to = start + 4 * index
                moved = pltpu.roll(source, (2 * LANES + to - at) % LANES, axis=1)
                if result[half] is None:
                    result[half] = moved
                else:
                    result[half] = jnp.where(quad == to // 4, moved, result[half])
        xz_send[edge, :8, :] = result[0]
        xz_send[edge, 8:, :] = result[1]
    xz_copies = [
        copy(xz_send.at[edge], xz_recv.at[3 - edge], 6 + edge, xz_sides[edge])
        for edge in range(4)
    ]
    for c in xz_copies:
        c.start()

    rim = in_mom & ((in_pitch < 2) | ((in_pitch >= CZ) & (in_pitch < CZ + 2)))
    rim3 = (lane3 < 2) | ((lane3 >= CZ) & (lane3 < CZ + 2))

    def spread(grid, x, first, count, received, start, whole):
        low, high = received
        mask = pair[:count] == x if whole else pair3[:count] == start // 2 + x
        moved = pltpu.roll(
            jnp.where(mask, high, low), (2 * LANES + CZ - start - 2 * x) % LANES, axis=1
        )
        at = slice(x * PY + first, x * PY + first + count)
        grid[at, :] += jnp.where((rim if whole else rim3)[:count], moved, 0.0)

    for c in za_copies:
        c.wait()
    received = pltpu.roll(za_recv[0], 64, axis=1), za_recv[1]
    for x in range(PX):
        for index, first in enumerate(outer):
            rows = slice(8 * index, 8 * index + 8)
            spread(mom, x, first, 8, [side[rows] for side in received], 0, True)
            spread(mass, x, first, 8, [side[16:] for side in received], PITCH * index, False)

    y_firsts = (0, CY)
    for side in range(2):
        y0 = y_firsts[side]
        y_send[side, 0:PX, :] = mom[pl.ds(y0, PX, stride=PY), :]
        y_send[side, PX : 2 * PX, :] = mom[pl.ds(y0 + 1, PX, stride=PY), :]
        y_send[side, 2 * PX : 3 * PX, :] = mass[pl.ds(y0, PX, stride=PY), :] + pltpu.roll(
            mass[pl.ds(y0 + 1, PX, stride=PY), :], 64, axis=1
        )
        y_send[side, 3 * PX :, :] = jnp.zeros((2, LANES), jnp.float32)
    y_copies = [
        copy(y_send.at[side], y_recv.at[1 - side], 4 + side, y_sides[side]) for side in range(2)
    ]
    for edge in range(4):
        x0, y0 = CX * (edge // 2), y_firsts[edge % 2]
        for layer in range(2):
            at = (x0 + layer) * PY + y0
            xy_send[edge, 2 * layer : 2 * layer + 2, :] = mom[at : at + 2, :]
            xy_send[edge, 4 + 2 * layer : 6 + 2 * layer, :] = mass[at : at + 2, :]
        y_copies.append(copy(xy_send.at[edge], xy_recv.at[3 - edge], 10 + edge, xy_sides[edge]))
    for c in y_copies:
        c.start()

    for c in zb_copies:
        c.wait()
    received = pltpu.roll(zb_recv[0], 64, axis=1), zb_recv[1]
    for x in range(PX):
        spread(mom, x, 8, CY - 8, [side[: CY - 8] for side in received], 0, True)
        for index, first in enumerate(groups):
            skip = 0 if index < 2 else 8
            count = third if index < 2 else 8
            rows = slice(CY - 8 + skip, CY - 8 + skip + count)
            spread(
                mass, x, first + skip, count, [side[rows] for side in received],
                PITCH * index, False,
            )

    width_x = lax.axis_size("gx") * CX
    height_y = lax.axis_size("gy") * CY
    depth_z = lax.axis_size("gz") * CZ
    first_z = lax.axis_index("gz") * CZ
    first_y = lax.axis_index("gy") * CY
    first_x = lax.axis_index("gx") * CX
    z_index = lax.rem(lane - 2 * PITCH - 1 + first_z + depth_z, depth_z)
    is_y = (lane >= PITCH) & (lane < 2 * PITCH)
    is_z = (lane >= 2 * PITCH) & (lane < 3 * PITCH)
    z_floor = is_z & (z_index < 2)
    z_top = is_z & (z_index >= depth_z - 2)
    fall = jnp.where(is_y, time_step * gravity, 0.0)
    row_index = lax.broadcasted_iota(jnp.int32, (PY, LANES), 0)
    y_floor = is_y & (lax.rem(row_index - 1 + first_y + height_y, height_y) < 2)

    def update(mom_values, mass_values, floor, count):
        inverse = 1.0 / (mass_values + mass_floor)
        inverse = jnp.where(
            lane[:count] < PITCH,
            inverse,
            jnp.where(
                is_y[:count],
                pltpu.roll(inverse, PITCH, axis=1),
                pltpu.roll(inverse, 2 * PITCH, axis=1),
            ),
        )
        values = mom_values * inverse - fall[:count]
        values = jnp.where(z_floor[:count] | floor, jnp.maximum(values, 0.0), values)
        return jnp.where(z_top[:count], jnp.minimum(values, 0.0), values)

    def off_outlet(x):
        x_index = lax.rem(first_x + x - 1 + width_x, width_x)
        return (x_index < width_x // 4) | (x_index >= width_x - width_x // 4)

    def update_layer(x):
        at = pl.ds(pl.multiple_of(x * PY, 8), PY)
        velocity_out[at, :] = update(mom[at, :], mass[at, :], y_floor & off_outlet(x), PY)

    def layers(step, carry):
        for member in range(7):
            update_layer(2 + 7 * step + member)
        return carry

    lax.fori_loop(0, 2, layers, 0)

    def right_sides(step, carry):
        for member in range(2):
            block = 2 * step + member
            row = row_of(block)
            wz, wzd = axis_weights(row, T_LZ, T_MZ, T_RZ, T_OZ, T_Z)
            wx = [row(T_WX + node) for node in range(6)]
            wxd = [row(T_WXD + node) for node in range(6)]
            at = pl.ds(pl.multiple_of(48 * block, 16), 48)
            for index, (along_x, along_z) in enumerate(((wx, wz), (wxd, wz), (wx, wzd))):
                high, low = split(jnp.concatenate([w * along_z for w in along_x], axis=0))
                cols = slice(index * LANES, (index + 1) * LANES)
                collect_high[at, cols] = high
                collect_low[at, cols] = low
        return carry

    lax.fori_loop(0, blocks // 2, right_sides, 0)
    for block in range(blocks):
        new_stress[:, block * BLOCK : (block + 1) * BLOCK] = stress_out[
            pl.ds(block, 6, stride=blocks), :
        ]

    for c in xz_copies:
        c.wait()
    lane8 = lane[:8]
    for side in range(2):
        for layer in range(2):
            for tile in range(PY // 8):
                half, start = tile // 8, 16 * (tile % 8)
                mom_value, mass_value = 0.0, 0.0
                for z_side in range(2):
                    source = xz_recv[2 * side + z_side, 8 * half : 8 * half + 8, :]
                    for index in range(4):
                        to = (PITCH * index if index < 3 else 0) + CZ * z_side
                        at = start + 4 * index + 2 * layer
                        moved = pltpu.roll(source, (LANES + to - at) % LANES, axis=1)
                        here = (lane8 >= to) & (lane8 < to + 2)
                        if index < 3:
                            mom_value = jnp.where(here, moved, mom_value)
                        else:
                            mass_value = jnp.where(here, moved, mass_value)
                at = firsts[side] + layer * PY + 8 * tile
                mom[at : at + 8, :] += mom_value
                mass[at : at + 8, :] += mass_value

    for c in x_copies:
        c.wait()
    near = lane[:short] < PITCH
    for side in range(2):
        for layer in range(2):
            start = firsts[side] + layer * PY
            mom[start : start + used, :] += x_recv[side, layer * used : (layer + 1) * used, :]
            at = 2 * used + layer * short
            got = x_recv[side, at : at + short, :]
            for part in range(3):
                first = start + part * short
                moved = pltpu.roll(got, LANES - PITCH * part, axis=1) if part else got
                mass[first : first + short, :] += jnp.where(near, moved, 0.0)
    for x in (0, 1, CX, CX + 1):
        update_layer(x)
    front = lane < 64
    for c in y_copies:
        c.wait()
    for side in range(2):
        y0 = y_firsts[side]
        got = y_recv[side, 2 * PX : 3 * PX, :]
        at0 = pl.ds(y0, PX, stride=PY)
        at1 = pl.ds(y0 + 1, PX, stride=PY)
        mom[at0, :] = mom[at0, :] + y_recv[side, 0:PX, :]
        mom[at1, :] = mom[at1, :] + y_recv[side, PX : 2 * PX, :]
        mass[at0, :] = mass[at0, :] + jnp.where(front[:PX], got, 0.0)
        mass[at1, :] = mass[at1, :] + jnp.where(front[:PX], pltpu.roll(got, 64, axis=1), 0.0)
    for edge in range(4):
        x0, y0 = CX * (edge // 2), y_firsts[edge % 2]
        for layer in range(2):
            at = (x0 + layer) * PY + y0
            mom[at : at + 2, :] += xy_recv[edge, 2 * layer : 2 * layer + 2, :]
            mass[at : at + 2, :] += xy_recv[edge, 4 + 2 * layer : 6 + 2 * layer, :]
    x_rows = lax.broadcasted_iota(jnp.int32, (PX, LANES), 0)
    outside = off_outlet(x_rows)
    for y in (0, 1, CY, CY + 1):
        at = pl.ds(y, PX, stride=PY)
        on_floor = lax.rem(first_y + (y - 1 + height_y), height_y) < 2
        velocity_out[at, :] = update(
            mom[at, :], mass[at, :], is_y[:PX] & outside & on_floor, PX
        )


def collect_kernel(
    tile_hbm,
    velocity,
    right_high,
    right_low,
    y_table,
    stress_in,
    new_velocity_ref,
    new_affine_ref,
    new_stress_hbm,
    grid_velocity_hbm,
    tile_ref,
    grid_velocity_ref,
    partial,
    final,
    copy_sem,
):
    blocks = tile_hbm.shape[0]
    tile_copy = pltpu.make_async_copy(tile_hbm, tile_ref, copy_sem.at[0])
    tile_copy.start()
    stress_copy = pltpu.make_async_copy(stress_in, new_stress_hbm, copy_sem.at[1])
    stress_copy.start()
    def output(step, carry):
        for member in range(4):
            x = 4 * step + member
            turned = jnp.transpose(velocity[pl.ds((x + 1) * PY + 1, CY), :])
            for dim in range(3):
                grid_velocity_ref[dim, x] = turned[PITCH * dim + 1 : PITCH * dim + 1 + CZ]
        return carry

    lax.fori_loop(0, CX // 4, output, 0)
    grid_copy = pltpu.make_async_copy(grid_velocity_ref, grid_velocity_hbm, copy_sem.at[2])
    grid_copy.start()
    tile_copy.wait()

    lanes = lax.broadcasted_iota(jnp.int32, (8, LANES), 1)

    def gather(block):
        tile_x, tile_y, tile_z = tile_coords(tile_ref, block)
        planes = []
        for node in range(6):
            at = pl.ds(pl.multiple_of((4 * tile_x + node) * PY + 4 * tile_y, 4), 8)
            planes.append(velocity[at, :])
        rows = []
        for dim in range(3):
            merged = None
            for node in range(6):
                moved = pltpu.roll(
                    planes[node],
                    LANES + 8 * node - PITCH * dim - 4 * tile_z,
                    axis=1,
                )
                merged = moved if merged is None else jnp.where(lanes < 8 * node, merged, moved)
            rows.append(merged)
        return jnp.concatenate(rows, axis=0)

    def contract(block, left_side):
        left_high, left_low = split(left_side[:, :48])
        at = pl.ds(pl.multiple_of(48 * block, 16), 48)
        both = jnp.dot(
            jnp.concatenate([left_high, left_low], axis=0),
            right_high[at, :],
            preferred_element_type=jnp.float32,
        )
        return (
            both[:24]
            + both[24:]
            + jnp.dot(left_high, right_low[at, :], preferred_element_type=jnp.float32)
        )

    def weigh(block, sums):
        def row(index):
            return jnp.broadcast_to(y_table[pl.ds(index * blocks + block, 1), :], (8, LANES))

        wy, wyd = axis_weights(row, 0, 1, 2, 3, 4)
        for dim in range(3):
            part = sums[8 * dim : 8 * dim + 8]
            terms = (
                (dim, wy * part[:, :128]),
                (3 + 3 * dim, wy * part[:, 128:256]),
                (4 + 3 * dim, wyd * part[:, :128]),
                (5 + 3 * dim, wy * part[:, 256:]),
            )
            for component, value in terms:
                at = pl.ds(pl.multiple_of(component * 8 * blocks + 8 * block, 8), 8)
                partial[at, :] = value

    def of_group(function, step, *values):
        return tuple(
            function(step * GROUP + member, *(value[member] for value in values))
            for member in range(GROUP)
        )

    def group(step, carry):
        left_sides, sums = carry
        following = of_group(gather, step + 2)
        products = of_group(contract, step + 1, left_sides)
        of_group(weigh, step, sums)
        return following, products

    steps = blocks // GROUP
    carry = of_group(gather, 1), of_group(contract, 0, of_group(gather, 0))
    left_sides, sums = lax.fori_loop(0, steps - 2, group, carry)
    of_group(weigh, steps - 2, sums)
    of_group(weigh, steps - 1, of_group(contract, steps - 1, left_sides))
    for component in range(12):
        total = partial[pl.ds(component * 8 * blocks, blocks, stride=8), :]
        for node in range(1, 6):
            total = total + partial[pl.ds(component * 8 * blocks + node, blocks, stride=8), :]
        if component >= 3:
            total = 4.0 * total
        final[component * blocks : (component + 1) * blocks, :] = total
    for block in range(blocks):
        cols = slice(block * BLOCK, (block + 1) * BLOCK)
        new_velocity_ref[:, cols] = final[pl.ds(block, 3, stride=blocks), :]
        new_affine_ref[:, cols] = final[pl.ds(3 * blocks + block, 9, stride=blocks), :]
    stress_copy.wait()
    grid_copy.wait()


def shards(
    point_frac,
    cell_offset,
    point_velocity,
    point_affine,
    point_stress,
    point_mass,
    block_tile,
    block_count,
):
    blocks = block_tile.shape[0]
    points = blocks * BLOCK
    vmem = pl.BlockSpec(memory_space=pltpu.VMEM)
    hbm = pl.BlockSpec(memory_space=pltpu.HBM)
    f32 = jnp.float32
    grid_shape = jax.ShapeDtypeStruct((ROWS, LANES), f32)
    face = PY + PY // 3
    arguments = [
        pltpu.with_memory_space_constraint(value, pltpu.HBM)
        for value in (
            block_tile,
            block_count,
            point_frac,
            cell_offset,
            point_velocity,
            point_affine,
            point_stress,
            point_mass.reshape(blocks, BLOCK),
        )
    ]
    right_shape = jax.ShapeDtypeStruct((48 * blocks, 3 * LANES), jnp.bfloat16)
    velocity, right_high, right_low, y_table, stress = pl.pallas_call(
        deposit_kernel,
        name="deposit",
        out_shape=(
            grid_shape,
            right_shape,
            right_shape,
            jax.ShapeDtypeStruct((5 * blocks, LANES), f32),
            jax.ShapeDtypeStruct((6, points), f32),
        ),
        in_specs=[hbm] * 8,
        out_specs=(vmem,) * 5,
        scratch_shapes=[
            pltpu.VMEM((ROWS, LANES), f32),
            pltpu.VMEM((ROWS, LANES), f32),
            pltpu.VMEM((T_SHARED * blocks, LANES), f32),
            pltpu.VMEM((6 * blocks, LANES), f32),
            pltpu.SMEM((blocks,), jnp.int32),
            pltpu.SMEM((blocks,), jnp.int32),
            pltpu.VMEM((3, points), f32),
            pltpu.VMEM((3, points), jnp.int32),
            pltpu.VMEM((3, points), f32),
            pltpu.VMEM((9, points), f32),
            pltpu.VMEM((6, points), f32),
            pltpu.VMEM((blocks, BLOCK), f32),
            pltpu.VMEM((48 * blocks, LANES), f32),
            pltpu.VMEM(((T_ALL - T_SHARED) * blocks, LANES), f32),
            pltpu.VMEM((6, 8 * blocks, 2 * LANES), jnp.bfloat16),
            pltpu.VMEM((6, 8 * blocks, 2 * LANES), jnp.bfloat16),
            pltpu.VMEM((2, 24, LANES), f32),
            pltpu.VMEM((2, 24, LANES), f32),
            pltpu.VMEM((2, CY - 8 + PY // 3, LANES), f32),
            pltpu.VMEM((2, CY - 8 + PY // 3, LANES), f32),
            pltpu.VMEM((2, 8 * (CY + 2) // 3, LANES), f32),
            pltpu.VMEM((2, 8 * (CY + 2) // 3, LANES), f32),
            pltpu.VMEM((4, 16, LANES), f32),
            pltpu.VMEM((4, 16, LANES), f32),
            pltpu.VMEM((2, 3 * PX + 2, LANES), f32),
            pltpu.VMEM((2, 3 * PX + 2, LANES), f32),
            pltpu.VMEM((4, 8, LANES), f32),
            pltpu.VMEM((4, 8, LANES), f32),
            pltpu.SemaphoreType.DMA((8,)),
            pltpu.SemaphoreType.DMA((16,)),
            pltpu.SemaphoreType.DMA((16,)),
        ],
        compiler_params=pltpu.CompilerParams(
            collective_id=0, has_side_effects=True, vmem_limit_bytes=VMEM_LIMIT
        ),
    )(*arguments)
    new_velocity, new_affine, new_stress, grid_velocity = pl.pallas_call(
        collect_kernel,
        name="collect",
        out_shape=(
            jax.ShapeDtypeStruct((3, points), f32),
            jax.ShapeDtypeStruct((9, points), f32),
            jax.ShapeDtypeStruct((6, points), f32),
            jax.ShapeDtypeStruct((3, CX, CZ, CY), f32),
        ),
        in_specs=[hbm] + [vmem] * 5,
        out_specs=(vmem, vmem, hbm, hbm),
        scratch_shapes=[
            pltpu.SMEM((blocks,), jnp.int32),
            pltpu.VMEM((3, CX, CZ, CY), f32),
            pltpu.VMEM((12 * 8 * blocks, LANES), f32),
            pltpu.VMEM((12 * blocks, LANES), f32),
            pltpu.SemaphoreType.DMA((3,)),
        ],
        compiler_params=pltpu.CompilerParams(vmem_limit_bytes=VMEM_LIMIT),
    )(arguments[0], velocity, right_high, right_low, y_table, stress)
    return (new_velocity, new_affine, new_stress, jnp.swapaxes(grid_velocity, 2, 3))


def solution(mesh):
    points = P(None, ("gx", "gy", "gz"))
    flat = P(("gx", "gy", "gz"))
    return jax.shard_map(
        shards,
        mesh=mesh,
        in_specs=(points,) * 5 + (flat,) * 3,
        out_specs=(points, points, points, P(None, "gx", "gy", "gz")),
        check_vma=False,
    )
```
